32 devices in a mesh: chan: 4 (over x, core), az: 2 (over y), rng: 4 (over z).
Axes of the slice: x: 2, y: 2, z: 4, core: 2. Of those that a mesh axis runs over, the one named last changes fastest.
Arguments:
- raw: float32 [2, 16, 64, 16384], P(None, 'chan', 'rng', 'az'), may hold values from -6 to 6
- taps: float32 [2, 17, 64], P(None, None, 'rng'), may hold values from -1.5 to 1.5
- recon: float32 [2, 16, 16, 16384], P(None, 'az', None, ('chan', 'rng')), may hold values from -1 to 1
- channel_slot: int32 [16], replicated, may hold values from 0 to 15, each once
Outputs:
- reconstructed: float32 [2, 16, 4, 16, 16384], P(None, None, None, 'az', ('chan', 'rng'))
The draws below stay inside these ranges and needn't reach their ends.
Inputs may be any that keep to these rules, and one draw needn't show every extreme that they name: `channel_slot`: a permutation of the channels.
All inputs are finite; a program needn't handle non-finite values.
Results may differ from the reference program's by a relative error of at most 0.0003.
Values sent between devices are 32-bit elements; how exact they have to be, the bound alone decides.
No kernel may reach another device: no remote copies, remote signals or barrier semaphores. Data moves between devices by JAX's collectives and lax.ppermute only.
A program may use at most 192 MiB of HBM per device.

```python
import jax
import jax.numpy as jnp
from jax import lax

CH = 16
NA = 16384
TAPS = 17
RSTRIP = 16
NR = 64
N_RNG = 4


def block_scale(stream_key, dims, split, least, high):
    def one(axis_at, shards_of):
        heights = jax.random.uniform(jax.random.fold_in(jax.random.fold_in(stream_key, 6), axis_at), (shards_of,), jnp.float32, least / len(split), high / len(split))
        return jnp.repeat(jnp.exp(heights), dims[axis_at] // shards_of).reshape((-1,) + (1,) * (len(dims) - axis_at - 1))

    loudness = one(*split[0])
    for cut in split[1:]:
        loudness = loudness * one(*cut)
    return loudness


def centred(rng, shape, scale, most, cuts=(), kind=jnp.bfloat16):
    values = jax.random.normal(rng, shape, jnp.float32) * scale
    if len(cuts) > 0:
        values = block_scale(rng, shape, cuts, -0.22, 0.18) * values
    return jnp.clip(values, min=-most, max=most).astype(kind)


def setup_inputs(seed: int = 0) -> dict:
    key_list = jax.random.split(jax.random.key(seed), 5)
    raw = centred(key_list[0], (2, CH, NR, NA), 1.0, 6.0, ((1, 4), (2, 4), (3, 2)), jnp.float32)
    taps = centred(key_list[1], (2, TAPS, NR), 0.25, 1.5, ((2, 4),), jnp.float32)
    recon = centred(key_list[2], (2, CH, CH, NA), (2 * CH) ** -0.5, 1.0, ((1, 2), (3, 16)), jnp.float32)
    channel_slot = jax.random.permutation(key_list[3], CH).astype(jnp.int32)
    return dict(raw=raw, taps=taps, recon=recon, channel_slot=channel_slot)


def reference(raw, taps, recon, channel_slot):
    width = taps.shape[1]
    half = (width - 1) // 2
    padded = jnp.pad(raw, ((0, 0), (0, 0), (half, half), (0, 0)))
    arranged = jnp.take(recon, channel_slot, axis=2)

    def strip(index):
        start = (index * RSTRIP).astype(jnp.int32)
        block = lax.dynamic_slice_in_dim(padded, start, RSTRIP + 2 * half, 2)
        coeffs = lax.dynamic_slice_in_dim(taps, start, RSTRIP, 2)
        real_part = jnp.zeros((CH, RSTRIP, NA), raw.dtype)
        imag_part = jnp.zeros((CH, RSTRIP, NA), raw.dtype)
        for offset in range(width):
            seg_real = block[0, :, offset:offset + RSTRIP, :]
            seg_imag = block[1, :, offset:offset + RSTRIP, :]
            tap_real = coeffs[0, offset][None, :, None]
            tap_imag = coeffs[1, offset][None, :, None]
            real_part = real_part + tap_real * seg_real - tap_imag * seg_imag
            imag_part = imag_part + tap_real * seg_imag + tap_imag * seg_real
        spectrum = jnp.fft.fft(real_part + 1j * imag_part, axis=-1, norm="ortho")
        spec_real = jnp.real(spectrum)
        spec_imag = jnp.imag(spectrum)
        high = lax.Precision.HIGHEST
        out_real = jnp.einsum("kcf,crf->krf", arranged[0], spec_real, precision=high) - jnp.einsum("kcf,crf->krf", arranged[1], spec_imag, precision=high)
        out_imag = jnp.einsum("kcf,crf->krf", arranged[0], spec_imag, precision=high) + jnp.einsum("kcf,crf->krf", arranged[1], spec_real, precision=high)
        return jnp.stack([out_real, out_imag])

    blocks = lax.map(strip, jnp.arange(N_RNG, dtype=jnp.int32))
    return jnp.moveaxis(blocks, 0, 2)
```

```python
import math

import jax
import jax.numpy as jnp
import ml_dtypes
import numpy as np
from jax import lax
from jax.experimental import pallas as pl
from jax.experimental.pallas import tpu as pltpu
from jax.sharding import PartitionSpec as P

LANES = 128
SUB = 8


def ring(size, step):
    return [(i, (i + step) % size) for i in range(size)]


def split_three(matrix):
    high = matrix.astype(np.float32).astype(ml_dtypes.bfloat16)
    low = (matrix - high.astype(np.float64)).astype(ml_dtypes.bfloat16)
    return np.concatenate([high, high, low], axis=1)


def two_parts(value):
    high = value.astype(jnp.bfloat16)
    return high, (value - high.astype(jnp.float32)).astype(jnp.bfloat16)


def fft_tables(slow, count, azs):
    own = slow // azs
    h = np.arange(slow)
    place = np.concatenate([(-i * own + np.arange(own)) % slow for i in range(azs)])
    angle = 2 * np.pi * ((h[:, None] * place[None, :]) % slow) / slow
    first = np.block([[np.cos(angle), np.sin(angle)], [-np.sin(angle), np.cos(angle)]])
    b = np.arange(LANES)
    tables = []
    for me in range(azs):
        turn = 2 * np.pi * ((h[:, None] * (b[None, :] + me * own * LANES)) % count) / count
        tables.append(np.stack([np.cos(turn), -np.sin(turn)]))
    m = np.arange(count // slow)
    angle = 2 * np.pi * ((m[:, None] * b[None, :]) % LANES) / LANES
    second = np.block([[np.cos(angle), np.sin(angle)], [-np.sin(angle), np.cos(angle)]])
    second = second / math.sqrt(count)
    return split_three(first), np.stack(tables).astype(np.float32), split_three(second)


def fft_kernel(azs, own, peers, rows, *refs):
    inputs = refs[1 : 1 + azs]
    first_ref, turn_ref, second_ref, out_ref, scratch = refs[1 + azs :]
    slow = own * azs
    subs = LANES // peers
    for tile in range(rows // SUB):
        for part in range(2):
            for i in range(azs):
                for a in range(own):
                    scratch[pl.ds(part * slow + i * own + a, SUB, stride=2 * slow), :] = inputs[i][
                        part, 0, tile * SUB : (tile + 1) * SUB, a * LANES : (a + 1) * LANES
                    ]
        for row in range(0, SUB, 2):
            x = jnp.concatenate(
                [scratch[(row + e) * 2 * slow : (row + e + 1) * 2 * slow, :] for e in range(2)], axis=1
            )
            high, low = two_parts(x)
            y = jnp.dot(
                first_ref[...],
                jnp.concatenate([high, low, high], axis=0),
                preferred_element_type=jnp.float32,
            )
            turned = []
            for e in range(2):
                real = y[:slow, e * LANES : (e + 1) * LANES]
                imag = y[slow:, e * LANES : (e + 1) * LANES]
                turned.append(
                    jnp.concatenate(
                        [
                            real * turn_ref[0, 0] - imag * turn_ref[0, 1],
                            real * turn_ref[0, 1] + imag * turn_ref[0, 0],
                        ],
                        axis=1,
                    )
                )
            high, low = two_parts(jnp.concatenate(turned, axis=0))
            z = lax.dot_general(
                second_ref[...],
                jnp.concatenate([high, low, high], axis=1),
                (((1,), (1,)), ((), ())),
                preferred_element_type=jnp.float32,
            )
            for part in range(2):
                for peer in range(peers):
                    for e in range(2):
                        out_ref[peer, part, tile, pl.ds(row + e, subs, stride=SUB), :] = z[
                            part * LANES + peer * subs : part * LANES + (peer + 1) * subs,
                            e * slow : (e + 1) * slow,
                        ]


def fft_call(index, raw, received, tables, peers, per, chunk, rows):
    azs = 1 + len(received)
    own = raw.shape[3] // LANES
    slow = own * azs
    subs = LANES // peers
    first, turn, second = tables
    row_at, row_count = rows
    grid = (row_count // SUB,)
    spec = pltpu.PrefetchScalarGridSpec(
        num_scalar_prefetch=1,
        grid=grid,
        in_specs=[
            pl.BlockSpec(
                (2, 1, SUB, own * LANES), lambda g, ix: (0, ix[0] * per + chunk, g + row_at // SUB, 0)
            )
        ]
        + [pl.BlockSpec((2, 1, SUB, own * LANES), lambda g, ix: (0, 0, g, 0))] * len(received)
        + [
            pl.BlockSpec(first.shape, lambda g, ix: (0, 0)),
            pl.BlockSpec((1, 2, slow, LANES), lambda g, ix: (ix[0], 0, 0, 0)),
            pl.BlockSpec(second.shape, lambda g, ix: (0, 0)),
        ],
        out_specs=pl.BlockSpec((peers, 2, 1, SUB * subs, LANES), lambda g, ix: (0, 0, g, 0, 0)),
        scratch_shapes=[pltpu.VMEM((SUB * 2 * slow, LANES), jnp.float32)],
    )
    out = jax.ShapeDtypeStruct((peers, 2, row_count // SUB, SUB * subs, LANES), jnp.float32)
    work = row_count * own * azs * LANES
    return pl.pallas_call(
        lambda *refs: fft_kernel(azs, own, peers, SUB, *refs),
        grid_spec=spec,
        out_shape=out,
        name="azimuth",
        cost_estimate=pl.CostEstimate(flops=work * 2 * 8 * 128 * 3, bytes_accessed=work * 16, transcendentals=0),
    )(index, raw, *received, first, turn, second)


def band_matrix(taps, me, azs):
    width, total = taps.shape[1:]
    half = (width - 1) // 2
    strips_rows = total
    at = jnp.arange(strips_rows, dtype=jnp.int32)
    tap = at[None, :] - at[:, None] + half
    hit = tap[:, :, None] == jnp.arange(width, dtype=jnp.int32)
    table = jnp.transpose(taps, (0, 2, 1))
    band = jnp.sum(jnp.where(hit[None], table[:, :, None, :], 0.0), axis=3)
    real = jnp.concatenate([band[0], -band[1]], axis=1)
    imag = jnp.concatenate([band[1], band[0]], axis=1)
    return jnp.stack([real, imag])


def filter_kernel(azs, chans, strips, tiles, subs, w_ref, *refs):
    ins, outs = refs[: len(tiles)], refs[len(tiles) :]
    w = w_ref[...]
    columns = w.shape[1] // 3
    rounded = w.astype(jnp.bfloat16).astype(jnp.float32)
    low_part = lax.broadcasted_iota(jnp.int32, w.shape, 1) >= 2 * columns
    weights = jnp.where(low_part, w - rounded, rounded).astype(jnp.bfloat16)
    step = 4
    for sub_at in range(0, subs, step):
        blocks = []
        for part in range(2):
            for strip in range(strips):
                for ref, count in zip(ins, tiles):
                    for tile in range(count):
                        blocks.append(
                            jnp.concatenate(
                                [
                                    ref[strip, part, tile, (sub_at + s) * SUB : (sub_at + s + 1) * SUB, :]
                                    for s in range(step)
                                ],
                                axis=1,
                            )
                        )
        high, low = two_parts(jnp.concatenate(blocks, axis=0))
        y = jnp.dot(
            weights, jnp.concatenate([high, low, high], axis=0), preferred_element_type=jnp.float32
        )
        at = 0
        for i in range(azs):
            for part in range(2):
                for strip in range(strips):
                    for s in range(step):
                        outs[i][part, 0, strip, sub_at + s, :, :] = y[
                            at : at + SUB, s * LANES : (s + 1) * LANES
                        ]
                    at += SUB


def filter_call(weights, pieces, chans, azs, subs):
    peers = pieces[0].shape[0]
    strips = peers // chans
    tiles = [p.shape[2] for p in pieces]
    out = jax.ShapeDtypeStruct((2, chans, strips, subs, SUB, LANES), jnp.float32)
    return pl.pallas_call(
        lambda *refs: filter_kernel(azs, chans, strips, tiles, subs, *refs),
        grid=(chans,),
        in_specs=[pl.BlockSpec(weights.shape, lambda g: (0, 0))]
        + [pl.BlockSpec((strips,) + p.shape[1:], lambda g: (g, 0, 0, 0, 0)) for p in pieces],
        out_specs=[pl.BlockSpec((2, 1, strips, subs, SUB, LANES), lambda g: (0, g, 0, 0, 0, 0))] * azs,
        out_shape=[out] * azs,
        name="range_filter",
        cost_estimate=pl.CostEstimate(
            flops=2 * weights.shape[0] * weights.shape[1] * chans * subs * LANES,
            bytes_accessed=8 * sum(math.prod(p.shape) for p in pieces),
            transcendentals=0,
        ),
    )(weights, *pieces)


def mix_kernel(azs, chans, local, per, chunk, kept, index_ref, slot_ref, *refs):
    data, mats = refs[:azs], refs[azs : 2 * azs]
    prior = refs[2 * azs] if kept else None
    out_ref = refs[-1]
    me = index_ref[0]
    strips = data[0].shape[2]
    here = mats[0].shape[1]
    pair = 2 if here % 2 == 0 else 1
    for j in range(azs):
        base = lax.rem(me - j + azs, azs) * here

        def body(step, _, j=j, base=base):
            totals = [[[None, None] for _ in range(strips)] for _ in range(pair)]
            if kept:
                for e in range(pair):
                    for s in range(strips):
                        for p in range(2):
                            totals[e][s][p] = prior[p, base + step * pair + e, s]
            for i in range(azs):
                source = lax.rem(me - i + azs, azs)
                for chan in range(chans):
                    slot = slot_ref[chan * local + source * per + chunk]
                    values = [(data[i][0, chan, s, 0], data[i][1, chan, s, 0]) for s in range(strips)]
                    for e in range(pair):
                        row = step * pair + e
                        ar = jnp.broadcast_to(mats[j][0, row, pl.ds(slot, 1), :], (SUB, LANES))
                        ai = jnp.broadcast_to(mats[j][1, row, pl.ds(slot, 1), :], (SUB, LANES))
                        for s, (dr, di) in enumerate(values):
                            real = ar * dr - ai * di
                            imag = ar * di + ai * dr
                            old = totals[e][s]
                            totals[e][s] = [
                                real if old[0] is None else old[0] + real,
                                imag if old[1] is None else old[1] + imag,
                            ]
            for e in range(pair):
                for s in range(strips):
                    for p in range(2):
                        out_ref[p, base + step * pair + e, s] = totals[e][s][p]
            return 0

        lax.fori_loop(0, here // pair, body, 0)


def mix_call(index, slots, data, mats, prior, chans, local, per, chunk):
    azs = len(data)
    _, _, strips, subs, _, _ = data[0].shape
    here, width = mats[0].shape[1:3]
    total = here * azs
    out = jax.ShapeDtypeStruct((2, total, strips, SUB, subs * LANES), jnp.float32)
    out_spec = pl.BlockSpec((2, total, strips, SUB, LANES), lambda g, ix, sl: (0, 0, 0, 0, g))
    kept = prior is not None
    return pl.pallas_call(
        lambda *refs: mix_kernel(azs, chans, local, per, chunk, kept, *refs),
        grid_spec=pltpu.PrefetchScalarGridSpec(
            num_scalar_prefetch=2,
            grid=(subs,),
            in_specs=[
                pl.BlockSpec((2, chans, strips, 1, SUB, LANES), lambda g, ix, sl: (0, 0, 0, g, 0, 0))
            ]
            * azs
            + [pl.BlockSpec((2, here, width, LANES), lambda g, ix, sl: (0, 0, 0, g))] * azs
            + [out_spec] * kept,
            out_specs=out_spec,
        ),
        out_shape=out,
        name="reconstruct",
        input_output_aliases={2 + 2 * azs: 0} if kept else {},
        cost_estimate=pl.CostEstimate(
            flops=8 * total * strips * SUB * subs * LANES * chans * azs,
            bytes_accessed=4 * (2 * total * strips * SUB * subs * LANES) * (2 if kept else 1),
            transcendentals=0,
        ),
    )(index, slots, *data, *mats, *([prior] if kept else []))


def with_halo(shard, sides, width):
    for axis, dim in sides:
        size, length = (lax.axis_size(axis), shard.shape[dim])
        up = [(i, (i + 1) % size) for i in range(size - 1)]
        down = [(j, i) for i, j in up]
        last = lax.slice_in_dim(shard, length - width, length, axis=dim)
        leading = lax.slice_in_dim(shard, 0, width, axis=dim)
        before = lax.ppermute(last, axis, up)
        after = lax.ppermute(leading, axis, down)
        shard = jnp.concatenate([before, shard, after], axis=dim)
    return shard


def phases(first, second, length):
    left = jnp.arange(first, dtype=jnp.int32)
    right = jnp.arange(second, dtype=jnp.int32)
    product = left[:, None] * right[None, :] % length
    angle = product.astype(jnp.float32) * (2.0 * math.pi / length)
    return (jnp.cos(angle), jnp.sin(angle))


def azimuth_fft(block):
    count = block.shape[-1]
    rows = math.isqrt(count)
    while count % rows:
        rows = rows - 1
    cols = count // rows
    lead = block.shape[1:-1]
    high = lax.Precision.HIGHEST
    real_in = block[0].reshape(lead + (rows, cols))
    imag_in = block[1].reshape(lead + (rows, cols))
    cosine_first, sine_first = phases(rows, rows, rows)
    first_real = jnp.einsum("...ab,af->...bf", real_in, cosine_first, precision=high) + jnp.einsum(
        "...ab,af->...bf", imag_in, sine_first, precision=high
    )
    first_imag = jnp.einsum("...ab,af->...bf", imag_in, cosine_first, precision=high) - jnp.einsum(
        "...ab,af->...bf", real_in, sine_first, precision=high
    )
    twist_cos, twist_sin = phases(cols, rows, count)
    turned_real = first_real * twist_cos + first_imag * twist_sin
    turned_imag = first_imag * twist_cos - first_real * twist_sin
    cosine_second, sine_second = phases(cols, cols, cols)
    out_real = jnp.einsum(
        "...bf,bg->...gf", turned_real, cosine_second, precision=high
    ) + jnp.einsum("...bf,bg->...gf", turned_imag, sine_second, precision=high)
    out_imag = jnp.einsum(
        "...bf,bg->...gf", turned_imag, cosine_second, precision=high
    ) - jnp.einsum("...bf,bg->...gf", turned_real, sine_second, precision=high)
    scale = 1.0 / math.sqrt(count)
    return jnp.stack([out_real.reshape(lead + (count,)), out_imag.reshape(lead + (count,))]) * scale


def general_shards(raw, taps, recon, channel_slot):
    width = taps.shape[1]
    half = (width - 1) // 2
    strip_rows = raw.shape[2]
    padded = with_halo(raw, (("rng", 2),), half)
    real_part = jnp.zeros(raw.shape[1:], jnp.float32)
    imag_part = jnp.zeros(raw.shape[1:], jnp.float32)
    for offset in range(width):
        seg_real = padded[0, :, offset : offset + strip_rows, :]
        seg_imag = padded[1, :, offset : offset + strip_rows, :]
        tap_real = taps[0, offset][None, :, None]
        tap_imag = taps[1, offset][None, :, None]
        real_part = real_part + tap_real * seg_real - tap_imag * seg_imag
        imag_part = imag_part + tap_real * seg_imag + tap_imag * seg_real
    filtered = jnp.stack([real_part, imag_part])
    spectrum = azimuth_fft(lax.all_to_all(filtered, "az", split_axis=2, concat_axis=3, tiled=True))
    strips = lax.axis_size("rng")
    groups = lax.axis_size("chan")
    local_channels = spectrum.shape[1]
    local_range = spectrum.shape[2]
    moved = lax.all_to_all(
        spectrum[:, None], ("chan", "rng"), split_axis=4, concat_axis=1, tiled=True
    )
    bins = moved.shape[-1]
    moved = moved.reshape((2, groups, strips, local_channels, local_range, bins))
    doppler = jnp.transpose(moved, (0, 1, 3, 2, 4, 5)).reshape(
        (2, groups * local_channels, strips * local_range, bins)
    )
    channels = doppler.shape[1]
    selector = (channel_slot[:, None] == jnp.arange(channels, dtype=jnp.int32)[None, :]).astype(
        jnp.float32
    )
    piece = lax.all_gather(recon, "az", axis=1, tiled=True)
    arranged = jnp.einsum("pkjf,cj->pkcf", piece, selector, precision=lax.Precision.HIGHEST)
    shape = (piece.shape[1], doppler.shape[2], doppler.shape[3])
    out_real = jnp.zeros(shape, jnp.float32)
    out_imag = jnp.zeros(shape, jnp.float32)
    for channel in range(channels):
        mat_real = arranged[0, :, channel, None, :]
        mat_imag = arranged[1, :, channel, None, :]
        data_real = doppler[0, channel][None]
        data_imag = doppler[1, channel][None]
        out_real = out_real + mat_real * data_real - mat_imag * data_imag
        out_imag = out_imag + mat_real * data_imag + mat_imag * data_real
    result = jnp.stack([out_real, out_imag])
    total_range = result.shape[2]
    return result.reshape((2, result.shape[1], strips, total_range // strips, result.shape[3]))


def shards(raw, taps, recon, channel_slot):
    chans, azs, strips = (lax.axis_size(n) for n in ("chan", "az", "rng"))
    _, local, rows, pulses = raw.shape
    fits = local % azs == 0 and rows == azs * SUB and pulses * azs == LANES * LANES
    if not (fits and LANES % (chans * strips) == 0):
        return general_shards(raw, taps, recon, channel_slot)
    me = lax.axis_index("az").astype(jnp.int32)
    index = me[None]
    per = local // azs
    count = pulses * azs
    peers = chans * strips
    slow = count // LANES
    subs = LANES // peers
    tables = [jnp.asarray(t) for t in fft_tables(slow, count, azs)]

    def give(step, chunk):
        to = lax.rem(me + step, azs)
        block = lax.dynamic_slice(raw, (0, to * per + chunk, 0, 0), (2, 1, rows, pulses))
        return lax.ppermute(block, "az", ring(azs, step))

    received = [[give(i, j) for i in range(1, azs)] for j in range(per)]
    mats = [recon] + [lax.ppermute(recon, "az", ring(azs, i)) for i in range(1, azs)]

    copies = jnp.broadcast_to(taps[None], (strips,) + taps.shape)
    all_taps = lax.all_to_all(copies, "rng", 0, 0, tiled=True)
    all_taps = jnp.transpose(all_taps, (1, 2, 0, 3)).reshape(2, taps.shape[1], strips * rows)
    band = band_matrix(all_taps, me, azs)
    band = band.reshape(2, strips, azs, SUB, 2 * strips * rows)
    band = jnp.transpose(band, (2, 0, 1, 3, 4)).reshape(azs, -1, 2 * strips * rows)
    band = lax.dynamic_slice_in_dim(jnp.concatenate([band, band]), me, azs, 0)
    weights = jnp.tile(band.reshape(-1, 2 * strips * rows), (1, 3))

    result = None
    for j in range(per):
        spectrum = fft_call(index, raw, received[j], tables, peers, per, j, (0, rows))
        moved = lax.all_to_all(spectrum, ("chan", "rng"), 0, 0, tiled=True)
        filtered = filter_call(weights, [moved], chans, azs, subs)
        data = [filtered[0]] + [
            lax.ppermute(filtered[i], "az", ring(azs, i)) for i in range(1, azs)
        ]
        result = mix_call(index, channel_slot, data, mats, result, chans, local, per, j)
    return result


def solution(mesh):
    return jax.shard_map(
        shards,
        mesh=mesh,
        in_specs=(
            P(None, "chan", "rng", "az"),
            P(None, None, "rng"),
            P(None, "az", None, ("chan", "rng")),
            P(),
        ),
        out_specs=P(None, None, None, "az", ("chan", "rng")),
        check_vma=False,
    )
```

```python
import math

import jax
import jax.numpy as jnp
import ml_dtypes
import numpy as np
from jax import lax
from jax.experimental import pallas as pl
from jax.experimental.pallas import tpu as pltpu
from jax.sharding import PartitionSpec as P


LANES = 128
SUB = 8
RESIDENT = pl.BlockSpec(memory_space=pltpu.VMEM)
SCALARS = pl.BlockSpec(memory_space=pltpu.SMEM)
WHOLE = 67043328


def ring(size, step):
    return [(i, (i + step) % size) for i in range(size)]


def split_three(matrix):
    high = matrix.astype(np.float32).astype(ml_dtypes.bfloat16)
    low = (matrix - high.astype(np.float64)).astype(ml_dtypes.bfloat16)
    return np.concatenate([high, high, low], axis=1)


def two_parts(value):
    high = value.astype(jnp.bfloat16)
    return high, (value - high.astype(jnp.float32)).astype(jnp.bfloat16)


def fft_tables(slow, count, azs):
    own = slow // azs
    h = np.arange(slow)
    place = np.concatenate([(-i * own + np.arange(own)) % slow for i in range(azs)])
    angle = 2 * np.pi * ((h[:, None] * place[None, :]) % slow) / slow
    first = np.block([[np.cos(angle), np.sin(angle)], [-np.sin(angle), np.cos(angle)]])
    b = np.arange(LANES)
    tables = []
    for me in range(azs):
        turn = 2 * np.pi * ((h[:, None] * (b[None, :] + me * own * LANES)) % count) / count
        tables.append(np.stack([np.cos(turn), -np.sin(turn)]))
    m = np.arange(count // slow)
    angle = 2 * np.pi * ((m[:, None] * b[None, :]) % LANES) / LANES
    second = np.block([[np.cos(angle), np.sin(angle)], [-np.sin(angle), np.cos(angle)]])
    second = second / math.sqrt(count)
    return split_three(first), np.stack(tables).astype(np.float32), split_three(second)


def fft_kernel(azs, own, peers, index_ref, *refs):
    inputs = refs[:azs]
    first_ref, turn_ref, second_ref = refs[azs : 3 + azs]
    out_ref, scratch = refs[-2:]
    slow = own * azs
    subs = LANES // peers
    me = index_ref[0]
    for part in range(2):
        for i in range(azs):
            for a in range(own):
                scratch[pl.ds(part * slow + i * own + a, SUB, stride=2 * slow), :] = inputs[i][
                    part, 0, :, a * LANES : (a + 1) * LANES
                ]
    for row in range(0, SUB, 2):
        x = jnp.concatenate(
            [scratch[(row + e) * 2 * slow : (row + e + 1) * 2 * slow, :] for e in range(2)], axis=1
        )
        high, low = two_parts(x)
        y = jnp.dot(
            first_ref[...],
            jnp.concatenate([high, low, high], axis=0),
            preferred_element_type=jnp.float32,
        )
        turned = []
        for e in range(2):
            real = y[:slow, e * LANES : (e + 1) * LANES]
            imag = y[slow:, e * LANES : (e + 1) * LANES]
            turned.append(
                jnp.concatenate(
                    [
                        real * turn_ref[me, 0] - imag * turn_ref[me, 1],
                        real * turn_ref[me, 1] + imag * turn_ref[me, 0],
                    ],
                    axis=1,
                )
            )
        high, low = two_parts(jnp.concatenate(turned, axis=0))
        z = lax.dot_general(
            second_ref[...],
            jnp.concatenate([high, low, high], axis=1),
            (((1,), (1,)), ((), ())),
            preferred_element_type=jnp.float32,
        )
        for part in range(2):
            for peer in range(peers):
                for e in range(2):
                    at = part * LANES + peer * subs
                    out_ref[peer, part, 0, pl.ds(row + e, subs, stride=SUB), :] = z[
                        at : at + subs, e * slow : (e + 1) * slow
                    ]


def fft_call(index, inputs, tables, peers, tiles, first, limit, prior=None):
    azs = len(inputs)
    steps = inputs[0].shape[1]
    own = inputs[0].shape[3] // LANES
    slow = own * azs
    subs = LANES // peers
    kept = prior is not None
    resident = steps == 1
    work = steps * SUB * slow * LANES
    if resident:
        specs = [RESIDENT] * (azs + 3)
    else:
        specs = [pl.BlockSpec((2, 1, SUB, own * LANES), lambda g: (0, g, 0, 0))] * azs
        specs += [pl.BlockSpec(t.shape, lambda g, n=t.ndim: (0,) * n) for t in tables]
    return pl.pallas_call(
        lambda *refs: fft_kernel(azs, own, peers, *refs),
        grid=(steps,),
        in_specs=[SCALARS] + specs + [pl.BlockSpec(memory_space=pl.ANY)] * kept,
        out_specs=pl.BlockSpec((peers, 2, 1, SUB * subs, LANES), lambda g: (0, 0, g + first, 0, 0)),
        out_shape=jax.ShapeDtypeStruct((peers, 2, tiles, SUB * subs, LANES), jnp.float32),
        scratch_shapes=[pltpu.VMEM((SUB * 2 * slow, LANES), jnp.float32)],
        input_output_aliases={azs + 4: 0} if kept else {},
        compiler_params=pltpu.CompilerParams(vmem_limit_bytes=limit),
        name="azimuth",
        cost_estimate=pl.CostEstimate(
            flops=work * 2 * 8 * LANES * 3, bytes_accessed=work * 16, transcendentals=0
        ),
    )(index, *inputs, *tables, *([prior] if kept else []))


def band_matrix(taps, lead, total_in, me, azs):
    width, total = taps.shape[1:]
    tap = jnp.arange(total_in, dtype=jnp.int32)[None, :] - jnp.arange(total, dtype=jnp.int32)[:, None] + lead
    hit = tap[:, :, None] == jnp.arange(width, dtype=jnp.int32)
    table = jnp.transpose(taps, (0, 2, 1))
    band = jnp.sum(jnp.where(hit[None], table[:, :, None, :], 0.0), axis=3)
    real = jnp.concatenate([band[0], -band[1]], axis=1)
    imag = jnp.concatenate([band[1], band[0]], axis=1)
    both = jnp.stack([real, imag]).reshape(2, total // (azs * SUB), azs, SUB, 2 * total_in)
    both = jnp.transpose(both, (2, 0, 1, 3, 4)).reshape(azs, -1, 2 * total_in)
    both = lax.dynamic_slice_in_dim(jnp.concatenate([both, both]), me, azs, 0)
    return jnp.tile(both.reshape(-1, 2 * total_in), (1, 3))


def rounded_weights(w):
    columns = w.shape[1] // 3
    rounded = w.astype(jnp.bfloat16).astype(jnp.float32)
    low_part = lax.broadcasted_iota(jnp.int32, w.shape, 1) >= 2 * columns
    return jnp.where(low_part, w - rounded, rounded).astype(jnp.bfloat16)


def weighted(weights, blocks):
    high, low = two_parts(jnp.concatenate(blocks, axis=0))
    return jnp.dot(
        weights, jnp.concatenate([high, low, high], axis=0), preferred_element_type=jnp.float32
    )


def early_filter_kernel(azs, width, w_ref, before, own, after, *outs):
    weights = rounded_weights(w_ref[...])

    def body(step, _):
        at = pl.ds(pl.multiple_of(step * width, width), width)
        y = weighted(
            weights,
            [
                block
                for part in range(2)
                for block in (before[part, 0, :, at], own[part, 0, :, at], after[part, 0, :, at])
            ],
        )
        for i in range(azs):
            for part in range(2):
                row = (i * 2 + part) * SUB
                outs[i][part, 0, :, at] = y[row : row + SUB]
        return 0

    lax.fori_loop(0, own.shape[3] // width, body, 0)


def early_filter_call(weights, before, raw, after, at, azs):
    _, count, _, pulses = before.shape
    rows = raw.shape[2]
    out = jax.ShapeDtypeStruct((2, count, SUB, pulses), jnp.float32)
    edge = pl.BlockSpec((2, 1, SUB, pulses), lambda g: (0, g, 0, 0))
    return pl.pallas_call(
        lambda *refs: early_filter_kernel(azs, 4 * LANES, *refs),
        grid=(count,),
        in_specs=[
            pl.BlockSpec(weights.shape, lambda g: (0, 0)),
            edge,
            pl.BlockSpec((2, 1, rows, pulses), lambda g: (0, g + at, 0, 0)),
            edge,
        ],
        out_specs=[edge] * azs,
        out_shape=[out] * azs,
        compiler_params=pltpu.CompilerParams(vmem_limit_bytes=WHOLE),
        name="strip_filter",
        cost_estimate=pl.CostEstimate(
            flops=2 * weights.shape[0] * weights.shape[1] * count * pulses,
            bytes_accessed=24 * count * rows * pulses,
            transcendentals=0,
        ),
    )(weights, before, raw, after)


def late_filter_kernel(azs, w_ref, in_ref, *outs):
    weights = rounded_weights(w_ref[...])
    strips, _, tiles, depth, _ = in_ref.shape
    subs = depth // SUB
    chan = pl.program_id(0)
    step = 2 if subs % 2 == 0 else 1

    for sub in range(0, subs, step):
        y = weighted(
            weights,
            [
                jnp.concatenate(
                    [
                        in_ref[strip, part, tile, (sub + s) * SUB : (sub + s + 1) * SUB, :]
                        for s in range(step)
                    ],
                    axis=1,
                )
                for part in range(2)
                for strip in range(strips)
                for tile in range(tiles)
            ],
        )
        at = 0
        for i in range(azs):
            for part in range(2):
                for strip in range(strips):
                    for s in range(step):
                        outs[i][part, chan, strip, sub + s, :, :] = y[
                            at : at + SUB, s * LANES : (s + 1) * LANES
                        ]
                    at += SUB


def late_filter_call(weights, moved, chans, azs):
    peers, _, _, depth, _ = moved.shape
    strips, subs = peers // chans, depth // SUB
    out = jax.ShapeDtypeStruct((2, chans, strips, subs, SUB, LANES), jnp.float32)
    return pl.pallas_call(
        lambda *refs: late_filter_kernel(azs, *refs),
        grid=(chans,),
        in_specs=[
            pl.BlockSpec(weights.shape, lambda g: (0, 0)),
            pl.BlockSpec((strips,) + moved.shape[1:], lambda g: (g, 0, 0, 0, 0)),
        ],
        out_specs=[RESIDENT] * azs,
        out_shape=[out] * azs,
        compiler_params=pltpu.CompilerParams(vmem_limit_bytes=32 << 20),
        name="range_filter",
        cost_estimate=pl.CostEstimate(
            flops=2 * weights.shape[0] * weights.shape[1] * chans * subs * LANES,
            bytes_accessed=8 * math.prod(moved.shape),
            transcendentals=0,
        ),
    )(weights, moved)


def mix_kernel(sources, azs, strips, kept, index_ref, slot_ref, *refs):
    out_ref, scratch = refs[-2:]
    mats = refs[len(refs) - 2 - kept - azs : len(refs) - 2 - kept]
    prior = refs[-3] if kept else None
    me = index_ref[0]
    g = pl.program_id(0)
    here = mats[0].shape[1]
    items = sources(me, g, refs)
    for n, (_, value) in enumerate(items):
        for s in range(strips):
            dr, di = value(s)
            scratch[n, s] = dr + di
    slots = [slot_ref[channel] for channel, _ in items]
    for j in range(azs):
        base = lax.rem(me - j + azs, azs) * here

        def body(step, _, j=j, base=base):
            totals = None
            for n, (_, value) in enumerate(items):
                ar = jnp.broadcast_to(mats[j][0, step, pl.ds(slots[n], 1), :], (SUB, LANES))
                ai = jnp.broadcast_to(mats[j][1, step, pl.ds(slots[n], 1), :], (SUB, LANES))
                both = ar + ai
                terms = []
                for s in range(strips):
                    dr, di = value(s)
                    terms += [ar * dr, ai * di, both * scratch[n, s]]
                totals = terms if totals is None else [t + u for t, u in zip(totals, terms)]
            row = base + step
            for s in range(strips):
                first, second, third = totals[3 * s : 3 * s + 3]
                real, imag = first - second, third - first - second
                if kept:
                    real, imag = real + prior[0, row, s], imag + prior[1, row, s]
                out_ref[0, row, s] = real
                out_ref[1, row, s] = imag
            return 0

        lax.fori_loop(0, here, body, 0)


def mix_call(index, slots, data, sources, mats, prior, strips, subs, items):
    azs = len(mats)
    total = mats[0].shape[1] * azs
    out = jax.ShapeDtypeStruct((2, total, strips, SUB, subs * LANES), jnp.float32)
    out_spec = pl.BlockSpec((2, total, strips, SUB, LANES), lambda g: (0, 0, 0, 0, g))
    kept = prior is not None
    return pl.pallas_call(
        lambda *refs: mix_kernel(sources, azs, strips, kept, *refs),
        grid=(subs,),
        in_specs=[SCALARS] * 2
        + [RESIDENT] * len(data)
        + [pl.BlockSpec(mats[0].shape[:3] + (LANES,), lambda g: (0, 0, 0, g))] * azs
        + [out_spec] * kept,
        out_specs=out_spec,
        out_shape=out,
        scratch_shapes=[pltpu.VMEM((items, strips, SUB, LANES), jnp.float32)],
        input_output_aliases={2 + len(data) + azs: 0} if kept else {},
        compiler_params=pltpu.CompilerParams(vmem_limit_bytes=32 << 20),
        name="reconstruct",
        cost_estimate=pl.CostEstimate(
            flops=8 * total * strips * SUB * subs * LANES * items,
            bytes_accessed=4 * (2 * total * strips * SUB * subs * LANES) * (2 if kept else 1),
            transcendentals=0,
        ),
    )(index, slots, *data, *mats, *([prior] if kept else []))


def with_halo(shard, sides, width):
    for axis, dim in sides:
        size, length = (lax.axis_size(axis), shard.shape[dim])
        up = [(i, (i + 1) % size) for i in range(size - 1)]
        down = [(j, i) for i, j in up]
        last = lax.slice_in_dim(shard, length - width, length, axis=dim)
        leading = lax.slice_in_dim(shard, 0, width, axis=dim)
        before = lax.ppermute(last, axis, up)
        after = lax.ppermute(leading, axis, down)
        shard = jnp.concatenate([before, shard, after], axis=dim)
    return shard


def phases(first, second, length):
    left = jnp.arange(first, dtype=jnp.int32)
    right = jnp.arange(second, dtype=jnp.int32)
    product = left[:, None] * right[None, :] % length
    angle = product.astype(jnp.float32) * (2.0 * math.pi / length)
    return (jnp.cos(angle), jnp.sin(angle))


def azimuth_fft(block):
    count = block.shape[-1]
    rows = math.isqrt(count)
    while count % rows:
        rows = rows - 1
    cols = count // rows
    lead = block.shape[1:-1]
    high = lax.Precision.HIGHEST
    real_in = block[0].reshape(lead + (rows, cols))
    imag_in = block[1].reshape(lead + (rows, cols))
    cosine_first, sine_first = phases(rows, rows, rows)
    first_real = jnp.einsum("...ab,af->...bf", real_in, cosine_first, precision=high) + jnp.einsum(
        "...ab,af->...bf", imag_in, sine_first, precision=high
    )
    first_imag = jnp.einsum("...ab,af->...bf", imag_in, cosine_first, precision=high) - jnp.einsum(
        "...ab,af->...bf", real_in, sine_first, precision=high
    )
    twist_cos, twist_sin = phases(cols, rows, count)
    turned_real = first_real * twist_cos + first_imag * twist_sin
    turned_imag = first_imag * twist_cos - first_real * twist_sin
    cosine_second, sine_second = phases(cols, cols, cols)
    out_real = jnp.einsum(
        "...bf,bg->...gf", turned_real, cosine_second, precision=high
    ) + jnp.einsum("...bf,bg->...gf", turned_imag, sine_second, precision=high)
    out_imag = jnp.einsum(
        "...bf,bg->...gf", turned_imag, cosine_second, precision=high
    ) - jnp.einsum("...bf,bg->...gf", turned_real, sine_second, precision=high)
    scale = 1.0 / math.sqrt(count)
    return jnp.stack([out_real.reshape(lead + (count,)), out_imag.reshape(lead + (count,))]) * scale


def general_shards(raw, taps, recon, channel_slot):
    width = taps.shape[1]
    half = (width - 1) // 2
    strip_rows = raw.shape[2]
    padded = with_halo(raw, (("rng", 2),), half)
    real_part = jnp.zeros(raw.shape[1:], jnp.float32)
    imag_part = jnp.zeros(raw.shape[1:], jnp.float32)
    for offset in range(width):
        seg_real = padded[0, :, offset : offset + strip_rows, :]
        seg_imag = padded[1, :, offset : offset + strip_rows, :]
        tap_real = taps[0, offset][None, :, None]
        tap_imag = taps[1, offset][None, :, None]
        real_part = real_part + tap_real * seg_real - tap_imag * seg_imag
        imag_part = imag_part + tap_real * seg_imag + tap_imag * seg_real
    filtered = jnp.stack([real_part, imag_part])
    spectrum = azimuth_fft(lax.all_to_all(filtered, "az", split_axis=2, concat_axis=3, tiled=True))
    strips = lax.axis_size("rng")
    groups = lax.axis_size("chan")
    local_channels = spectrum.shape[1]
    local_range = spectrum.shape[2]
    moved = lax.all_to_all(
        spectrum[:, None], ("chan", "rng"), split_axis=4, concat_axis=1, tiled=True
    )
    bins = moved.shape[-1]
    moved = moved.reshape((2, groups, strips, local_channels, local_range, bins))
    doppler = jnp.transpose(moved, (0, 1, 3, 2, 4, 5)).reshape(
        (2, groups * local_channels, strips * local_range, bins)
    )
    channels = doppler.shape[1]
    selector = (channel_slot[:, None] == jnp.arange(channels, dtype=jnp.int32)[None, :]).astype(
        jnp.float32
    )
    piece = lax.all_gather(recon, "az", axis=1, tiled=True)
    arranged = jnp.einsum("pkjf,cj->pkcf", piece, selector, precision=lax.Precision.HIGHEST)
    shape = (piece.shape[1], doppler.shape[2], doppler.shape[3])
    out_real = jnp.zeros(shape, jnp.float32)
    out_imag = jnp.zeros(shape, jnp.float32)
    for channel in range(channels):
        mat_real = arranged[0, :, channel, None, :]
        mat_imag = arranged[1, :, channel, None, :]
        data_real = doppler[0, channel][None]
        data_imag = doppler[1, channel][None]
        out_real = out_real + mat_real * data_real - mat_imag * data_imag
        out_imag = out_imag + mat_real * data_imag + mat_imag * data_real
    result = jnp.stack([out_real, out_imag])
    total_range = result.shape[2]
    return result.reshape((2, result.shape[1], strips, total_range // strips, result.shape[3]))


def shards(raw, taps, recon, channel_slot):
    chans, azs, strips = (lax.axis_size(n) for n in ("chan", "az", "rng"))
    _, local, rows, pulses = raw.shape
    width = taps.shape[1]
    half = (width - 1) // 2
    peers = chans * strips
    fits = local > azs and rows == azs * SUB and pulses * azs == LANES * LANES and half == SUB
    if not (fits and LANES % peers == 0):
        return general_shards(raw, taps, recon, channel_slot)
    me = lax.axis_index("az").astype(jnp.int32)
    index = me[None]
    count = pulses * azs
    slow = count // LANES
    subs = LANES // peers
    tables = [jnp.asarray(t) for t in fft_tables(slow, count, azs)]
    rest = local - azs

    def give(step, at):
        to = lax.rem(me + step, azs)
        block = lax.dynamic_slice(raw, (0, to, at, 0), (2, 1, SUB, pulses))
        return lax.ppermute(block, "az", ring(azs, step)) if step else block

    def turn(spectra):
        return lax.all_to_all(spectra, ("chan", "rng"), 0, 0, tiled=True)

    received = [[give(i, n * SUB) for i in range(azs)] for n in range(rows // SUB)]
    near = lax.axis_index("rng").astype(jnp.int32)
    parts = [taps] + [lax.ppermute(taps, "rng", ring(strips, strips - i)) for i in range(1, strips)]
    all_taps = lax.dynamic_slice_in_dim(jnp.stack(parts + parts), strips - near, strips, 0)
    all_taps = jnp.transpose(all_taps, (1, 2, 0, 3)).reshape(2, width, strips * rows)
    up = ring(strips, 1)[:-1]
    down = [(b, a) for a, b in up]
    before = lax.ppermute(raw[:, azs:, rows - half :, :], "rng", up)
    after = lax.ppermute(raw[:, azs:, :half, :], "rng", down)

    early_weights = band_matrix(taps, 0, rows + 2 * half, me, azs)
    late_weights = band_matrix(all_taps, half, strips * rows, me, azs)

    spectra = None
    for n in range(rows // SUB):
        spectra = fft_call(index, received[n], tables, peers, rows // SUB, n, 32 << 20, spectra)
    late = turn(spectra)

    filtered = early_filter_call(early_weights, before, raw, after, azs, azs)
    swapped = [filtered[0]] + [lax.ppermute(filtered[i], "az", ring(azs, i)) for i in range(1, azs)]
    mats = [recon] + [lax.ppermute(recon, "az", ring(azs, i)) for i in range(1, azs)]
    spectra = fft_call(index, swapped, tables, peers, rest, 0, WHOLE)
    early = turn(spectra)

    filtered = late_filter_call(late_weights, late, chans, azs)
    data = [filtered[0]] + [lax.ppermute(filtered[i], "az", ring(azs, i)) for i in range(1, azs)]

    def late_sources(me, g, refs):
        return [
            (
                chan * local + lax.rem(me - i + azs, azs),
                lambda s, i=i, chan=chan: (refs[i][0, chan, s, g], refs[i][1, chan, s, g]),
            )
            for i in range(azs)
            for chan in range(chans)
        ]

    def early_sources(me, g, refs):
        at = pl.ds(pl.multiple_of(g * SUB, SUB), SUB)
        return [
            (
                chan * local + azs + c,
                lambda s, c=c, chan=chan: tuple(refs[0][chan * strips + s, p, c, at, :] for p in range(2)),
            )
            for chan in range(chans)
            for c in range(rest)
        ]

    def mix(data, sources, prior, items):
        return mix_call(index, channel_slot, data, sources, mats, prior, strips, subs, items)

    result = mix(data, late_sources, None, chans * azs)
    return mix([early], early_sources, result, chans * rest)


def solution(mesh):
    return jax.shard_map(
        shards,
        mesh=mesh,
        in_specs=(
            P(None, "chan", "rng", "az"),
            P(None, None, "rng"),
            P(None, "az", None, ("chan", "rng")),
            P(),
        ),
        out_specs=P(None, None, None, "az", ("chan", "rng")),
        check_vma=False,
    )
```

```python
import math

import jax
import jax.numpy as jnp
import ml_dtypes
import numpy as np
from jax import lax
from jax.experimental import pallas as pl
from jax.experimental.pallas import tpu as pltpu
from jax.sharding import PartitionSpec as P


LANES = 128
SUB = 8
RESIDENT = pl.BlockSpec(memory_space=pltpu.VMEM)
SCALARS = pl.BlockSpec(memory_space=pltpu.SMEM)
WHOLE = 67043328


def ring(size, step):
    return [(i, (i + step) % size) for i in range(size)]


def split_three(matrix):
    high = matrix.astype(np.float32).astype(ml_dtypes.bfloat16)
    low = (matrix - high.astype(np.float64)).astype(ml_dtypes.bfloat16)
    return np.concatenate([high, high, low], axis=1)


def two_parts(value):
    high = value.astype(jnp.bfloat16)
    return high, (value - high.astype(jnp.float32)).astype(jnp.bfloat16)


def fft_tables(slow, count, azs):
    own = slow // azs
    h = np.arange(slow)
    place = np.concatenate([(-i * own + np.arange(own)) % slow for i in range(azs)])
    angle = 2 * np.pi * ((h[:, None] * place[None, :]) % slow) / slow
    first = np.block([[np.cos(angle), np.sin(angle)], [-np.sin(angle), np.cos(angle)]])
    b = np.arange(LANES)
    tables = []
    for me in range(azs):
        turn = 2 * np.pi * ((h[:, None] * (b[None, :] + me * own * LANES)) % count) / count
        tables.append(np.stack([np.cos(turn), -np.sin(turn)]))
    m = np.arange(count // slow)
    angle = 2 * np.pi * ((m[:, None] * b[None, :]) % LANES) / LANES
    second = np.block([[np.cos(angle), np.sin(angle)], [-np.sin(angle), np.cos(angle)]])
    second = second / math.sqrt(count)
    return split_three(first), np.stack(tables).astype(np.float32), split_three(second)


def fft_kernel(azs, own, peers, index_ref, *refs):
    inputs = refs[:azs]
    first_ref, turn_ref, second_ref = refs[azs : 3 + azs]
    out_ref, scratch = refs[-2:]
    slow = own * azs
    subs = LANES // peers
    me = index_ref[0]
    for part in range(2):
        for i in range(azs):
            for a in range(own):
                scratch[pl.ds(part * slow + i * own + a, SUB, stride=2 * slow), :] = inputs[i][
                    part, 0, :, a * LANES : (a + 1) * LANES
                ]
    for row in range(0, SUB, 2):
        x = jnp.concatenate(
            [scratch[(row + e) * 2 * slow : (row + e + 1) * 2 * slow, :] for e in range(2)], axis=1
        )
        high, low = two_parts(x)
        y = jnp.dot(
            first_ref[...],
            jnp.concatenate([high, low, high], axis=0),
            preferred_element_type=jnp.float32,
        )
        turned = []
        for e in range(2):
            real = y[:slow, e * LANES : (e + 1) * LANES]
            imag = y[slow:, e * LANES : (e + 1) * LANES]
            turned.append(
                jnp.concatenate(
                    [
                        real * turn_ref[me, 0] - imag * turn_ref[me, 1],
                        real * turn_ref[me, 1] + imag * turn_ref[me, 0],
                    ],
                    axis=1,
                )
            )
        high, low = two_parts(jnp.concatenate(turned, axis=0))
        z = lax.dot_general(
            second_ref[...],
            jnp.concatenate([high, low, high], axis=1),
            (((1,), (1,)), ((), ())),
            preferred_element_type=jnp.float32,
        )
        for part in range(2):
            for peer in range(peers):
                for e in range(2):
                    at = part * LANES + peer * subs
                    out_ref[peer, part, 0, pl.ds(row + e, subs, stride=SUB), :] = z[
                        at : at + subs, e * slow : (e + 1) * slow
                    ]


def fft_call(index, inputs, tables, peers, tiles, first, limit, prior=None):
    azs = len(inputs)
    steps = inputs[0].shape[1]
    own = inputs[0].shape[3] // LANES
    slow = own * azs
    subs = LANES // peers
    kept = prior is not None
    resident = steps == 1
    work = steps * SUB * slow * LANES
    if resident:
        specs = [RESIDENT] * (azs + 3)
    else:
        specs = [pl.BlockSpec((2, 1, SUB, own * LANES), lambda g: (0, g, 0, 0))] * azs
        specs += [pl.BlockSpec(t.shape, lambda g, n=t.ndim: (0,) * n) for t in tables]
    return pl.pallas_call(
        lambda *refs: fft_kernel(azs, own, peers, *refs),
        grid=(steps,),
        in_specs=[SCALARS] + specs + [pl.BlockSpec(memory_space=pl.ANY)] * kept,
        out_specs=pl.BlockSpec((peers, 2, 1, SUB * subs, LANES), lambda g: (0, 0, g + first, 0, 0)),
        out_shape=jax.ShapeDtypeStruct((peers, 2, tiles, SUB * subs, LANES), jnp.float32),
        scratch_shapes=[pltpu.VMEM((SUB * 2 * slow, LANES), jnp.float32)],
        input_output_aliases={azs + 4: 0} if kept else {},
        compiler_params=pltpu.CompilerParams(vmem_limit_bytes=limit),
        name="azimuth",
        cost_estimate=pl.CostEstimate(
            flops=work * 2 * 8 * LANES * 3, bytes_accessed=work * 16, transcendentals=0
        ),
    )(index, *inputs, *tables, *([prior] if kept else []))


def band_matrix(taps, lead, total_in, me, azs):
    width, total = taps.shape[1:]
    tap = jnp.arange(total_in, dtype=jnp.int32)[None, :] - jnp.arange(total, dtype=jnp.int32)[:, None] + lead
    hit = tap[:, :, None] == jnp.arange(width, dtype=jnp.int32)
    table = jnp.transpose(taps, (0, 2, 1))
    band = jnp.sum(jnp.where(hit[None], table[:, :, None, :], 0.0), axis=3)
    real = jnp.concatenate([band[0], -band[1]], axis=1)
    imag = jnp.concatenate([band[1], band[0]], axis=1)
    both = jnp.stack([real, imag]).reshape(2, total // (azs * SUB), azs, SUB, 2 * total_in)
    both = jnp.transpose(both, (2, 0, 1, 3, 4)).reshape(azs, -1, 2 * total_in)
    both = lax.dynamic_slice_in_dim(jnp.concatenate([both, both]), me, azs, 0)
    return jnp.tile(both.reshape(-1, 2 * total_in), (1, 3))


def rounded_weights(w):
    columns = w.shape[1] // 3
    rounded = w.astype(jnp.bfloat16).astype(jnp.float32)
    low_part = lax.broadcasted_iota(jnp.int32, w.shape, 1) >= 2 * columns
    return jnp.where(low_part, w - rounded, rounded).astype(jnp.bfloat16)


def weighted(weights, blocks):
    high, low = two_parts(jnp.concatenate(blocks, axis=0))
    return jnp.dot(
        weights, jnp.concatenate([high, low, high], axis=0), preferred_element_type=jnp.float32
    )


def early_filter_kernel(azs, width, w_ref, before, own, after, *outs):
    weights = rounded_weights(w_ref[...])

    def body(step, _):
        at = pl.ds(pl.multiple_of(step * width, width), width)
        y = weighted(
            weights,
            [
                block
                for part in range(2)
                for block in (before[part, 0, :, at], own[part, 0, :, at], after[part, 0, :, at])
            ],
        )
        for i in range(azs):
            for part in range(2):
                row = (i * 2 + part) * SUB
                outs[i][part, 0, :, at] = y[row : row + SUB]
        return 0

    lax.fori_loop(0, own.shape[3] // width, body, 0, unroll=2)


def early_filter_call(weights, before, raw, after, at, azs):
    _, count, _, pulses = before.shape
    rows = raw.shape[2]
    out = jax.ShapeDtypeStruct((2, count, SUB, pulses), jnp.float32)
    edge = pl.BlockSpec((2, 1, SUB, pulses), lambda g: (0, g, 0, 0))
    return pl.pallas_call(
        lambda *refs: early_filter_kernel(azs, 4 * LANES, *refs),
        grid=(count,),
        in_specs=[
            pl.BlockSpec(weights.shape, lambda g: (0, 0)),
            edge,
            pl.BlockSpec((2, 1, rows, pulses), lambda g: (0, g + at, 0, 0)),
            edge,
        ],
        out_specs=[edge] * azs,
        out_shape=[out] * azs,
        compiler_params=pltpu.CompilerParams(vmem_limit_bytes=WHOLE),
        name="strip_filter",
        cost_estimate=pl.CostEstimate(
            flops=2 * weights.shape[0] * weights.shape[1] * count * pulses,
            bytes_accessed=24 * count * rows * pulses,
            transcendentals=0,
        ),
    )(weights, before, raw, after)


def late_filter_kernel(azs, w_ref, in_ref, *outs):
    weights = rounded_weights(w_ref[...])
    strips, _, tiles, depth, _ = in_ref.shape
    subs = depth // SUB
    chan = pl.program_id(0)
    step = 2 if subs % 2 == 0 else 1

    for sub in range(0, subs, step):
        y = weighted(
            weights,
            [
                jnp.concatenate(
                    [
                        in_ref[strip, part, tile, (sub + s) * SUB : (sub + s + 1) * SUB, :]
                        for s in range(step)
                    ],
                    axis=1,
                )
                for part in range(2)
                for strip in range(strips)
                for tile in range(tiles)
            ],
        )
        at = 0
        for i in range(azs):
            for part in range(2):
                for strip in range(strips):
                    for s in range(step):
                        outs[i][part, chan, strip, sub + s, :, :] = y[
                            at : at + SUB, s * LANES : (s + 1) * LANES
                        ]
                    at += SUB


def late_filter_call(weights, moved, chans, azs):
    peers, _, _, depth, _ = moved.shape
    strips, subs = peers // chans, depth // SUB
    out = jax.ShapeDtypeStruct((2, chans, strips, subs, SUB, LANES), jnp.float32)
    return pl.pallas_call(
        lambda *refs: late_filter_kernel(azs, *refs),
        grid=(chans,),
        in_specs=[
            pl.BlockSpec(weights.shape, lambda g: (0, 0)),
            pl.BlockSpec((strips,) + moved.shape[1:], lambda g: (g, 0, 0, 0, 0)),
        ],
        out_specs=[RESIDENT] * azs,
        out_shape=[out] * azs,
        compiler_params=pltpu.CompilerParams(vmem_limit_bytes=32 << 20),
        name="range_filter",
        cost_estimate=pl.CostEstimate(
            flops=2 * weights.shape[0] * weights.shape[1] * chans * subs * LANES,
            bytes_accessed=8 * math.prod(moved.shape),
            transcendentals=0,
        ),
    )(weights, moved)


def mix_kernel(sources, matrix, total, strips, kept, out_ref, prior, scratch):
    for n, value in enumerate(sources):
        for s in range(strips):
            dr, di = value(s)
            scratch[n, s] = dr + di

    def body(row, _):
        totals = None
        for n, value in enumerate(sources):
            ar = jnp.broadcast_to(matrix(0, row, n), (SUB, LANES))
            ai = jnp.broadcast_to(matrix(1, row, n), (SUB, LANES))
            both = ar + ai
            terms = []
            for s in range(strips):
                dr, di = value(s)
                terms += [ar * dr, ai * di, both * scratch[n, s]]
            totals = terms if totals is None else [t + u for t, u in zip(totals, terms)]
        for s in range(strips):
            first, second, third = totals[3 * s : 3 * s + 3]
            real, imag = first - second, third - first - second
            if kept:
                out_ref[0, row, s] = real + prior[0, 0, row, s]
                out_ref[1, row, s] = imag + prior[0, 1, row, s]
            else:
                out_ref[0, 0, row, s] = real
                out_ref[0, 1, row, s] = imag
        return 0

    lax.fori_loop(0, total, body, 0, unroll=math.gcd(total, 8))


def mix_late_kernel(azs, chans, local, rest, index_ref, slot_ref, *refs):
    data, mats = refs[:azs], refs[azs : 2 * azs]
    out_ref, next_ref, own, scratch = refs[2 * azs :]
    me = index_ref[0]
    g = pl.program_id(0)
    strips = data[0].shape[2]
    here = mats[0].shape[1]
    late = [(i, chan) for i in range(azs) for chan in range(chans)]
    late_slots = [slot_ref[chan * local + lax.rem(me - i + azs, azs)] for i, chan in late]
    next_slots = [slot_ref[chan * local + azs + c] for chan in range(chans) for c in range(rest)]
    for j in range(azs):
        base = lax.rem(me - j + azs, azs) * here

        def arrange(row, _, j=j, base=base):
            for part in range(2):
                for n, slot in enumerate(late_slots):
                    own[part, base + row, n : n + 1, :] = mats[j][part, row, pl.ds(slot, 1), :]
                for n, slot in enumerate(next_slots):
                    next_ref[0, part, base + row, n : n + 1, :] = mats[j][part, row, pl.ds(slot, 1), :]
            return 0

        lax.fori_loop(0, here, arrange, 0, unroll=2)
    sources = [
        lambda s, i=i, chan=chan: (data[i][0, chan, s, g], data[i][1, chan, s, g]) for i, chan in late
    ]
    mix_kernel(
        sources,
        lambda part, row, n: own[part, row, n : n + 1, :],
        here * azs,
        strips,
        False,
        out_ref,
        None,
        scratch,
    )


def mix_late_call(index, slots, data, mats, chans, local, rest):
    azs = len(mats)
    _, _, strips, subs, _, _ = data[0].shape
    here = mats[0].shape[1]
    total = here * azs
    sums = jax.ShapeDtypeStruct((subs, 2, total, strips, SUB, LANES), jnp.float32)
    arranged = jax.ShapeDtypeStruct((subs, 2, total, chans * rest, LANES), jnp.float32)
    return pl.pallas_call(
        lambda *refs: mix_late_kernel(azs, chans, local, rest, *refs),
        grid=(subs,),
        in_specs=[SCALARS] * 2
        + [RESIDENT] * azs
        + [pl.BlockSpec(mats[0].shape[:3] + (LANES,), lambda g: (0, 0, 0, g))] * azs,
        out_specs=[
            pl.BlockSpec((1,) + sums.shape[1:], lambda g: (g, 0, 0, 0, 0, 0)),
            pl.BlockSpec((1,) + arranged.shape[1:], lambda g: (g, 0, 0, 0, 0)),
        ],
        out_shape=[sums, arranged],
        scratch_shapes=[
            pltpu.VMEM((2, total, chans * azs, LANES), jnp.float32),
            pltpu.VMEM((chans * azs, strips, SUB, LANES), jnp.float32),
        ],
        compiler_params=pltpu.CompilerParams(vmem_limit_bytes=50 << 20),
        name="reconstruct_late",
        cost_estimate=pl.CostEstimate(
            flops=8 * total * strips * SUB * subs * LANES * chans * azs,
            bytes_accessed=4 * math.prod(sums.shape),
            transcendentals=0,
        ),
    )(index, slots, *data, *mats)


def mix_early_kernel(chans, rest, data, mats, prior, out_ref, scratch):
    g = pl.program_id(0)
    strips = data.shape[0] // chans
    at = pl.ds(pl.multiple_of(g * SUB, SUB), SUB)
    sources = [
        lambda s, c=c, chan=chan: tuple(data[chan * strips + s, p, c, at, :] for p in range(2))
        for chan in range(chans)
        for c in range(rest)
    ]
    mix_kernel(
        sources,
        lambda part, row, n: mats[0, part, row, n : n + 1, :],
        prior.shape[2],
        strips,
        True,
        out_ref,
        prior,
        scratch,
    )


def mix_early_call(early, mats, prior, chans, rest):
    subs, _, total, strips, _, _ = prior.shape
    out = jax.ShapeDtypeStruct((2, total, strips, SUB, subs * LANES), jnp.float32)
    return pl.pallas_call(
        lambda *refs: mix_early_kernel(chans, rest, *refs),
        grid=(subs,),
        in_specs=[
            RESIDENT,
            pl.BlockSpec((1,) + mats.shape[1:], lambda g: (g, 0, 0, 0, 0)),
            pl.BlockSpec((1,) + prior.shape[1:], lambda g: (g, 0, 0, 0, 0, 0)),
        ],
        out_specs=pl.BlockSpec((2, total, strips, SUB, LANES), lambda g: (0, 0, 0, 0, g)),
        out_shape=out,
        scratch_shapes=[pltpu.VMEM((chans * rest, strips, SUB, LANES), jnp.float32)],
        compiler_params=pltpu.CompilerParams(vmem_limit_bytes=50 << 20),
        name="reconstruct",
        cost_estimate=pl.CostEstimate(
            flops=8 * math.prod(out.shape) * chans * rest,
            bytes_accessed=8 * math.prod(out.shape),
            transcendentals=0,
        ),
    )(early, mats, prior)


def with_halo(shard, sides, width):
    for axis, dim in sides:
        size, length = (lax.axis_size(axis), shard.shape[dim])
        up = [(i, (i + 1) % size) for i in range(size - 1)]
        down = [(j, i) for i, j in up]
        last = lax.slice_in_dim(shard, length - width, length, axis=dim)
        leading = lax.slice_in_dim(shard, 0, width, axis=dim)
        before = lax.ppermute(last, axis, up)
        after = lax.ppermute(leading, axis, down)
        shard = jnp.concatenate([before, shard, after], axis=dim)
    return shard


def phases(first, second, length):
    left = jnp.arange(first, dtype=jnp.int32)
    right = jnp.arange(second, dtype=jnp.int32)
    product = left[:, None] * right[None, :] % length
    angle = product.astype(jnp.float32) * (2.0 * math.pi / length)
    return (jnp.cos(angle), jnp.sin(angle))


def azimuth_fft(block):
    count = block.shape[-1]
    rows = math.isqrt(count)
    while count % rows:
        rows = rows - 1
    cols = count // rows
    lead = block.shape[1:-1]
    high = lax.Precision.HIGHEST
    real_in = block[0].reshape(lead + (rows, cols))
    imag_in = block[1].reshape(lead + (rows, cols))
    cosine_first, sine_first = phases(rows, rows, rows)
    first_real = jnp.einsum("...ab,af->...bf", real_in, cosine_first, precision=high) + jnp.einsum(
        "...ab,af->...bf", imag_in, sine_first, precision=high
    )
    first_imag = jnp.einsum("...ab,af->...bf", imag_in, cosine_first, precision=high) - jnp.einsum(
        "...ab,af->...bf", real_in, sine_first, precision=high
    )
    twist_cos, twist_sin = phases(cols, rows, count)
    turned_real = first_real * twist_cos + first_imag * twist_sin
    turned_imag = first_imag * twist_cos - first_real * twist_sin
    cosine_second, sine_second = phases(cols, cols, cols)
    out_real = jnp.einsum(
        "...bf,bg->...gf", turned_real, cosine_second, precision=high
    ) + jnp.einsum("...bf,bg->...gf", turned_imag, sine_second, precision=high)
    out_imag = jnp.einsum(
        "...bf,bg->...gf", turned_imag, cosine_second, precision=high
    ) - jnp.einsum("...bf,bg->...gf", turned_real, sine_second, precision=high)
    scale = 1.0 / math.sqrt(count)
    return jnp.stack([out_real.reshape(lead + (count,)), out_imag.reshape(lead + (count,))]) * scale


def general_shards(raw, taps, recon, channel_slot):
    width = taps.shape[1]
    half = (width - 1) // 2
    strip_rows = raw.shape[2]
    padded = with_halo(raw, (("rng", 2),), half)
    real_part = jnp.zeros(raw.shape[1:], jnp.float32)
    imag_part = jnp.zeros(raw.shape[1:], jnp.float32)
    for offset in range(width):
        seg_real = padded[0, :, offset : offset + strip_rows, :]
        seg_imag = padded[1, :, offset : offset + strip_rows, :]
        tap_real = taps[0, offset][None, :, None]
        tap_imag = taps[1, offset][None, :, None]
        real_part = real_part + tap_real * seg_real - tap_imag * seg_imag
        imag_part = imag_part + tap_real * seg_imag + tap_imag * seg_real
    filtered = jnp.stack([real_part, imag_part])
    spectrum = azimuth_fft(lax.all_to_all(filtered, "az", split_axis=2, concat_axis=3, tiled=True))
    strips = lax.axis_size("rng")
    groups = lax.axis_size("chan")
    local_channels = spectrum.shape[1]
    local_range = spectrum.shape[2]
    moved = lax.all_to_all(
        spectrum[:, None], ("chan", "rng"), split_axis=4, concat_axis=1, tiled=True
    )
    bins = moved.shape[-1]
    moved = moved.reshape((2, groups, strips, local_channels, local_range, bins))
    doppler = jnp.transpose(moved, (0, 1, 3, 2, 4, 5)).reshape(
        (2, groups * local_channels, strips * local_range, bins)
    )
    channels = doppler.shape[1]
    selector = (channel_slot[:, None] == jnp.arange(channels, dtype=jnp.int32)[None, :]).astype(
        jnp.float32
    )
    piece = lax.all_gather(recon, "az", axis=1, tiled=True)
    arranged = jnp.einsum("pkjf,cj->pkcf", piece, selector, precision=lax.Precision.HIGHEST)
    shape = (piece.shape[1], doppler.shape[2], doppler.shape[3])
    out_real = jnp.zeros(shape, jnp.float32)
    out_imag = jnp.zeros(shape, jnp.float32)
    for channel in range(channels):
        mat_real = arranged[0, :, channel, None, :]
        mat_imag = arranged[1, :, channel, None, :]
        data_real = doppler[0, channel][None]
        data_imag = doppler[1, channel][None]
        out_real = out_real + mat_real * data_real - mat_imag * data_imag
        out_imag = out_imag + mat_real * data_imag + mat_imag * data_real
    result = jnp.stack([out_real, out_imag])
    total_range = result.shape[2]
    return result.reshape((2, result.shape[1], strips, total_range // strips, result.shape[3]))


def shards(raw, taps, recon, channel_slot):
    chans, azs, strips = (lax.axis_size(n) for n in ("chan", "az", "rng"))
    _, local, rows, pulses = raw.shape
    width = taps.shape[1]
    half = (width - 1) // 2
    peers = chans * strips
    fits = local > azs and rows == azs * SUB and pulses * azs == LANES * LANES and half == SUB
    if not (fits and LANES % peers == 0):
        return general_shards(raw, taps, recon, channel_slot)
    me = lax.axis_index("az").astype(jnp.int32)
    index = me[None]
    count = pulses * azs
    slow = count // LANES
    tables = [jnp.asarray(t) for t in fft_tables(slow, count, azs)]
    rest = local - azs

    def give(step, at):
        to = lax.rem(me + step, azs)
        block = lax.dynamic_slice(raw, (0, to, at, 0), (2, 1, SUB, pulses))
        return lax.ppermute(block, "az", ring(azs, step)) if step else block

    def turn(spectra):
        return lax.all_to_all(spectra, ("chan", "rng"), 0, 0, tiled=True)

    received = [[give(i, n * SUB) for i in range(azs)] for n in range(rows // SUB)]
    near = lax.axis_index("rng").astype(jnp.int32)
    parts = [taps] + [lax.ppermute(taps, "rng", ring(strips, strips - i)) for i in range(1, strips)]
    strip = jnp.arange(strips, dtype=jnp.int32)[:, None, None, None]
    all_taps = sum(
        jnp.where(strip == lax.rem(near + i, strips), part[None], 0.0) for i, part in enumerate(parts)
    )
    all_taps = jnp.transpose(all_taps, (1, 2, 0, 3)).reshape(2, width, strips * rows)
    up = ring(strips, 1)[:-1]
    down = [(b, a) for a, b in up]
    before = lax.ppermute(raw[:, azs:, rows - half :, :], "rng", up)
    after = lax.ppermute(raw[:, azs:, :half, :], "rng", down)

    early_weights = band_matrix(taps, 0, rows + 2 * half, me, azs)
    late_weights = band_matrix(all_taps, half, strips * rows, me, azs)

    spectra = None
    for n in range(rows // SUB):
        spectra = fft_call(index, received[n], tables, peers, rows // SUB, n, 32 << 20, spectra)
    late = turn(spectra)

    filtered = early_filter_call(early_weights, before, raw, after, azs, azs)
    swapped = [filtered[0]] + [lax.ppermute(filtered[i], "az", ring(azs, i)) for i in range(1, azs)]
    mats = [recon] + [lax.ppermute(recon, "az", ring(azs, i)) for i in range(1, azs)]
    swapped[0], late_weights = lax.optimization_barrier((swapped[0], late_weights))
    spectra = fft_call(index, swapped, tables, peers, rest, 0, WHOLE)
    early = turn(spectra)

    filtered = late_filter_call(late_weights, late, chans, azs)
    data = [filtered[0]] + [lax.ppermute(filtered[i], "az", ring(azs, i)) for i in range(1, azs)]

    sums, arranged = mix_late_call(index, channel_slot, data, mats, chans, local, rest)
    return mix_early_call(early, arranged, sums, chans, rest)


def solution(mesh):
    return jax.shard_map(
        shards,
        mesh=mesh,
        in_specs=(
            P(None, "chan", "rng", "az"),
            P(None, None, "rng"),
            P(None, "az", None, ("chan", "rng")),
            P(),
        ),
        out_specs=P(None, None, None, "az", ("chan", "rng")),
        check_vma=False,
    )
```

```python
import math

import jax
import jax.numpy as jnp
import ml_dtypes
import numpy as np
from jax import lax
from jax.experimental import pallas as pl
from jax.experimental.pallas import tpu as pltpu
from jax.sharding import PartitionSpec as P


LANES = 128
SUB = 8
RESIDENT = pl.BlockSpec(memory_space=pltpu.VMEM)
SCALARS = pl.BlockSpec(memory_space=pltpu.SMEM)
WHOLE = 67043328


def ring(size, step):
    return [(i, (i + step) % size) for i in range(size)]


def split_three(matrix):
    high = matrix.astype(np.float32).astype(ml_dtypes.bfloat16)
    low = (matrix - high.astype(np.float64)).astype(ml_dtypes.bfloat16)
    return np.concatenate([high, high, low], axis=1)


def two_parts(value):
    high = value.astype(jnp.bfloat16)
    return high, (value - high.astype(jnp.float32)).astype(jnp.bfloat16)


def fft_tables(slow, count, azs):
    own = slow // azs
    h = np.arange(slow)
    place = np.concatenate([(-i * own + np.arange(own)) % slow for i in range(azs)])
    angle = 2 * np.pi * ((h[:, None] * place[None, :]) % slow) / slow
    first = np.block([[np.cos(angle), np.sin(angle)], [-np.sin(angle), np.cos(angle)]])
    b = np.arange(LANES)
    tables = []
    for me in range(azs):
        turn = 2 * np.pi * ((h[:, None] * (b[None, :] + me * own * LANES)) % count) / count
        tables.append(np.stack([np.cos(turn), -np.sin(turn)]))
    m = np.arange(count // slow)
    angle = 2 * np.pi * ((m[:, None] * b[None, :]) % LANES) / LANES
    second = np.block([[np.cos(angle), np.sin(angle)], [-np.sin(angle), np.cos(angle)]])
    second = second / math.sqrt(count)
    return split_three(first), np.stack(tables).astype(np.float32), split_three(second)


def fft_kernel(azs, own, peers, index_ref, *refs):
    inputs = refs[:azs]
    first_ref, turn_ref, second_ref = refs[azs : 3 + azs]
    out_ref, scratch = refs[-2:]
    slow = own * azs
    subs = LANES // peers
    me = index_ref[0]
    for part in range(2):
        for i in range(azs):
            for a in range(own):
                scratch[pl.ds(part * slow + i * own + a, SUB, stride=2 * slow), :] = inputs[i][
                    part, 0, :, a * LANES : (a + 1) * LANES
                ]
    for row in range(0, SUB, 2):
        x = jnp.concatenate(
            [scratch[(row + e) * 2 * slow : (row + e + 1) * 2 * slow, :] for e in range(2)], axis=1
        )
        high, low = two_parts(x)
        y = jnp.dot(
            first_ref[...],
            jnp.concatenate([high, low, high], axis=0),
            preferred_element_type=jnp.float32,
        )
        turned = []
        for e in range(2):
            real = y[:slow, e * LANES : (e + 1) * LANES]
            imag = y[slow:, e * LANES : (e + 1) * LANES]
            turned.append(
                jnp.concatenate(
                    [
                        real * turn_ref[me, 0] - imag * turn_ref[me, 1],
                        real * turn_ref[me, 1] + imag * turn_ref[me, 0],
                    ],
                    axis=1,
                )
            )
        high, low = two_parts(jnp.concatenate(turned, axis=0))
        z = lax.dot_general(
            second_ref[...],
            jnp.concatenate([high, low, high], axis=1),
            (((1,), (1,)), ((), ())),
            preferred_element_type=jnp.float32,
        )
        for part in range(2):
            for peer in range(peers):
                for e in range(2):
                    at = part * LANES + peer * subs
                    out_ref[peer, part, 0, pl.ds(row + e, subs, stride=SUB), :] = z[
                        at : at + subs, e * slow : (e + 1) * slow
                    ]


def fft_tile_kernel(azs, own, peers, tile, index_ref, *refs):
    out_ref, scratch, block, done = refs[-4:]
    fft_kernel(azs, own, peers, index_ref, *refs[: azs + 3], block, scratch)
    copy = pltpu.make_async_copy(block, out_ref.at[:, :, pl.ds(tile, 1)], done)
    copy.start()
    copy.wait()


def fft_call(index, inputs, tables, peers, tiles, first, limit, prior=None):
    azs = len(inputs)
    steps = inputs[0].shape[1]
    own = inputs[0].shape[3] // LANES
    slow = own * azs
    subs = LANES // peers
    kept = prior is not None
    work = steps * SUB * slow * LANES
    tile = (peers, 2, 1, SUB * subs, LANES)
    scratch = [pltpu.VMEM((SUB * 2 * slow, LANES), jnp.float32)]
    if steps == 1:
        how = dict(
            in_specs=[SCALARS] + [RESIDENT] * (azs + 3) + [pl.BlockSpec(memory_space=pl.ANY)] * kept,
            out_specs=pl.BlockSpec(memory_space=pl.ANY),
            scratch_shapes=scratch + [pltpu.VMEM(tile, jnp.float32), pltpu.SemaphoreType.DMA],
            input_output_aliases={azs + 4: 0} if kept else {},
        )
        kernel = lambda *refs: fft_tile_kernel(azs, own, peers, first, *refs)
    else:
        how = dict(
            grid=(steps,),
            in_specs=[SCALARS]
            + [pl.BlockSpec((2, 1, SUB, own * LANES), lambda g: (0, g, 0, 0))] * azs
            + [pl.BlockSpec(t.shape, lambda g, n=t.ndim: (0,) * n) for t in tables],
            out_specs=pl.BlockSpec(tile, lambda g: (0, 0, g + first, 0, 0)),
            scratch_shapes=scratch,
        )
        kernel = lambda *refs: fft_kernel(azs, own, peers, *refs)
    return pl.pallas_call(
        kernel,
        out_shape=jax.ShapeDtypeStruct((peers, 2, tiles, SUB * subs, LANES), jnp.float32),
        compiler_params=pltpu.CompilerParams(vmem_limit_bytes=limit),
        name="azimuth",
        cost_estimate=pl.CostEstimate(
            flops=work * 2 * 8 * LANES * 3, bytes_accessed=work * 16, transcendentals=0
        ),
        **how,
    )(index, *inputs, *tables, *([prior] if kept else []))


def band_matrix(taps, lead, total_in, me, azs):
    width, total = taps.shape[1:]
    tap = jnp.arange(total_in, dtype=jnp.int32)[None, :] - jnp.arange(total, dtype=jnp.int32)[:, None] + lead
    hit = tap[:, :, None] == jnp.arange(width, dtype=jnp.int32)
    table = jnp.transpose(taps, (0, 2, 1))
    band = jnp.sum(jnp.where(hit[None], table[:, :, None, :], 0.0), axis=3)
    real = jnp.concatenate([band[0], -band[1]], axis=1)
    imag = jnp.concatenate([band[1], band[0]], axis=1)
    both = jnp.stack([real, imag]).reshape(2, total // (azs * SUB), azs, SUB, 2 * total_in)
    both = jnp.transpose(both, (2, 0, 1, 3, 4)).reshape(azs, -1, 2 * total_in)
    both = lax.dynamic_slice_in_dim(jnp.concatenate([both, both]), me, azs, 0)
    return jnp.tile(both.reshape(-1, 2 * total_in), (1, 3))


def rounded_weights(w):
    columns = w.shape[1] // 3
    rounded = w.astype(jnp.bfloat16).astype(jnp.float32)
    low_part = lax.broadcasted_iota(jnp.int32, w.shape, 1) >= 2 * columns
    return jnp.where(low_part, w - rounded, rounded).astype(jnp.bfloat16)


def weighted(weights, blocks):
    high, low = two_parts(jnp.concatenate(blocks, axis=0))
    return jnp.dot(
        weights, jnp.concatenate([high, low, high], axis=0), preferred_element_type=jnp.float32
    )


def early_filter_kernel(azs, width, w_ref, before, own, after, *outs):
    weights = rounded_weights(w_ref[...])

    def body(step, _):
        at = pl.ds(pl.multiple_of(step * width, width), width)
        y = weighted(
            weights,
            [
                block
                for part in range(2)
                for block in (before[part, 0, :, at], own[part, 0, :, at], after[part, 0, :, at])
            ],
        )
        for i in range(azs):
            for part in range(2):
                row = (i * 2 + part) * SUB
                outs[i][part, 0, :, at] = y[row : row + SUB]
        return 0

    lax.fori_loop(0, own.shape[3] // width, body, 0, unroll=2)


def early_filter_call(weights, before, raw, after, at, azs):
    _, count, _, pulses = before.shape
    rows = raw.shape[2]
    out = jax.ShapeDtypeStruct((2, count, SUB, pulses), jnp.float32)
    edge = pl.BlockSpec((2, 1, SUB, pulses), lambda g: (0, g, 0, 0))
    return pl.pallas_call(
        lambda *refs: early_filter_kernel(azs, 4 * LANES, *refs),
        grid=(count,),
        in_specs=[
            pl.BlockSpec(weights.shape, lambda g: (0, 0)),
            edge,
            pl.BlockSpec((2, 1, rows, pulses), lambda g: (0, g + at, 0, 0)),
            edge,
        ],
        out_specs=[edge] * azs,
        out_shape=[out] * azs,
        compiler_params=pltpu.CompilerParams(vmem_limit_bytes=WHOLE),
        name="strip_filter",
        cost_estimate=pl.CostEstimate(
            flops=2 * weights.shape[0] * weights.shape[1] * count * pulses,
            bytes_accessed=24 * count * rows * pulses,
            transcendentals=0,
        ),
    )(weights, before, raw, after)


def late_filter_kernel(azs, w_ref, in_ref, *outs):
    weights = rounded_weights(w_ref[...])
    strips, _, tiles, depth, _ = in_ref.shape
    subs = depth // SUB
    chan = pl.program_id(0)
    step = 2 if subs % 2 == 0 else 1

    for sub in range(0, subs, step):
        y = weighted(
            weights,
            [
                jnp.concatenate(
                    [
                        in_ref[strip, part, tile, (sub + s) * SUB : (sub + s + 1) * SUB, :]
                        for s in range(step)
                    ],
                    axis=1,
                )
                for part in range(2)
                for strip in range(strips)
                for tile in range(tiles)
            ],
        )
        at = 0
        for i in range(azs):
            for part in range(2):
                for strip in range(strips):
                    for s in range(step):
                        outs[i][part, chan, strip, sub + s, :, :] = y[
                            at : at + SUB, s * LANES : (s + 1) * LANES
                        ]
                    at += SUB


def late_filter_call(weights, moved, chans, azs):
    peers, _, _, depth, _ = moved.shape
    strips, subs = peers // chans, depth // SUB
    out = jax.ShapeDtypeStruct((2, chans, strips, subs, SUB, LANES), jnp.float32)
    return pl.pallas_call(
        lambda *refs: late_filter_kernel(azs, *refs),
        grid=(chans,),
        in_specs=[
            pl.BlockSpec(weights.shape, lambda g: (0, 0)),
            pl.BlockSpec((strips,) + moved.shape[1:], lambda g: (g, 0, 0, 0, 0)),
        ],
        out_specs=[RESIDENT] * azs,
        out_shape=[out] * azs,
        compiler_params=pltpu.CompilerParams(vmem_limit_bytes=32 << 20),
        name="range_filter",
        cost_estimate=pl.CostEstimate(
            flops=2 * weights.shape[0] * weights.shape[1] * chans * subs * LANES,
            bytes_accessed=8 * math.prod(moved.shape),
            transcendentals=0,
        ),
    )(weights, moved)


def mix_kernel(sources, matrix, total, strips, kept, out_ref, prior, scratch):
    for n, value in enumerate(sources):
        for s in range(strips):
            dr, di = value(s)
            scratch[n, s] = dr + di

    def body(row, _):
        totals = None
        for n, value in enumerate(sources):
            ar = jnp.broadcast_to(matrix(0, row, n), (SUB, LANES))
            ai = jnp.broadcast_to(matrix(1, row, n), (SUB, LANES))
            both = ar + ai
            terms = []
            for s in range(strips):
                dr, di = value(s)
                terms += [ar * dr, ai * di, both * scratch[n, s]]
            totals = terms if totals is None else [t + u for t, u in zip(totals, terms)]
        for s in range(strips):
            first, second, third = totals[3 * s : 3 * s + 3]
            real, imag = first - second, third - first - second
            if kept:
                out_ref[0, row, s] = real + prior[0, 0, row, s]
                out_ref[1, row, s] = imag + prior[0, 1, row, s]
            else:
                out_ref[0, 0, row, s] = real
                out_ref[0, 1, row, s] = imag
        return 0

    lax.fori_loop(0, total, body, 0, unroll=math.gcd(total, 16 if kept else 8))


def mix_late_kernel(azs, chans, local, rest, index_ref, slot_ref, *refs):
    data, mats = refs[:azs], refs[azs : 2 * azs]
    out_ref, next_ref, own, scratch = refs[2 * azs :]
    me = index_ref[0]
    strips = data[0].shape[2]
    here = mats[0].shape[1]
    late = [(i, chan) for i in range(azs) for chan in range(chans)]
    late_slots = [slot_ref[chan * local + lax.rem(me - i + azs, azs)] for i, chan in late]
    next_slots = [slot_ref[chan * local + azs + c] for chan in range(chans) for c in range(rest)]
    for j in range(azs):
        base = lax.rem(me - j + azs, azs) * here

        def arrange(row, _, j=j, base=base):
            for part in range(2):
                for n, slot in enumerate(late_slots):
                    own[part, base + row, n : n + 1, :] = mats[j][part, row, pl.ds(slot, 1), :]
                for n, slot in enumerate(next_slots):
                    next_ref[0, part, base + row, n : n + 1, :] = mats[j][part, row, pl.ds(slot, 1), :]
            return 0

        lax.fori_loop(0, here, arrange, 0, unroll=2)
    sources = [
        lambda s, i=i, chan=chan: (data[i][0, chan, s, 0], data[i][1, chan, s, 0]) for i, chan in late
    ]
    mix_kernel(
        sources,
        lambda part, row, n: own[part, row, n : n + 1, :],
        here * azs,
        strips,
        False,
        out_ref,
        None,
        scratch,
    )


def mix_late_call(index, slots, data, mats, chans, local, rest):
    azs = len(mats)
    _, _, strips, subs, _, _ = data[0].shape
    here = mats[0].shape[1]
    total = here * azs
    sums = jax.ShapeDtypeStruct((subs, 2, total, strips, SUB, LANES), jnp.float32)
    arranged = jax.ShapeDtypeStruct((subs, 2, total, chans * rest, LANES), jnp.float32)
    return pl.pallas_call(
        lambda *refs: mix_late_kernel(azs, chans, local, rest, *refs),
        grid=(subs,),
        in_specs=[SCALARS] * 2
        + [pl.BlockSpec((2, chans, strips, 1, SUB, LANES), lambda g: (0, 0, 0, g, 0, 0))] * azs
        + [pl.BlockSpec(mats[0].shape[:3] + (LANES,), lambda g: (0, 0, 0, g))] * azs,
        out_specs=[
            pl.BlockSpec((1,) + sums.shape[1:], lambda g: (g, 0, 0, 0, 0, 0)),
            pl.BlockSpec((1,) + arranged.shape[1:], lambda g: (g, 0, 0, 0, 0)),
        ],
        out_shape=[sums, arranged],
        scratch_shapes=[
            pltpu.VMEM((2, total, chans * azs, LANES), jnp.float32),
            pltpu.VMEM((chans * azs, strips, SUB, LANES), jnp.float32),
        ],
        compiler_params=pltpu.CompilerParams(vmem_limit_bytes=50 << 20),
        name="reconstruct_late",
        cost_estimate=pl.CostEstimate(
            flops=8 * total * strips * SUB * subs * LANES * chans * azs,
            bytes_accessed=4 * math.prod(sums.shape),
            transcendentals=0,
        ),
    )(index, slots, *data, *mats)


def mix_early_kernel(chans, rest, data, mats, prior, out_ref, scratch):
    strips = data.shape[0] // chans
    sources = [
        lambda s, c=c, chan=chan: tuple(data[chan * strips + s, p, c] for p in range(2))
        for chan in range(chans)
        for c in range(rest)
    ]
    mix_kernel(
        sources,
        lambda part, row, n: mats[0, part, row, n : n + 1, :],
        prior.shape[2],
        strips,
        True,
        out_ref,
        prior,
        scratch,
    )


def mix_early_call(early, mats, prior, chans, rest):
    subs, _, total, strips, _, _ = prior.shape
    out = jax.ShapeDtypeStruct((2, total, strips, SUB, subs * LANES), jnp.float32)
    return pl.pallas_call(
        lambda *refs: mix_early_kernel(chans, rest, *refs),
        grid=(subs,),
        in_specs=[
            pl.BlockSpec(early.shape[:3] + (SUB, LANES), lambda g: (0, 0, 0, g, 0)),
            pl.BlockSpec((1,) + mats.shape[1:], lambda g: (g, 0, 0, 0, 0)),
            pl.BlockSpec((1,) + prior.shape[1:], lambda g: (g, 0, 0, 0, 0, 0)),
        ],
        out_specs=pl.BlockSpec((2, total, strips, SUB, LANES), lambda g: (0, 0, 0, 0, g)),
        out_shape=out,
        scratch_shapes=[pltpu.VMEM((chans * rest, strips, SUB, LANES), jnp.float32)],
        compiler_params=pltpu.CompilerParams(vmem_limit_bytes=50 << 20),
        name="reconstruct",
        cost_estimate=pl.CostEstimate(
            flops=8 * math.prod(out.shape) * chans * rest,
            bytes_accessed=8 * math.prod(out.shape),
            transcendentals=0,
        ),
    )(early, mats, prior)


def with_halo(shard, sides, width):
    for axis, dim in sides:
        size, length = (lax.axis_size(axis), shard.shape[dim])
        up = [(i, (i + 1) % size) for i in range(size - 1)]
        down = [(j, i) for i, j in up]
        last = lax.slice_in_dim(shard, length - width, length, axis=dim)
        leading = lax.slice_in_dim(shard, 0, width, axis=dim)
        before = lax.ppermute(last, axis, up)
        after = lax.ppermute(leading, axis, down)
        shard = jnp.concatenate([before, shard, after], axis=dim)
    return shard


def phases(first, second, length):
    left = jnp.arange(first, dtype=jnp.int32)
    right = jnp.arange(second, dtype=jnp.int32)
    product = left[:, None] * right[None, :] % length
    angle = product.astype(jnp.float32) * (2.0 * math.pi / length)
    return (jnp.cos(angle), jnp.sin(angle))


def azimuth_fft(block):
    count = block.shape[-1]
    rows = math.isqrt(count)
    while count % rows:
        rows = rows - 1
    cols = count // rows
    lead = block.shape[1:-1]
    high = lax.Precision.HIGHEST
    real_in = block[0].reshape(lead + (rows, cols))
    imag_in = block[1].reshape(lead + (rows, cols))
    cosine_first, sine_first = phases(rows, rows, rows)
    first_real = jnp.einsum("...ab,af->...bf", real_in, cosine_first, precision=high) + jnp.einsum(
        "...ab,af->...bf", imag_in, sine_first, precision=high
    )
    first_imag = jnp.einsum("...ab,af->...bf", imag_in, cosine_first, precision=high) - jnp.einsum(
        "...ab,af->...bf", real_in, sine_first, precision=high
    )
    twist_cos, twist_sin = phases(cols, rows, count)
    turned_real = first_real * twist_cos + first_imag * twist_sin
    turned_imag = first_imag * twist_cos - first_real * twist_sin
    cosine_second, sine_second = phases(cols, cols, cols)
    out_real = jnp.einsum(
        "...bf,bg->...gf", turned_real, cosine_second, precision=high
    ) + jnp.einsum("...bf,bg->...gf", turned_imag, sine_second, precision=high)
    out_imag = jnp.einsum(
        "...bf,bg->...gf", turned_imag, cosine_second, precision=high
    ) - jnp.einsum("...bf,bg->...gf", turned_real, sine_second, precision=high)
    scale = 1.0 / math.sqrt(count)
    return jnp.stack([out_real.reshape(lead + (count,)), out_imag.reshape(lead + (count,))]) * scale


def general_shards(raw, taps, recon, channel_slot):
    width = taps.shape[1]
    half = (width - 1) // 2
    strip_rows = raw.shape[2]
    padded = with_halo(raw, (("rng", 2),), half)
    real_part = jnp.zeros(raw.shape[1:], jnp.float32)
    imag_part = jnp.zeros(raw.shape[1:], jnp.float32)
    for offset in range(width):
        seg_real = padded[0, :, offset : offset + strip_rows, :]
        seg_imag = padded[1, :, offset : offset + strip_rows, :]
        tap_real = taps[0, offset][None, :, None]
        tap_imag = taps[1, offset][None, :, None]
        real_part = real_part + tap_real * seg_real - tap_imag * seg_imag
        imag_part = imag_part + tap_real * seg_imag + tap_imag * seg_real
    filtered = jnp.stack([real_part, imag_part])
    spectrum = azimuth_fft(lax.all_to_all(filtered, "az", split_axis=2, concat_axis=3, tiled=True))
    strips = lax.axis_size("rng")
    groups = lax.axis_size("chan")
    local_channels = spectrum.shape[1]
    local_range = spectrum.shape[2]
    moved = lax.all_to_all(
        spectrum[:, None], ("chan", "rng"), split_axis=4, concat_axis=1, tiled=True
    )
    bins = moved.shape[-1]
    moved = moved.reshape((2, groups, strips, local_channels, local_range, bins))
    doppler = jnp.transpose(moved, (0, 1, 3, 2, 4, 5)).reshape(
        (2, groups * local_channels, strips * local_range, bins)
    )
    channels = doppler.shape[1]
    selector = (channel_slot[:, None] == jnp.arange(channels, dtype=jnp.int32)[None, :]).astype(
        jnp.float32
    )
    piece = lax.all_gather(recon, "az", axis=1, tiled=True)
    arranged = jnp.einsum("pkjf,cj->pkcf", piece, selector, precision=lax.Precision.HIGHEST)
    shape = (piece.shape[1], doppler.shape[2], doppler.shape[3])
    out_real = jnp.zeros(shape, jnp.float32)
    out_imag = jnp.zeros(shape, jnp.float32)
    for channel in range(channels):
        mat_real = arranged[0, :, channel, None, :]
        mat_imag = arranged[1, :, channel, None, :]
        data_real = doppler[0, channel][None]
        data_imag = doppler[1, channel][None]
        out_real = out_real + mat_real * data_real - mat_imag * data_imag
        out_imag = out_imag + mat_real * data_imag + mat_imag * data_real
    result = jnp.stack([out_real, out_imag])
    total_range = result.shape[2]
    return result.reshape((2, result.shape[1], strips, total_range // strips, result.shape[3]))


def shards(raw, taps, recon, channel_slot):
    chans, azs, strips = (lax.axis_size(n) for n in ("chan", "az", "rng"))
    _, local, rows, pulses = raw.shape
    width = taps.shape[1]
    half = (width - 1) // 2
    peers = chans * strips
    fits = local > azs and rows == azs * SUB and pulses * azs == LANES * LANES and half == SUB
    if not (fits and LANES % peers == 0):
        return general_shards(raw, taps, recon, channel_slot)
    me = lax.axis_index("az").astype(jnp.int32)
    index = me[None]
    count = pulses * azs
    slow = count // LANES
    tables = [jnp.asarray(t) for t in fft_tables(slow, count, azs)]
    rest = local - azs

    def give(step, at):
        to = lax.rem(me + step, azs)
        source = raw if at == 0 and step else lax.optimization_barrier(raw)
        block = lax.dynamic_slice(source, (0, to, at, 0), (2, 1, SUB, pulses))
        return lax.ppermute(block, "az", ring(azs, step)) if step else block

    def turn(spectra):
        return lax.all_to_all(spectra, ("chan", "rng"), 0, 0, tiled=True)

    received = [[give(i, n * SUB) for i in range(azs)] for n in range(rows // SUB)]
    near = lax.axis_index("rng").astype(jnp.int32)
    parts = [taps] + [lax.ppermute(taps, "rng", ring(strips, strips - i)) for i in range(1, strips)]
    strip = jnp.arange(strips, dtype=jnp.int32)[:, None, None, None]
    all_taps = sum(
        jnp.where(strip == lax.rem(near + i, strips), part[None], 0.0) for i, part in enumerate(parts)
    )
    all_taps = jnp.transpose(all_taps, (1, 2, 0, 3)).reshape(2, width, strips * rows)
    up = ring(strips, 1)[:-1]
    down = [(b, a) for a, b in up]
    before = lax.ppermute(raw[:, azs:, rows - half :, :], "rng", up)
    after = lax.ppermute(raw[:, azs:, :half, :], "rng", down)

    early_weights = band_matrix(taps, 0, rows + 2 * half, me, azs)
    late_weights = band_matrix(all_taps, half, strips * rows, me, azs)

    spectra = None
    for n in range(rows // SUB):
        spectra = fft_call(index, received[n], tables, peers, rows // SUB, n, 32 << 20, spectra)
    late = turn(spectra)

    filtered = early_filter_call(early_weights, before, raw, after, azs, azs)
    swapped = [filtered[0]] + [lax.ppermute(filtered[i], "az", ring(azs, i)) for i in range(1, azs)]
    mats = [recon] + [lax.ppermute(recon, "az", ring(azs, i)) for i in range(1, azs)]
    swapped[0], late_weights = lax.optimization_barrier((swapped[0], late_weights))
    spectra = fft_call(index, swapped, tables, peers, rest, 0, WHOLE)
    early = turn(spectra)

    filtered = late_filter_call(late_weights, late, chans, azs)
    data = [filtered[0]] + [lax.ppermute(filtered[i], "az", ring(azs, i)) for i in range(1, azs)]

    sums, arranged = mix_late_call(index, channel_slot, data, mats, chans, local, rest)
    return mix_early_call(early, arranged, sums, chans, rest)


def solution(mesh):
    return jax.shard_map(
        shards,
        mesh=mesh,
        in_specs=(
            P(None, "chan", "rng", "az"),
            P(None, None, "rng"),
            P(None, "az", None, ("chan", "rng")),
            P(),
        ),
        out_specs=P(None, None, None, "az", ("chan", "rng")),
        check_vma=False,
    )
```

```python
import math

import jax
import jax.numpy as jnp
import ml_dtypes
import numpy as np
from jax import lax
from jax.experimental import pallas as pl
from jax.experimental.pallas import tpu as pltpu
from jax.sharding import PartitionSpec as P


LANES = 128
SUB = 8
RESIDENT = pl.BlockSpec(memory_space=pltpu.VMEM)
SCALARS = pl.BlockSpec(memory_space=pltpu.SMEM)
WHOLE = 67043328


def ring(size, step):
    return [(i, (i + step) % size) for i in range(size)]


def split_three(matrix):
    high = matrix.astype(np.float32).astype(ml_dtypes.bfloat16)
    low = (matrix - high.astype(np.float64)).astype(ml_dtypes.bfloat16)
    return np.concatenate([high, high, low], axis=1)


def two_parts(value):
    high = value.astype(jnp.bfloat16)
    return high, (value - high.astype(jnp.float32)).astype(jnp.bfloat16)


def fft_tables(slow, count, azs):
    own = slow // azs
    h = np.arange(slow)
    place = np.concatenate([(-i * own + np.arange(own)) % slow for i in range(azs)])
    angle = 2 * np.pi * ((h[:, None] * place[None, :]) % slow) / slow
    first = np.block([[np.cos(angle), np.sin(angle)], [-np.sin(angle), np.cos(angle)]])
    b = np.arange(LANES)
    tables = []
    for me in range(azs):
        turn = 2 * np.pi * ((h[:, None] * (b[None, :] + me * own * LANES)) % count) / count
        tables.append(np.stack([np.cos(turn), -np.sin(turn)]))
    m = np.arange(count // slow)
    angle = 2 * np.pi * ((m[:, None] * b[None, :]) % LANES) / LANES
    second = np.block([[np.cos(angle), np.sin(angle)], [-np.sin(angle), np.cos(angle)]])
    second = second / math.sqrt(count)
    return split_three(first), np.stack(tables).astype(np.float32), split_three(second)


def fft_kernel(azs, own, peers, index_ref, *refs):
    inputs = refs[:azs]
    first_ref, turn_ref, second_ref = refs[azs : 3 + azs]
    out_ref, scratch = refs[-2:]
    slow = own * azs
    subs = LANES // peers
    me = index_ref[0]
    for part in range(2):
        for i in range(azs):
            for a in range(own):
                at = (part * slow + i * own + a) * SUB
                scratch[at : at + SUB, :] = inputs[i][
                    part, 0, :, a * LANES : (a + 1) * LANES
                ]
    for row in range(0, SUB, 2):
        x = jnp.concatenate(
            [scratch[pl.ds(row + e, 2 * slow, stride=SUB), :] for e in range(2)], axis=1
        )
        high, low = two_parts(x)
        y = jnp.dot(
            first_ref[...],
            jnp.concatenate([high, low, high], axis=0),
            preferred_element_type=jnp.float32,
        )
        turned = []
        for e in range(2):
            real = y[:slow, e * LANES : (e + 1) * LANES]
            imag = y[slow:, e * LANES : (e + 1) * LANES]
            turned.append(
                jnp.concatenate(
                    [
                        real * turn_ref[me, 0] - imag * turn_ref[me, 1],
                        real * turn_ref[me, 1] + imag * turn_ref[me, 0],
                    ],
                    axis=1,
                )
            )
        high, low = two_parts(jnp.concatenate(turned, axis=0))
        z = lax.dot_general(
            second_ref[...],
            jnp.concatenate([high, low, high], axis=1),
            (((1,), (1,)), ((), ())),
            preferred_element_type=jnp.float32,
        )
        for part in range(2):
            for peer in range(peers):
                for e in range(2):
                    at = part * LANES + peer * subs
                    out_ref[peer, part, 0, pl.ds(row + e, subs, stride=SUB), :] = z[
                        at : at + subs, e * slow : (e + 1) * slow
                    ]


def fft_tile_kernel(azs, own, peers, tile, index_ref, *refs):
    out_ref, scratch, block, done = refs[-4:]
    fft_kernel(azs, own, peers, index_ref, *refs[: azs + 3], block, scratch)
    copy = pltpu.make_async_copy(block, out_ref.at[:, :, pl.ds(tile, 1)], done)
    copy.start()
    copy.wait()


def fft_call(index, inputs, tables, peers, tiles, first, limit, prior=None):
    azs = len(inputs)
    steps = inputs[0].shape[1]
    own = inputs[0].shape[3] // LANES
    slow = own * azs
    subs = LANES // peers
    kept = prior is not None
    work = steps * SUB * slow * LANES
    tile = (peers, 2, 1, SUB * subs, LANES)
    scratch = [pltpu.VMEM((SUB * 2 * slow, LANES), jnp.float32)]
    if steps == 1:
        how = dict(
            in_specs=[SCALARS] + [RESIDENT] * (azs + 3) + [pl.BlockSpec(memory_space=pl.ANY)] * kept,
            out_specs=pl.BlockSpec(memory_space=pl.ANY),
            scratch_shapes=scratch + [pltpu.VMEM(tile, jnp.float32), pltpu.SemaphoreType.DMA],
            input_output_aliases={azs + 4: 0} if kept else {},
        )
        kernel = lambda *refs: fft_tile_kernel(azs, own, peers, first, *refs)
    else:
        how = dict(
            grid=(steps,),
            in_specs=[SCALARS]
            + [pl.BlockSpec((2, 1, SUB, own * LANES), lambda g: (0, g, 0, 0))] * azs
            + [pl.BlockSpec(t.shape, lambda g, n=t.ndim: (0,) * n) for t in tables],
            out_specs=pl.BlockSpec(tile, lambda g: (0, 0, g + first, 0, 0)),
            scratch_shapes=scratch,
        )
        kernel = lambda *refs: fft_kernel(azs, own, peers, *refs)
    return pl.pallas_call(
        kernel,
        out_shape=jax.ShapeDtypeStruct((peers, 2, tiles, SUB * subs, LANES), jnp.float32),
        compiler_params=pltpu.CompilerParams(vmem_limit_bytes=limit),
        name="azimuth",
        cost_estimate=pl.CostEstimate(
            flops=work * 2 * 8 * LANES * 3, bytes_accessed=work * 16, transcendentals=0
        ),
        **how,
    )(index, *inputs, *tables, *([prior] if kept else []))


def band_matrix(taps, lead, total_in, me, azs):
    width, total = taps.shape[1:]
    tap = jnp.arange(total_in, dtype=jnp.int32)[None, :] - jnp.arange(total, dtype=jnp.int32)[:, None] + lead
    hit = tap[:, :, None] == jnp.arange(width, dtype=jnp.int32)
    table = jnp.transpose(taps, (0, 2, 1))
    band = jnp.sum(jnp.where(hit[None], table[:, :, None, :], 0.0), axis=3)
    real = jnp.concatenate([band[0], -band[1]], axis=1)
    imag = jnp.concatenate([band[1], band[0]], axis=1)
    both = jnp.stack([real, imag]).reshape(2, total // (azs * SUB), azs, SUB, 2 * total_in)
    both = jnp.transpose(both, (2, 0, 1, 3, 4)).reshape(azs, -1, 2 * total_in)
    both = lax.dynamic_slice_in_dim(jnp.concatenate([both, both]), me, azs, 0)
    return jnp.tile(both.reshape(-1, 2 * total_in), (1, 3))


def rounded_weights(w):
    columns = w.shape[1] // 3
    rounded = w.astype(jnp.bfloat16).astype(jnp.float32)
    low_part = lax.broadcasted_iota(jnp.int32, w.shape, 1) >= 2 * columns
    return jnp.where(low_part, w - rounded, rounded).astype(jnp.bfloat16)


def weighted(weights, blocks):
    high, low = two_parts(jnp.concatenate(blocks, axis=0))
    return jnp.dot(
        weights, jnp.concatenate([high, low, high], axis=0), preferred_element_type=jnp.float32
    )


def early_filter_kernel(azs, width, w_ref, before, own, after, *outs):
    weights = rounded_weights(w_ref[...])

    def body(step, _):
        at = pl.ds(pl.multiple_of(step * width, width), width)
        y = weighted(
            weights,
            [
                block
                for part in range(2)
                for block in (before[part, 0, :, at], own[part, 0, :, at], after[part, 0, :, at])
            ],
        )
        for i in range(azs):
            for part in range(2):
                row = (i * 2 + part) * SUB
                outs[i][part, 0, :, at] = y[row : row + SUB]
        return 0

    lax.fori_loop(0, own.shape[3] // width, body, 0, unroll=2)


def early_filter_call(weights, before, raw, after, at, azs):
    _, count, _, pulses = before.shape
    rows = raw.shape[2]
    out = jax.ShapeDtypeStruct((2, count, SUB, pulses), jnp.float32)
    edge = pl.BlockSpec((2, 1, SUB, pulses), lambda g: (0, g, 0, 0))
    return pl.pallas_call(
        lambda *refs: early_filter_kernel(azs, 4 * LANES, *refs),
        grid=(count,),
        in_specs=[
            pl.BlockSpec(weights.shape, lambda g: (0, 0)),
            edge,
            pl.BlockSpec((2, 1, rows, pulses), lambda g: (0, g + at, 0, 0)),
            edge,
        ],
        out_specs=[edge] * azs,
        out_shape=[out] * azs,
        compiler_params=pltpu.CompilerParams(vmem_limit_bytes=WHOLE),
        name="strip_filter",
        cost_estimate=pl.CostEstimate(
            flops=2 * weights.shape[0] * weights.shape[1] * count * pulses,
            bytes_accessed=24 * count * rows * pulses,
            transcendentals=0,
        ),
    )(weights, before, raw, after)


def late_filter_kernel(azs, w_ref, in_ref, *outs):
    weights = rounded_weights(w_ref[...])
    strips, _, tiles, depth, _ = in_ref.shape
    subs = depth // SUB
    chan = pl.program_id(0)
    step = 2 if subs % 2 == 0 else 1

    for sub in range(0, subs, step):
        y = weighted(
            weights,
            [
                jnp.concatenate(
                    [
                        in_ref[strip, part, tile, (sub + s) * SUB : (sub + s + 1) * SUB, :]
                        for s in range(step)
                    ],
                    axis=1,
                )
                for part in range(2)
                for strip in range(strips)
                for tile in range(tiles)
            ],
        )
        at = 0
        for i in range(azs):
            for part in range(2):
                for strip in range(strips):
                    for s in range(step):
                        outs[i][part, chan, strip, sub + s, :, :] = y[
                            at : at + SUB, s * LANES : (s + 1) * LANES
                        ]
                    at += SUB


def late_filter_call(weights, moved, chans, azs):
    peers, _, _, depth, _ = moved.shape
    strips, subs = peers // chans, depth // SUB
    out = jax.ShapeDtypeStruct((2, chans, strips, subs, SUB, LANES), jnp.float32)
    return pl.pallas_call(
        lambda *refs: late_filter_kernel(azs, *refs),
        grid=(chans,),
        in_specs=[
            pl.BlockSpec(weights.shape, lambda g: (0, 0)),
            pl.BlockSpec((strips,) + moved.shape[1:], lambda g: (g, 0, 0, 0, 0)),
        ],
        out_specs=[RESIDENT] * azs,
        out_shape=[out] * azs,
        compiler_params=pltpu.CompilerParams(vmem_limit_bytes=32 << 20),
        name="range_filter",
        cost_estimate=pl.CostEstimate(
            flops=2 * weights.shape[0] * weights.shape[1] * chans * subs * LANES,
            bytes_accessed=8 * math.prod(moved.shape),
            transcendentals=0,
        ),
    )(weights, moved)


def mix_kernel(sources, matrix, total, strips, kept, out_ref, prior, scratch):
    for n, value in enumerate(sources):
        for s in range(strips):
            dr, di = value(s)
            scratch[n, s] = dr + di

    def body(row, _):
        totals = None
        for n, value in enumerate(sources):
            ar = jnp.broadcast_to(matrix(0, row, n), (SUB, LANES))
            ai = jnp.broadcast_to(matrix(1, row, n), (SUB, LANES))
            both = ar + ai
            terms = []
            for s in range(strips):
                dr, di = value(s)
                terms += [ar * dr, ai * di, both * scratch[n, s]]
            totals = terms if totals is None else [t + u for t, u in zip(totals, terms)]
        for s in range(strips):
            first, second, third = totals[3 * s : 3 * s + 3]
            real, imag = first - second, third - first - second
            if kept:
                out_ref[0, row, s] = real + prior[0, 0, row, s]
                out_ref[1, row, s] = imag + prior[0, 1, row, s]
            else:
                out_ref[0, 0, row, s] = real
                out_ref[0, 1, row, s] = imag
        return 0

    lax.fori_loop(0, total, body, 0, unroll=math.gcd(total, 16 if kept else 8))


def mix_late_kernel(azs, chans, local, rest, index_ref, slot_ref, *refs):
    data, mats = refs[:azs], refs[azs : 2 * azs]
    out_ref, next_ref, own, scratch = refs[2 * azs :]
    me = index_ref[0]
    strips = data[0].shape[2]
    here = mats[0].shape[1]
    late = [(i, chan) for i in range(azs) for chan in range(chans)]
    late_slots = [slot_ref[chan * local + lax.rem(me - i + azs, azs)] for i, chan in late]
    next_slots = [slot_ref[chan * local + azs + c] for chan in range(chans) for c in range(rest)]
    for j in range(azs):
        base = lax.rem(me - j + azs, azs) * here

        def arrange(row, _, j=j, base=base):
            for part in range(2):
                for n, slot in enumerate(late_slots):
                    own[part, base + row, n : n + 1, :] = mats[j][part, row, pl.ds(slot, 1), :]
                for n, slot in enumerate(next_slots):
                    next_ref[0, part, base + row, n : n + 1, :] = mats[j][part, row, pl.ds(slot, 1), :]
            return 0

        lax.fori_loop(0, here, arrange, 0, unroll=2)
    sources = [
        lambda s, i=i, chan=chan: (data[i][0, chan, s, 0], data[i][1, chan, s, 0]) for i, chan in late
    ]
    mix_kernel(
        sources,
        lambda part, row, n: own[part, row, n : n + 1, :],
        here * azs,
        strips,
        False,
        out_ref,
        None,
        scratch,
    )


def mix_late_call(index, slots, data, mats, chans, local, rest):
    azs = len(mats)
    _, _, strips, subs, _, _ = data[0].shape
    here = mats[0].shape[1]
    total = here * azs
    sums = jax.ShapeDtypeStruct((subs, 2, total, strips, SUB, LANES), jnp.float32)
    arranged = jax.ShapeDtypeStruct((subs, 2, total, chans * rest, LANES), jnp.float32)
    return pl.pallas_call(
        lambda *refs: mix_late_kernel(azs, chans, local, rest, *refs),
        grid=(subs,),
        in_specs=[SCALARS] * 2
        + [pl.BlockSpec((2, chans, strips, 1, SUB, LANES), lambda g: (0, 0, 0, g, 0, 0))] * azs
        + [pl.BlockSpec(mats[0].shape[:3] + (LANES,), lambda g: (0, 0, 0, g))] * azs,
        out_specs=[
            pl.BlockSpec((1,) + sums.shape[1:], lambda g: (g, 0, 0, 0, 0, 0)),
            pl.BlockSpec((1,) + arranged.shape[1:], lambda g: (g, 0, 0, 0, 0)),
        ],
        out_shape=[sums, arranged],
        scratch_shapes=[
            pltpu.VMEM((2, total, chans * azs, LANES), jnp.float32),
            pltpu.VMEM((chans * azs, strips, SUB, LANES), jnp.float32),
        ],
        compiler_params=pltpu.CompilerParams(vmem_limit_bytes=50 << 20),
        name="reconstruct_late",
        cost_estimate=pl.CostEstimate(
            flops=8 * total * strips * SUB * subs * LANES * chans * azs,
            bytes_accessed=4 * math.prod(sums.shape),
            transcendentals=0,
        ),
    )(index, slots, *data, *mats)


def mix_early_kernel(chans, rest, data, mats, prior, out_ref, scratch):
    strips = data.shape[0] // chans
    sources = [
        lambda s, c=c, chan=chan: tuple(data[chan * strips + s, p, c] for p in range(2))
        for chan in range(chans)
        for c in range(rest)
    ]
    mix_kernel(
        sources,
        lambda part, row, n: mats[0, part, row, n : n + 1, :],
        prior.shape[2],
        strips,
        True,
        out_ref,
        prior,
        scratch,
    )


def mix_early_call(early, mats, prior, chans, rest):
    subs, _, total, strips, _, _ = prior.shape
    out = jax.ShapeDtypeStruct((2, total, strips, SUB, subs * LANES), jnp.float32)
    return pl.pallas_call(
        lambda *refs: mix_early_kernel(chans, rest, *refs),
        grid=(subs,),
        in_specs=[
            pl.BlockSpec(early.shape[:3] + (SUB, LANES), lambda g: (0, 0, 0, g, 0)),
            pl.BlockSpec((1,) + mats.shape[1:], lambda g: (g, 0, 0, 0, 0)),
            pl.BlockSpec((1,) + prior.shape[1:], lambda g: (g, 0, 0, 0, 0, 0)),
        ],
        out_specs=pl.BlockSpec((2, total, strips, SUB, LANES), lambda g: (0, 0, 0, 0, g)),
        out_shape=out,
        scratch_shapes=[pltpu.VMEM((chans * rest, strips, SUB, LANES), jnp.float32)],
        compiler_params=pltpu.CompilerParams(vmem_limit_bytes=50 << 20),
        name="reconstruct",
        cost_estimate=pl.CostEstimate(
            flops=8 * math.prod(out.shape) * chans * rest,
            bytes_accessed=8 * math.prod(out.shape),
            transcendentals=0,
        ),
    )(early, mats, prior)


def with_halo(shard, sides, width):
    for axis, dim in sides:
        size, length = (lax.axis_size(axis), shard.shape[dim])
        up = [(i, (i + 1) % size) for i in range(size - 1)]
        down = [(j, i) for i, j in up]
        last = lax.slice_in_dim(shard, length - width, length, axis=dim)
        leading = lax.slice_in_dim(shard, 0, width, axis=dim)
        before = lax.ppermute(last, axis, up)
        after = lax.ppermute(leading, axis, down)
        shard = jnp.concatenate([before, shard, after], axis=dim)
    return shard


def phases(first, second, length):
    left = jnp.arange(first, dtype=jnp.int32)
    right = jnp.arange(second, dtype=jnp.int32)
    product = left[:, None] * right[None, :] % length
    angle = product.astype(jnp.float32) * (2.0 * math.pi / length)
    return (jnp.cos(angle), jnp.sin(angle))


def azimuth_fft(block):
    count = block.shape[-1]
    rows = math.isqrt(count)
    while count % rows:
        rows = rows - 1
    cols = count // rows
    lead = block.shape[1:-1]
    high = lax.Precision.HIGHEST
    real_in = block[0].reshape(lead + (rows, cols))
    imag_in = block[1].reshape(lead + (rows, cols))
    cosine_first, sine_first = phases(rows, rows, rows)
    first_real = jnp.einsum("...ab,af->...bf", real_in, cosine_first, precision=high) + jnp.einsum(
        "...ab,af->...bf", imag_in, sine_first, precision=high
    )
    first_imag = jnp.einsum("...ab,af->...bf", imag_in, cosine_first, precision=high) - jnp.einsum(
        "...ab,af->...bf", real_in, sine_first, precision=high
    )
    twist_cos, twist_sin = phases(cols, rows, count)
    turned_real = first_real * twist_cos + first_imag * twist_sin
    turned_imag = first_imag * twist_cos - first_real * twist_sin
    cosine_second, sine_second = phases(cols, cols, cols)
    out_real = jnp.einsum(
        "...bf,bg->...gf", turned_real, cosine_second, precision=high
    ) + jnp.einsum("...bf,bg->...gf", turned_imag, sine_second, precision=high)
    out_imag = jnp.einsum(
        "...bf,bg->...gf", turned_imag, cosine_second, precision=high
    ) - jnp.einsum("...bf,bg->...gf", turned_real, sine_second, precision=high)
    scale = 1.0 / math.sqrt(count)
    return jnp.stack([out_real.reshape(lead + (count,)), out_imag.reshape(lead + (count,))]) * scale


def general_shards(raw, taps, recon, channel_slot):
    width = taps.shape[1]
    half = (width - 1) // 2
    strip_rows = raw.shape[2]
    padded = with_halo(raw, (("rng", 2),), half)
    real_part = jnp.zeros(raw.shape[1:], jnp.float32)
    imag_part = jnp.zeros(raw.shape[1:], jnp.float32)
    for offset in range(width):
        seg_real = padded[0, :, offset : offset + strip_rows, :]
        seg_imag = padded[1, :, offset : offset + strip_rows, :]
        tap_real = taps[0, offset][None, :, None]
        tap_imag = taps[1, offset][None, :, None]
        real_part = real_part + tap_real * seg_real - tap_imag * seg_imag
        imag_part = imag_part + tap_real * seg_imag + tap_imag * seg_real
    filtered = jnp.stack([real_part, imag_part])
    spectrum = azimuth_fft(lax.all_to_all(filtered, "az", split_axis=2, concat_axis=3, tiled=True))
    strips = lax.axis_size("rng")
    groups = lax.axis_size("chan")
    local_channels = spectrum.shape[1]
    local_range = spectrum.shape[2]
    moved = lax.all_to_all(
        spectrum[:, None], ("chan", "rng"), split_axis=4, concat_axis=1, tiled=True
    )
    bins = moved.shape[-1]
    moved = moved.reshape((2, groups, strips, local_channels, local_range, bins))
    doppler = jnp.transpose(moved, (0, 1, 3, 2, 4, 5)).reshape(
        (2, groups * local_channels, strips * local_range, bins)
    )
    channels = doppler.shape[1]
    selector = (channel_slot[:, None] == jnp.arange(channels, dtype=jnp.int32)[None, :]).astype(
        jnp.float32
    )
    piece = lax.all_gather(recon, "az", axis=1, tiled=True)
    arranged = jnp.einsum("pkjf,cj->pkcf", piece, selector, precision=lax.Precision.HIGHEST)
    shape = (piece.shape[1], doppler.shape[2], doppler.shape[3])
    out_real = jnp.zeros(shape, jnp.float32)
    out_imag = jnp.zeros(shape, jnp.float32)
    for channel in range(channels):
        mat_real = arranged[0, :, channel, None, :]
        mat_imag = arranged[1, :, channel, None, :]
        data_real = doppler[0, channel][None]
        data_imag = doppler[1, channel][None]
        out_real = out_real + mat_real * data_real - mat_imag * data_imag
        out_imag = out_imag + mat_real * data_imag + mat_imag * data_real
    result = jnp.stack([out_real, out_imag])
    total_range = result.shape[2]
    return result.reshape((2, result.shape[1], strips, total_range // strips, result.shape[3]))


def shards(raw, taps, recon, channel_slot):
    chans, azs, strips = (lax.axis_size(n) for n in ("chan", "az", "rng"))
    _, local, rows, pulses = raw.shape
    width = taps.shape[1]
    half = (width - 1) // 2
    peers = chans * strips
    fits = local > azs and rows == azs * SUB and pulses * azs == LANES * LANES and half == SUB
    if not (fits and LANES % peers == 0):
        return general_shards(raw, taps, recon, channel_slot)
    me = lax.axis_index("az").astype(jnp.int32)
    index = me[None]
    count = pulses * azs
    slow = count // LANES
    tables = [jnp.asarray(t) for t in fft_tables(slow, count, azs)]
    rest = local - azs

    def give(step, at):
        to = lax.rem(me + step, azs)
        source = raw if at == 0 and step else lax.optimization_barrier(raw)
        block = lax.dynamic_slice(source, (0, to, at, 0), (2, 1, SUB, pulses))
        return lax.ppermute(block, "az", ring(azs, step)) if step else block

    def turn(spectra):
        return lax.all_to_all(spectra, ("chan", "rng"), 0, 0, tiled=True)

    received = [[give(i, n * SUB) for i in range(azs)] for n in range(rows // SUB)]
    near = lax.axis_index("rng").astype(jnp.int32)
    parts = [taps] + [lax.ppermute(taps, "rng", ring(strips, strips - i)) for i in range(1, strips)]
    strip = jnp.arange(strips, dtype=jnp.int32)[:, None, None, None]
    all_taps = sum(
        jnp.where(strip == lax.rem(near + i, strips), part[None], 0.0) for i, part in enumerate(parts)
    )
    all_taps = jnp.transpose(all_taps, (1, 2, 0, 3)).reshape(2, width, strips * rows)
    up = ring(strips, 1)[:-1]
    down = [(b, a) for a, b in up]
    before = lax.ppermute(raw[:, azs:, rows - half :, :], "rng", up)
    after = lax.ppermute(raw[:, azs:, :half, :], "rng", down)

    early_weights = band_matrix(taps, 0, rows + 2 * half, me, azs)
    late_weights = band_matrix(all_taps, half, strips * rows, me, azs)

    spectra = None
    for n in range(rows // SUB):
        spectra = fft_call(index, received[n], tables, peers, rows // SUB, n, 32 << 20, spectra)
    late = turn(spectra)

    filtered = early_filter_call(early_weights, before, raw, after, azs, azs)
    swapped = [filtered[0]] + [lax.ppermute(filtered[i], "az", ring(azs, i)) for i in range(1, azs)]
    mats = [recon] + [lax.ppermute(recon, "az", ring(azs, i)) for i in range(1, azs)]
    swapped[0], late_weights = lax.optimization_barrier((swapped[0], late_weights))
    spectra = fft_call(index, swapped, tables, peers, rest, 0, WHOLE)
    early = turn(spectra)

    filtered = late_filter_call(late_weights, late, chans, azs)
    data = [filtered[0]] + [lax.ppermute(filtered[i], "az", ring(azs, i)) for i in range(1, azs)]

    sums, arranged = mix_late_call(index, channel_slot, data, mats, chans, local, rest)
    return mix_early_call(early, arranged, sums, chans, rest)


def solution(mesh):
    return jax.shard_map(
        shards,
        mesh=mesh,
        in_specs=(
            P(None, "chan", "rng", "az"),
            P(None, None, "rng"),
            P(None, "az", None, ("chan", "rng")),
            P(),
        ),
        out_specs=P(None, None, None, "az", ("chan", "rng")),
        check_vma=False,
    )
```

```python
import math

import jax
import jax.numpy as jnp
import ml_dtypes
import numpy as np
from jax import lax
from jax.experimental import pallas as pl
from jax.experimental.pallas import tpu as pltpu
from jax.sharding import PartitionSpec as P


LANES = 128
SUB = 8
RESIDENT = pl.BlockSpec(memory_space=pltpu.VMEM)
SCALARS = pl.BlockSpec(memory_space=pltpu.SMEM)
WHOLE = 67043328


def ring(size, step):
    return [(i, (i + step) % size) for i in range(size)]


def split_three(matrix):
    high = matrix.astype(np.float32).astype(ml_dtypes.bfloat16)
    low = (matrix - high.astype(np.float64)).astype(ml_dtypes.bfloat16)
    return np.concatenate([high, high, low], axis=1)


def two_parts(value):
    high = value.astype(jnp.bfloat16)
    return high, (value - high.astype(jnp.float32)).astype(jnp.bfloat16)


def fft_tables(slow, count, azs):
    own = slow // azs
    h = np.arange(slow)
    place = np.concatenate([(-i * own + np.arange(own)) % slow for i in range(azs)])
    angle = 2 * np.pi * ((h[:, None] * place[None, :]) % slow) / slow
    first = np.block([[np.cos(angle), np.sin(angle)], [-np.sin(angle), np.cos(angle)]])
    b = np.arange(LANES)
    tables = []
    for me in range(azs):
        turn = 2 * np.pi * ((h[:, None] * (b[None, :] + me * own * LANES)) % count) / count
        tables.append(np.stack([np.cos(turn), -np.sin(turn)]))
    m = np.arange(count // slow)
    angle = 2 * np.pi * ((m[:, None] * b[None, :]) % LANES) / LANES
    second = np.block([[np.cos(angle), np.sin(angle)], [-np.sin(angle), np.cos(angle)]])
    second = second / math.sqrt(count)
    return split_three(first), np.stack(tables).astype(np.float32), split_three(second)


def fft_kernel(azs, own, peers, index_ref, *refs):
    inputs = refs[:azs]
    first_ref, turn_ref, second_ref = refs[azs : 3 + azs]
    out_ref, scratch = refs[-2:]
    slow = own * azs
    subs = LANES // peers
    me = index_ref[0]
    for part in range(2):
        for i in range(azs):
            for a in range(own):
                at = (part * slow + i * own + a) * SUB
                scratch[at : at + SUB, :] = inputs[i][
                    part, 0, :, a * LANES : (a + 1) * LANES
                ]
    for row in range(0, SUB, 2):
        x = jnp.concatenate(
            [scratch[pl.ds(row + e, 2 * slow, stride=SUB), :] for e in range(2)], axis=1
        )
        high, low = two_parts(x)
        y = jnp.dot(
            first_ref[...],
            jnp.concatenate([high, low, high], axis=0),
            preferred_element_type=jnp.float32,
        )
        turned = []
        for e in range(2):
            real = y[:slow, e * LANES : (e + 1) * LANES]
            imag = y[slow:, e * LANES : (e + 1) * LANES]
            turned.append(
                jnp.concatenate(
                    [
                        real * turn_ref[me, 0] - imag * turn_ref[me, 1],
                        real * turn_ref[me, 1] + imag * turn_ref[me, 0],
                    ],
                    axis=1,
                )
            )
        high, low = two_parts(jnp.concatenate(turned, axis=0))
        z = lax.dot_general(
            second_ref[...],
            jnp.concatenate([high, low, high], axis=1),
            (((1,), (1,)), ((), ())),
            preferred_element_type=jnp.float32,
        )
        for part in range(2):
            for peer in range(peers):
                for e in range(2):
                    at = part * LANES + peer * subs
                    out_ref[peer, part, 0, pl.ds(row + e, subs, stride=SUB), :] = z[
                        at : at + subs, e * slow : (e + 1) * slow
                    ]


def fft_tile_kernel(azs, own, peers, tile, index_ref, *refs):
    out_ref, scratch, block, done = refs[-4:]
    fft_kernel(azs, own, peers, index_ref, *refs[: azs + 3], block, scratch)
    copy = pltpu.make_async_copy(block, out_ref.at[:, :, pl.ds(tile, 1)], done)
    copy.start()
    copy.wait()


def fft_call(index, inputs, tables, peers, tiles, first, limit, prior=None):
    azs = len(inputs)
    steps = inputs[0].shape[1]
    own = inputs[0].shape[3] // LANES
    slow = own * azs
    subs = LANES // peers
    kept = prior is not None
    work = steps * SUB * slow * LANES
    tile = (peers, 2, 1, SUB * subs, LANES)
    scratch = [pltpu.VMEM((SUB * 2 * slow, LANES), jnp.float32)]
    if limit < WHOLE:
        how = dict(
            in_specs=[SCALARS] + [RESIDENT] * (azs + 3) + [pl.BlockSpec(memory_space=pl.ANY)] * kept,
            out_specs=pl.BlockSpec(memory_space=pl.ANY),
            scratch_shapes=scratch + [pltpu.VMEM(tile, jnp.float32), pltpu.SemaphoreType.DMA],
            input_output_aliases={azs + 4: 0} if kept else {},
        )
        kernel = lambda *refs: fft_tile_kernel(azs, own, peers, first, *refs)
    else:
        how = dict(
            grid=(steps,),
            in_specs=[SCALARS]
            + [pl.BlockSpec((2, 1, SUB, own * LANES), lambda g: (0, g, 0, 0))] * azs
            + [pl.BlockSpec(t.shape, lambda g, n=t.ndim: (0,) * n) for t in tables]
            + [pl.BlockSpec(memory_space=pl.ANY)] * kept,
            out_specs=pl.BlockSpec(tile, lambda g: (0, 0, g + first, 0, 0)),
            scratch_shapes=scratch,
            input_output_aliases={azs + 4: 0} if kept else {},
        )
        kernel = lambda *refs: fft_kernel(azs, own, peers, *refs)
    return pl.pallas_call(
        kernel,
        out_shape=jax.ShapeDtypeStruct((peers, 2, tiles, SUB * subs, LANES), jnp.float32),
        compiler_params=pltpu.CompilerParams(vmem_limit_bytes=limit),
        name="azimuth",
        cost_estimate=pl.CostEstimate(
            flops=work * 2 * 8 * LANES * 3, bytes_accessed=work * 16, transcendentals=0
        ),
        **how,
    )(index, *inputs, *tables, *([prior] if kept else []))


def band_matrix(taps, lead, total_in, me, azs):
    width, total = taps.shape[1:]
    tap = jnp.arange(total_in, dtype=jnp.int32)[None, :] - jnp.arange(total, dtype=jnp.int32)[:, None] + lead
    hit = tap[:, :, None] == jnp.arange(width, dtype=jnp.int32)
    table = jnp.transpose(taps, (0, 2, 1))
    band = jnp.sum(jnp.where(hit[None], table[:, :, None, :], 0.0), axis=3)
    real = jnp.concatenate([band[0], -band[1]], axis=1)
    imag = jnp.concatenate([band[1], band[0]], axis=1)
    both = jnp.stack([real, imag]).reshape(2, total // (azs * SUB), azs, SUB, 2 * total_in)
    both = jnp.transpose(both, (2, 0, 1, 3, 4)).reshape(azs, -1, 2 * total_in)
    both = lax.dynamic_slice_in_dim(jnp.concatenate([both, both]), me, azs, 0)
    return jnp.tile(both.reshape(-1, 2 * total_in), (1, 3))


def rounded_weights(w):
    columns = w.shape[1] // 3
    rounded = w.astype(jnp.bfloat16).astype(jnp.float32)
    low_part = lax.broadcasted_iota(jnp.int32, w.shape, 1) >= 2 * columns
    return jnp.where(low_part, w - rounded, rounded).astype(jnp.bfloat16)


def weighted(weights, blocks):
    high, low = two_parts(jnp.concatenate(blocks, axis=0))
    return jnp.dot(
        weights, jnp.concatenate([high, low, high], axis=0), preferred_element_type=jnp.float32
    )


def early_filter_kernel(azs, width, w_ref, before, own, after, *outs):
    weights = rounded_weights(w_ref[...])

    def body(step, _):
        at = pl.ds(pl.multiple_of(step * width, width), width)
        y = weighted(
            weights,
            [
                block
                for part in range(2)
                for block in (before[part, 0, :, at], own[part, 0, :, at], after[part, 0, :, at])
            ],
        )
        for i in range(azs):
            for part in range(2):
                row = (i * 2 + part) * SUB
                outs[i][part, 0, :, at] = y[row : row + SUB]
        return 0

    lax.fori_loop(0, own.shape[3] // width, body, 0, unroll=2)


def early_filter_call(weights, before, raw, after, at, azs):
    _, count, _, pulses = before.shape
    rows = raw.shape[2]
    out = jax.ShapeDtypeStruct((2, count, SUB, pulses), jnp.float32)
    edge = pl.BlockSpec((2, 1, SUB, pulses), lambda g: (0, g, 0, 0))
    return pl.pallas_call(
        lambda *refs: early_filter_kernel(azs, 4 * LANES, *refs),
        grid=(count,),
        in_specs=[
            pl.BlockSpec(weights.shape, lambda g: (0, 0)),
            edge,
            pl.BlockSpec((2, 1, rows, pulses), lambda g: (0, g + at, 0, 0)),
            edge,
        ],
        out_specs=[edge] * azs,
        out_shape=[out] * azs,
        compiler_params=pltpu.CompilerParams(vmem_limit_bytes=WHOLE),
        name="strip_filter",
        cost_estimate=pl.CostEstimate(
            flops=2 * weights.shape[0] * weights.shape[1] * count * pulses,
            bytes_accessed=24 * count * rows * pulses,
            transcendentals=0,
        ),
    )(weights, before, raw, after)


def late_filter_kernel(azs, w_ref, in_ref, *outs):
    weights = rounded_weights(w_ref[...])
    strips, _, tiles, depth, _ = in_ref.shape
    subs = depth // SUB
    chan = pl.program_id(0)
    step = 2 if subs % 2 == 0 else 1

    for sub in range(0, subs, step):
        y = weighted(
            weights,
            [
                jnp.concatenate(
                    [
                        in_ref[strip, part, tile, (sub + s) * SUB : (sub + s + 1) * SUB, :]
                        for s in range(step)
                    ],
                    axis=1,
                )
                for part in range(2)
                for strip in range(strips)
                for tile in range(tiles)
            ],
        )
        at = 0
        for i in range(azs):
            for part in range(2):
                for strip in range(strips):
                    for s in range(step):
                        outs[i][part, chan, strip, sub + s, :, :] = y[
                            at : at + SUB, s * LANES : (s + 1) * LANES
                        ]
                    at += SUB


def late_filter_call(weights, moved, chans, azs):
    peers, _, _, depth, _ = moved.shape
    strips, subs = peers // chans, depth // SUB
    out = jax.ShapeDtypeStruct((2, chans, strips, subs, SUB, LANES), jnp.float32)
    return pl.pallas_call(
        lambda *refs: late_filter_kernel(azs, *refs),
        grid=(chans,),
        in_specs=[
            pl.BlockSpec(weights.shape, lambda g: (0, 0)),
            pl.BlockSpec((strips,) + moved.shape[1:], lambda g: (g, 0, 0, 0, 0)),
        ],
        out_specs=[RESIDENT] * azs,
        out_shape=[out] * azs,
        compiler_params=pltpu.CompilerParams(vmem_limit_bytes=32 << 20),
        name="range_filter",
        cost_estimate=pl.CostEstimate(
            flops=2 * weights.shape[0] * weights.shape[1] * chans * subs * LANES,
            bytes_accessed=8 * math.prod(moved.shape),
            transcendentals=0,
        ),
    )(weights, moved)


def mix_kernel(sources, matrix, total, strips, kept, out_ref, prior, scratch):
    for n, value in enumerate(sources):
        for s in range(strips):
            dr, di = value(s)
            scratch[n, s] = dr + di

    def body(row, _):
        totals = None
        for n, value in enumerate(sources):
            ar = jnp.broadcast_to(matrix(0, row, n), (SUB, LANES))
            ai = jnp.broadcast_to(matrix(1, row, n), (SUB, LANES))
            both = ar + ai
            terms = []
            for s in range(strips):
                dr, di = value(s)
                terms += [ar * dr, ai * di, both * scratch[n, s]]
            totals = terms if totals is None else [t + u for t, u in zip(totals, terms)]
        for s in range(strips):
            first, second, third = totals[3 * s : 3 * s + 3]
            real, imag = first - second, third - first - second
            if kept:
                out_ref[0, row, s] = real + prior[0, 0, row, s]
                out_ref[1, row, s] = imag + prior[0, 1, row, s]
            else:
                out_ref[0, 0, row, s] = real
                out_ref[0, 1, row, s] = imag
        return 0

    lax.fori_loop(0, total, body, 0, unroll=math.gcd(total, 16 if kept else 8))


def mix_late_kernel(azs, chans, local, rest, index_ref, slot_ref, *refs):
    data, mats = refs[:azs], refs[azs : 2 * azs]
    out_ref, next_ref, own, scratch = refs[2 * azs :]
    me = index_ref[0]
    strips = data[0].shape[2]
    here = mats[0].shape[1]
    late = [(i, chan) for i in range(azs) for chan in range(chans)]
    late_slots = [slot_ref[chan * local + lax.rem(me - i + azs, azs)] for i, chan in late]
    next_slots = [slot_ref[chan * local + azs + c] for chan in range(chans) for c in range(rest)]
    for j in range(azs):
        base = lax.rem(me - j + azs, azs) * here

        def arrange(row, _, j=j, base=base):
            for part in range(2):
                for n, slot in enumerate(late_slots):
                    own[part, base + row, n : n + 1, :] = mats[j][part, row, pl.ds(slot, 1), :]
                for n, slot in enumerate(next_slots):
                    next_ref[0, part, base + row, n : n + 1, :] = mats[j][part, row, pl.ds(slot, 1), :]
            return 0

        lax.fori_loop(0, here, arrange, 0, unroll=2)
    sources = [
        lambda s, i=i, chan=chan: (data[i][0, chan, s, 0], data[i][1, chan, s, 0]) for i, chan in late
    ]
    mix_kernel(
        sources,
        lambda part, row, n: own[part, row, n : n + 1, :],
        here * azs,
        strips,
        False,
        out_ref,
        None,
        scratch,
    )


def mix_late_call(index, slots, data, mats, chans, local, rest):
    azs = len(mats)
    _, _, strips, subs, _, _ = data[0].shape
    here = mats[0].shape[1]
    total = here * azs
    sums = jax.ShapeDtypeStruct((subs, 2, total, strips, SUB, LANES), jnp.float32)
    arranged = jax.ShapeDtypeStruct((subs, 2, total, chans * rest, LANES), jnp.float32)
    return pl.pallas_call(
        lambda *refs: mix_late_kernel(azs, chans, local, rest, *refs),
        grid=(subs,),
        in_specs=[SCALARS] * 2
        + [pl.BlockSpec((2, chans, strips, 1, SUB, LANES), lambda g: (0, 0, 0, g, 0, 0))] * azs
        + [pl.BlockSpec(mats[0].shape[:3] + (LANES,), lambda g: (0, 0, 0, g))] * azs,
        out_specs=[
            pl.BlockSpec((1,) + sums.shape[1:], lambda g: (g, 0, 0, 0, 0, 0)),
            pl.BlockSpec((1,) + arranged.shape[1:], lambda g: (g, 0, 0, 0, 0)),
        ],
        out_shape=[sums, arranged],
        scratch_shapes=[
            pltpu.VMEM((2, total, chans * azs, LANES), jnp.float32),
            pltpu.VMEM((chans * azs, strips, SUB, LANES), jnp.float32),
        ],
        compiler_params=pltpu.CompilerParams(vmem_limit_bytes=50 << 20),
        name="reconstruct_late",
        cost_estimate=pl.CostEstimate(
            flops=8 * total * strips * SUB * subs * LANES * chans * azs,
            bytes_accessed=4 * math.prod(sums.shape),
            transcendentals=0,
        ),
    )(index, slots, *data, *mats)


def mix_early_kernel(chans, rest, data, mats, prior, out_ref, scratch):
    strips = data.shape[0] // chans
    sources = [
        lambda s, c=c, chan=chan: tuple(data[chan * strips + s, p, c] for p in range(2))
        for chan in range(chans)
        for c in range(rest)
    ]
    mix_kernel(
        sources,
        lambda part, row, n: mats[0, part, row, n : n + 1, :],
        prior.shape[2],
        strips,
        True,
        out_ref,
        prior,
        scratch,
    )


def mix_early_call(early, mats, prior, chans, rest):
    subs, _, total, strips, _, _ = prior.shape
    out = jax.ShapeDtypeStruct((2, total, strips, SUB, subs * LANES), jnp.float32)
    return pl.pallas_call(
        lambda *refs: mix_early_kernel(chans, rest, *refs),
        grid=(subs,),
        in_specs=[
            pl.BlockSpec(early.shape[:3] + (SUB, LANES), lambda g: (0, 0, 0, g, 0)),
            pl.BlockSpec((1,) + mats.shape[1:], lambda g: (g, 0, 0, 0, 0)),
            pl.BlockSpec((1,) + prior.shape[1:], lambda g: (g, 0, 0, 0, 0, 0)),
        ],
        out_specs=pl.BlockSpec((2, total, strips, SUB, LANES), lambda g: (0, 0, 0, 0, g)),
        out_shape=out,
        scratch_shapes=[pltpu.VMEM((chans * rest, strips, SUB, LANES), jnp.float32)],
        compiler_params=pltpu.CompilerParams(vmem_limit_bytes=50 << 20),
        name="reconstruct",
        cost_estimate=pl.CostEstimate(
            flops=8 * math.prod(out.shape) * chans * rest,
            bytes_accessed=8 * math.prod(out.shape),
            transcendentals=0,
        ),
    )(early, mats, prior)


def with_halo(shard, sides, width):
    for axis, dim in sides:
        size, length = (lax.axis_size(axis), shard.shape[dim])
        up = [(i, (i + 1) % size) for i in range(size - 1)]
        down = [(j, i) for i, j in up]
        last = lax.slice_in_dim(shard, length - width, length, axis=dim)
        leading = lax.slice_in_dim(shard, 0, width, axis=dim)
        before = lax.ppermute(last, axis, up)
        after = lax.ppermute(leading, axis, down)
        shard = jnp.concatenate([before, shard, after], axis=dim)
    return shard


def phases(first, second, length):
    left = jnp.arange(first, dtype=jnp.int32)
    right = jnp.arange(second, dtype=jnp.int32)
    product = left[:, None] * right[None, :] % length
    angle = product.astype(jnp.float32) * (2.0 * math.pi / length)
    return (jnp.cos(angle), jnp.sin(angle))


def azimuth_fft(block):
    count = block.shape[-1]
    rows = math.isqrt(count)
    while count % rows:
        rows = rows - 1
    cols = count // rows
    lead = block.shape[1:-1]
    high = lax.Precision.HIGHEST
    real_in = block[0].reshape(lead + (rows, cols))
    imag_in = block[1].reshape(lead + (rows, cols))
    cosine_first, sine_first = phases(rows, rows, rows)
    first_real = jnp.einsum("...ab,af->...bf", real_in, cosine_first, precision=high) + jnp.einsum(
        "...ab,af->...bf", imag_in, sine_first, precision=high
    )
    first_imag = jnp.einsum("...ab,af->...bf", imag_in, cosine_first, precision=high) - jnp.einsum(
        "...ab,af->...bf", real_in, sine_first, precision=high
    )
    twist_cos, twist_sin = phases(cols, rows, count)
    turned_real = first_real * twist_cos + first_imag * twist_sin
    turned_imag = first_imag * twist_cos - first_real * twist_sin
    cosine_second, sine_second = phases(cols, cols, cols)
    out_real = jnp.einsum(
        "...bf,bg->...gf", turned_real, cosine_second, precision=high
    ) + jnp.einsum("...bf,bg->...gf", turned_imag, sine_second, precision=high)
    out_imag = jnp.einsum(
        "...bf,bg->...gf", turned_imag, cosine_second, precision=high
    ) - jnp.einsum("...bf,bg->...gf", turned_real, sine_second, precision=high)
    scale = 1.0 / math.sqrt(count)
    return jnp.stack([out_real.reshape(lead + (count,)), out_imag.reshape(lead + (count,))]) * scale


def general_shards(raw, taps, recon, channel_slot):
    width = taps.shape[1]
    half = (width - 1) // 2
    strip_rows = raw.shape[2]
    padded = with_halo(raw, (("rng", 2),), half)
    real_part = jnp.zeros(raw.shape[1:], jnp.float32)
    imag_part = jnp.zeros(raw.shape[1:], jnp.float32)
    for offset in range(width):
        seg_real = padded[0, :, offset : offset + strip_rows, :]
        seg_imag = padded[1, :, offset : offset + strip_rows, :]
        tap_real = taps[0, offset][None, :, None]
        tap_imag = taps[1, offset][None, :, None]
        real_part = real_part + tap_real * seg_real - tap_imag * seg_imag
        imag_part = imag_part + tap_real * seg_imag + tap_imag * seg_real
    filtered = jnp.stack([real_part, imag_part])
    spectrum = azimuth_fft(lax.all_to_all(filtered, "az", split_axis=2, concat_axis=3, tiled=True))
    strips = lax.axis_size("rng")
    groups = lax.axis_size("chan")
    local_channels = spectrum.shape[1]
    local_range = spectrum.shape[2]
    moved = lax.all_to_all(
        spectrum[:, None], ("chan", "rng"), split_axis=4, concat_axis=1, tiled=True
    )
    bins = moved.shape[-1]
    moved = moved.reshape((2, groups, strips, local_channels, local_range, bins))
    doppler = jnp.transpose(moved, (0, 1, 3, 2, 4, 5)).reshape(
        (2, groups * local_channels, strips * local_range, bins)
    )
    channels = doppler.shape[1]
    selector = (channel_slot[:, None] == jnp.arange(channels, dtype=jnp.int32)[None, :]).astype(
        jnp.float32
    )
    piece = lax.all_gather(recon, "az", axis=1, tiled=True)
    arranged = jnp.einsum("pkjf,cj->pkcf", piece, selector, precision=lax.Precision.HIGHEST)
    shape = (piece.shape[1], doppler.shape[2], doppler.shape[3])
    out_real = jnp.zeros(shape, jnp.float32)
    out_imag = jnp.zeros(shape, jnp.float32)
    for channel in range(channels):
        mat_real = arranged[0, :, channel, None, :]
        mat_imag = arranged[1, :, channel, None, :]
        data_real = doppler[0, channel][None]
        data_imag = doppler[1, channel][None]
        out_real = out_real + mat_real * data_real - mat_imag * data_imag
        out_imag = out_imag + mat_real * data_imag + mat_imag * data_real
    result = jnp.stack([out_real, out_imag])
    total_range = result.shape[2]
    return result.reshape((2, result.shape[1], strips, total_range // strips, result.shape[3]))


def shards(raw, taps, recon, channel_slot):
    chans, azs, strips = (lax.axis_size(n) for n in ("chan", "az", "rng"))
    _, local, rows, pulses = raw.shape
    width = taps.shape[1]
    half = (width - 1) // 2
    peers = chans * strips
    fits = local > azs and rows == azs * SUB and pulses * azs == LANES * LANES and half == SUB
    if not (fits and LANES % peers == 0):
        return general_shards(raw, taps, recon, channel_slot)
    me = lax.axis_index("az").astype(jnp.int32)
    index = me[None]
    count = pulses * azs
    slow = count // LANES
    tables = [jnp.asarray(t) for t in fft_tables(slow, count, azs)]
    rest = local - azs

    def give(step, at):
        to = lax.rem(me + step, azs)
        source = raw if at == 0 and step else lax.optimization_barrier(raw)
        block = lax.dynamic_slice(source, (0, to, at, 0), (2, 1, SUB, pulses))
        return lax.ppermute(block, "az", ring(azs, step)) if step else block

    def turn(spectra):
        return lax.all_to_all(spectra, ("chan", "rng"), 0, 0, tiled=True)

    received = [[give(i, n * SUB) for i in range(azs)] for n in range(rows // SUB)]
    near = lax.axis_index("rng").astype(jnp.int32)
    parts = [taps] + [lax.ppermute(taps, "rng", ring(strips, strips - i)) for i in range(1, strips)]
    strip = jnp.arange(strips, dtype=jnp.int32)[:, None, None, None]
    all_taps = sum(
        jnp.where(strip == lax.rem(near + i, strips), part[None], 0.0) for i, part in enumerate(parts)
    )
    all_taps = jnp.transpose(all_taps, (1, 2, 0, 3)).reshape(2, width, strips * rows)
    up = ring(strips, 1)[:-1]
    down = [(b, a) for a, b in up]


    def edge(c, at):
        source = raw if c == 0 else lax.optimization_barrier(raw)
        return source[:, azs + c : azs + c + 1, at : at + half, :]

    before = [lax.ppermute(edge(c, rows - half), "rng", up) for c in range(rest)]
    after = [lax.ppermute(edge(c, 0), "rng", down) for c in range(rest)]

    early_weights = band_matrix(taps, 0, rows + 2 * half, me, azs)
    late_weights = band_matrix(all_taps, half, strips * rows, me, azs)

    spectra = None
    for n in range(rows // SUB):
        spectra = fft_call(index, received[n], tables, peers, rows // SUB, n, 32 << 20, spectra)
    late = turn(spectra)

    swapped = []
    for c in range(rest):
        filtered = early_filter_call(early_weights, before[c], raw, after[c], azs + c, azs)
        swapped.append([filtered[0]] + [lax.ppermute(filtered[i], "az", ring(azs, i)) for i in range(1, azs)])
    mats = [recon] + [lax.ppermute(recon, "az", ring(azs, i)) for i in range(1, azs)]
    swapped[0][0], late_weights = lax.optimization_barrier((swapped[0][0], late_weights))
    spectra = None
    for c in range(rest):
        spectra = fft_call(index, swapped[c], tables, peers, rest, c, WHOLE, spectra)
    early = turn(spectra)

    filtered = late_filter_call(late_weights, late, chans, azs)
    data = [filtered[0]] + [lax.ppermute(filtered[i], "az", ring(azs, i)) for i in range(1, azs)]

    sums, arranged = mix_late_call(index, channel_slot, data, mats, chans, local, rest)
    return mix_early_call(early, arranged, sums, chans, rest)


def solution(mesh):
    return jax.shard_map(
        shards,
        mesh=mesh,
        in_specs=(
            P(None, "chan", "rng", "az"),
            P(None, None, "rng"),
            P(None, "az", None, ("chan", "rng")),
            P(),
        ),
        out_specs=P(None, None, None, "az", ("chan", "rng")),
        check_vma=False,
    )
```

```python
import math

import jax
import jax.numpy as jnp
import ml_dtypes
import numpy as np
from jax import lax
from jax.experimental import pallas as pl
from jax.experimental.pallas import tpu as pltpu
from jax.sharding import PartitionSpec as P


LANES = 128
SUB = 8
RESIDENT = pl.BlockSpec(memory_space=pltpu.VMEM)
SCALARS = pl.BlockSpec(memory_space=pltpu.SMEM)
WHOLE = 67043328


def ring(size, step):
    return [(i, (i + step) % size) for i in range(size)]


def split_three(matrix):
    high = matrix.astype(np.float32).astype(ml_dtypes.bfloat16)
    low = (matrix - high.astype(np.float64)).astype(ml_dtypes.bfloat16)
    return np.concatenate([high, high, low], axis=1)


def two_parts(value):
    high = value.astype(jnp.bfloat16)
    return high, (value - high.astype(jnp.float32)).astype(jnp.bfloat16)


def fft_tables(slow, count, azs):
    own = slow // azs
    h = np.arange(slow)
    place = np.concatenate([(-i * own + np.arange(own)) % slow for i in range(azs)])
    angle = 2 * np.pi * ((h[:, None] * place[None, :]) % slow) / slow
    first = np.block([[np.cos(angle), np.sin(angle)], [-np.sin(angle), np.cos(angle)]])
    b = np.arange(LANES)
    tables = []
    for me in range(azs):
        turn = 2 * np.pi * ((h[:, None] * (b[None, :] + me * own * LANES)) % count) / count
        tables.append(np.stack([np.cos(turn), -np.sin(turn)]))
    m = np.arange(count // slow)
    angle = 2 * np.pi * ((m[:, None] * b[None, :]) % LANES) / LANES
    second = np.block([[np.cos(angle), np.sin(angle)], [-np.sin(angle), np.cos(angle)]])
    second = second / math.sqrt(count)
    return split_three(first), np.stack(tables).astype(np.float32), split_three(second)


def fft_kernel(azs, own, peers, index_ref, *refs):
    inputs = refs[:azs]
    first_ref, turn_ref, second_ref = refs[azs : 3 + azs]
    out_ref, scratch = refs[-2:]
    slow = own * azs
    subs = LANES // peers
    me = index_ref[0]
    for part in range(2):
        for i in range(azs):
            for a in range(own):
                at = (part * slow + i * own + a) * SUB
                scratch[at : at + SUB, :] = inputs[i][
                    part, 0, :, a * LANES : (a + 1) * LANES
                ]
    for row in range(0, SUB, 2):
        x = jnp.concatenate(
            [scratch[pl.ds(row + e, 2 * slow, stride=SUB), :] for e in range(2)], axis=1
        )
        high, low = two_parts(x)
        y = jnp.dot(
            first_ref[...],
            jnp.concatenate([high, low, high], axis=0),
            preferred_element_type=jnp.float32,
        )
        turned = []
        for e in range(2):
            real = y[:slow, e * LANES : (e + 1) * LANES]
            imag = y[slow:, e * LANES : (e + 1) * LANES]
            turned.append(
                jnp.concatenate(
                    [
                        real * turn_ref[me, 0] - imag * turn_ref[me, 1],
                        real * turn_ref[me, 1] + imag * turn_ref[me, 0],
                    ],
                    axis=1,
                )
            )
        high, low = two_parts(jnp.concatenate(turned, axis=0))
        z = lax.dot_general(
            second_ref[...],
            jnp.concatenate([high, low, high], axis=1),
            (((1,), (1,)), ((), ())),
            preferred_element_type=jnp.float32,
        )
        for part in range(2):
            for peer in range(peers):
                for e in range(2):
                    at = part * LANES + peer * subs
                    out_ref[peer, part, 0, pl.ds(row + e, subs, stride=SUB), :] = z[
                        at : at + subs, e * slow : (e + 1) * slow
                    ]


def fft_tile_kernel(azs, own, peers, tile, index_ref, *refs):
    out_ref, scratch, block, done = refs[-4:]
    fft_kernel(azs, own, peers, index_ref, *refs[: azs + 3], block, scratch)
    copy = pltpu.make_async_copy(block, out_ref.at[:, :, pl.ds(tile, 1)], done)
    copy.start()
    copy.wait()


def fft_call(index, inputs, tables, peers, tiles, first, limit, prior=None):
    azs = len(inputs)
    steps = inputs[0].shape[1]
    own = inputs[0].shape[3] // LANES
    slow = own * azs
    subs = LANES // peers
    kept = prior is not None
    work = steps * SUB * slow * LANES
    tile = (peers, 2, 1, SUB * subs, LANES)
    scratch = [pltpu.VMEM((SUB * 2 * slow, LANES), jnp.float32)]
    if limit < WHOLE:
        how = dict(
            in_specs=[SCALARS] + [RESIDENT] * (azs + 3) + [pl.BlockSpec(memory_space=pl.ANY)] * kept,
            out_specs=pl.BlockSpec(memory_space=pl.ANY),
            scratch_shapes=scratch + [pltpu.VMEM(tile, jnp.float32), pltpu.SemaphoreType.DMA],
            input_output_aliases={azs + 4: 0} if kept else {},
        )
        kernel = lambda *refs: fft_tile_kernel(azs, own, peers, first, *refs)
    else:
        how = dict(
            grid=(steps,),
            in_specs=[SCALARS]
            + [pl.BlockSpec((2, 1, SUB, own * LANES), lambda g: (0, g, 0, 0))] * azs
            + [pl.BlockSpec(t.shape, lambda g, n=t.ndim: (0,) * n) for t in tables]
            + [pl.BlockSpec(memory_space=pl.ANY)] * kept,
            out_specs=pl.BlockSpec(tile, lambda g: (0, 0, g + first, 0, 0)),
            scratch_shapes=scratch,
            input_output_aliases={azs + 4: 0} if kept else {},
        )
        kernel = lambda *refs: fft_kernel(azs, own, peers, *refs)
    return pl.pallas_call(
        kernel,
        out_shape=jax.ShapeDtypeStruct((peers, 2, tiles, SUB * subs, LANES), jnp.float32),
        compiler_params=pltpu.CompilerParams(vmem_limit_bytes=limit),
        name="azimuth",
        cost_estimate=pl.CostEstimate(
            flops=work * 2 * 8 * LANES * 3, bytes_accessed=work * 16, transcendentals=0
        ),
        **how,
    )(index, *inputs, *tables, *([prior] if kept else []))


def band_matrix(taps, lead, total_in, me, azs):
    width, total = taps.shape[1:]
    tap = jnp.arange(total_in, dtype=jnp.int32)[None, :] - jnp.arange(total, dtype=jnp.int32)[:, None] + lead
    hit = tap[:, :, None] == jnp.arange(width, dtype=jnp.int32)
    table = jnp.transpose(taps, (0, 2, 1))
    band = jnp.sum(jnp.where(hit[None], table[:, :, None, :], 0.0), axis=3)
    real = jnp.concatenate([band[0], -band[1]], axis=1)
    imag = jnp.concatenate([band[1], band[0]], axis=1)
    both = jnp.stack([real, imag]).reshape(2, total // (azs * SUB), azs, SUB, 2 * total_in)
    both = jnp.transpose(both, (2, 0, 1, 3, 4)).reshape(azs, -1, 2 * total_in)
    both = lax.dynamic_slice_in_dim(jnp.concatenate([both, both]), me, azs, 0)
    return jnp.tile(both.reshape(-1, 2 * total_in), (1, 3))


def rounded_weights(w):
    columns = w.shape[1] // 3
    rounded = w.astype(jnp.bfloat16).astype(jnp.float32)
    low_part = lax.broadcasted_iota(jnp.int32, w.shape, 1) >= 2 * columns
    return jnp.where(low_part, w - rounded, rounded).astype(jnp.bfloat16)


def weighted(weights, blocks):
    high, low = two_parts(jnp.concatenate(blocks, axis=0))
    return jnp.dot(
        weights, jnp.concatenate([high, low, high], axis=0), preferred_element_type=jnp.float32
    )


def early_filter_kernel(azs, width, w_ref, before, own, after, *outs):
    weights = rounded_weights(w_ref[...])

    def body(step, _):
        at = pl.ds(pl.multiple_of(step * width, width), width)
        y = weighted(
            weights,
            [
                block
                for part in range(2)
                for block in (before[part, 0, :, at], own[part, 0, :, at], after[part, 0, :, at])
            ],
        )
        for i in range(azs):
            for part in range(2):
                row = (i * 2 + part) * SUB
                outs[i][part, 0, :, at] = y[row : row + SUB]
        return 0

    lax.fori_loop(0, own.shape[3] // width, body, 0, unroll=2)


def early_filter_call(weights, before, raw, after, at, azs):
    _, count, _, pulses = before.shape
    rows = raw.shape[2]
    out = jax.ShapeDtypeStruct((2, count, SUB, pulses), jnp.float32)
    edge = pl.BlockSpec((2, 1, SUB, pulses), lambda g: (0, g, 0, 0))
    return pl.pallas_call(
        lambda *refs: early_filter_kernel(azs, 4 * LANES, *refs),
        grid=(count,),
        in_specs=[
            pl.BlockSpec(weights.shape, lambda g: (0, 0)),
            edge,
            pl.BlockSpec((2, 1, rows, pulses), lambda g: (0, g + at, 0, 0)),
            edge,
        ],
        out_specs=[edge] * azs,
        out_shape=[out] * azs,
        compiler_params=pltpu.CompilerParams(vmem_limit_bytes=WHOLE),
        name="strip_filter",
        cost_estimate=pl.CostEstimate(
            flops=2 * weights.shape[0] * weights.shape[1] * count * pulses,
            bytes_accessed=24 * count * rows * pulses,
            transcendentals=0,
        ),
    )(weights, before, raw, after)


def late_filter_kernel(azs, w_ref, in_ref, *outs):
    weights = rounded_weights(w_ref[...])
    strips, _, tiles, depth, _ = in_ref.shape
    subs = depth // SUB
    chan = pl.program_id(0)
    step = 2 if subs % 2 == 0 else 1

    for sub in range(0, subs, step):
        y = weighted(
            weights,
            [
                jnp.concatenate(
                    [
                        in_ref[strip, part, tile, (sub + s) * SUB : (sub + s + 1) * SUB, :]
                        for s in range(step)
                    ],
                    axis=1,
                )
                for part in range(2)
                for strip in range(strips)
                for tile in range(tiles)
            ],
        )
        at = 0
        for i in range(azs):
            for part in range(2):
                for strip in range(strips):
                    for s in range(step):
                        outs[i][part, chan, strip, sub + s, :, :] = y[
                            at : at + SUB, s * LANES : (s + 1) * LANES
                        ]
                    at += SUB


def late_filter_call(weights, moved, chans, azs):
    peers, _, _, depth, _ = moved.shape
    strips, subs = peers // chans, depth // SUB
    out = jax.ShapeDtypeStruct((2, chans, strips, subs, SUB, LANES), jnp.float32)
    return pl.pallas_call(
        lambda *refs: late_filter_kernel(azs, *refs),
        grid=(chans,),
        in_specs=[
            pl.BlockSpec(weights.shape, lambda g: (0, 0)),
            pl.BlockSpec((strips,) + moved.shape[1:], lambda g: (g, 0, 0, 0, 0)),
        ],
        out_specs=[RESIDENT] * azs,
        out_shape=[out] * azs,
        compiler_params=pltpu.CompilerParams(vmem_limit_bytes=32 << 20),
        name="range_filter",
        cost_estimate=pl.CostEstimate(
            flops=2 * weights.shape[0] * weights.shape[1] * chans * subs * LANES,
            bytes_accessed=8 * math.prod(moved.shape),
            transcendentals=0,
        ),
    )(weights, moved)


def mix_kernel(sources, matrix, total, strips, kept, out_ref, prior, scratch):
    for n, value in enumerate(sources):
        for s in range(strips):
            dr, di = value(s)
            scratch[n, s] = dr + di

    def body(row, _):
        totals = None
        for n, value in enumerate(sources):
            ar = jnp.broadcast_to(matrix(0, row, n), (SUB, LANES))
            ai = jnp.broadcast_to(matrix(1, row, n), (SUB, LANES))
            both = ar + ai
            terms = []
            for s in range(strips):
                dr, di = value(s)
                terms += [ar * dr, ai * di, both * scratch[n, s]]
            totals = terms if totals is None else [t + u for t, u in zip(totals, terms)]
        for s in range(strips):
            first, second, third = totals[3 * s : 3 * s + 3]
            real, imag = first - second, third - first - second
            if kept:
                out_ref[0, row, s] = real + prior[0, 0, row, s]
                out_ref[1, row, s] = imag + prior[0, 1, row, s]
            else:
                out_ref[0, 0, row, s] = real
                out_ref[0, 1, row, s] = imag
        return 0

    lax.fori_loop(0, total, body, 0, unroll=math.gcd(total, 16 if kept else 8))


def mix_late_kernel(azs, chans, local, rest, index_ref, slot_ref, *refs):
    data, mats = refs[:azs], refs[azs : 2 * azs]
    out_ref, next_ref, own, scratch = refs[2 * azs :]
    me = index_ref[0]
    strips = data[0].shape[2]
    here = mats[0].shape[1]
    late = [(i, chan) for i in range(azs) for chan in range(chans)]
    late_slots = [slot_ref[chan * local + lax.rem(me - i + azs, azs)] for i, chan in late]
    next_slots = [slot_ref[chan * local + azs + c] for chan in range(chans) for c in range(rest)]
    for j in range(azs):
        base = lax.rem(me - j + azs, azs) * here

        def arrange(row, _, j=j, base=base):
            for part in range(2):
                for n, slot in enumerate(late_slots):
                    own[part, base + row, n : n + 1, :] = mats[j][part, row, pl.ds(slot, 1), :]
                for n, slot in enumerate(next_slots):
                    next_ref[0, part, base + row, n : n + 1, :] = mats[j][part, row, pl.ds(slot, 1), :]
            return 0

        lax.fori_loop(0, here, arrange, 0, unroll=2)
    sources = [
        lambda s, i=i, chan=chan: (data[i][0, chan, s, 0], data[i][1, chan, s, 0]) for i, chan in late
    ]
    mix_kernel(
        sources,
        lambda part, row, n: own[part, row, n : n + 1, :],
        here * azs,
        strips,
        False,
        out_ref,
        None,
        scratch,
    )


def mix_late_call(index, slots, data, mats, chans, local, rest):
    azs = len(mats)
    _, _, strips, subs, _, _ = data[0].shape
    here = mats[0].shape[1]
    total = here * azs
    sums = jax.ShapeDtypeStruct((subs, 2, total, strips, SUB, LANES), jnp.float32)
    arranged = jax.ShapeDtypeStruct((subs, 2, total, chans * rest, LANES), jnp.float32)
    return pl.pallas_call(
        lambda *refs: mix_late_kernel(azs, chans, local, rest, *refs),
        grid=(subs,),
        in_specs=[SCALARS] * 2
        + [pl.BlockSpec((2, chans, strips, 1, SUB, LANES), lambda g: (0, 0, 0, g, 0, 0))] * azs
        + [pl.BlockSpec(mats[0].shape[:3] + (LANES,), lambda g: (0, 0, 0, g))] * azs,
        out_specs=[
            pl.BlockSpec((1,) + sums.shape[1:], lambda g: (g, 0, 0, 0, 0, 0)),
            pl.BlockSpec((1,) + arranged.shape[1:], lambda g: (g, 0, 0, 0, 0)),
        ],
        out_shape=[sums, arranged],
        scratch_shapes=[
            pltpu.VMEM((2, total, chans * azs, LANES), jnp.float32),
            pltpu.VMEM((chans * azs, strips, SUB, LANES), jnp.float32),
        ],
        compiler_params=pltpu.CompilerParams(vmem_limit_bytes=50 << 20),
        name="reconstruct_late",
        cost_estimate=pl.CostEstimate(
            flops=8 * total * strips * SUB * subs * LANES * chans * azs,
            bytes_accessed=4 * math.prod(sums.shape),
            transcendentals=0,
        ),
    )(index, slots, *data, *mats)


def mix_early_kernel(chans, rest, subs, data, mats, prior_ref, out_ref, prior, block, scratch, came, went):
    strips = data.shape[0] // chans
    total = prior.shape[2]

    def fetch(g):
        return pltpu.make_async_copy(prior_ref.at[pl.ds(g, 1)], prior.at[pl.ds(g, 1)], came.at[g])

    def leave(g):
        lanes = pl.ds(pl.multiple_of(g * LANES, LANES), LANES)
        return pltpu.make_async_copy(block.at[g], out_ref.at[:, :, :, :, lanes], went.at[g])

    for g in range(subs):
        fetch(g).start()

    def one(g, _):
        at = pl.ds(pl.multiple_of(g * SUB, SUB), SUB)
        sources = [
            lambda s, c=c, chan=chan: tuple(data[chan * strips + s, p, c, at, :] for p in range(2))
            for chan in range(chans)
            for c in range(rest)
        ]
        fetch(g).wait()
        mix_kernel(
            sources,
            lambda part, row, n: mats[g, part, row, n : n + 1, :],
            total,
            strips,
            True,
            block.at[g],
            prior.at[pl.ds(g, 1)],
            scratch,
        )
        leave(g).start()
        return 0

    lax.fori_loop(0, subs, one, 0)
    for g in range(subs):
        leave(g).wait()


def mix_early_call(early, mats, prior, chans, rest):
    subs, _, total, strips, _, _ = prior.shape
    out = jax.ShapeDtypeStruct((2, total, strips, SUB, subs * LANES), jnp.float32)
    return pl.pallas_call(
        lambda *refs: mix_early_kernel(chans, rest, subs, *refs),
        in_specs=[RESIDENT, RESIDENT, pl.BlockSpec(memory_space=pl.ANY)],
        out_specs=pl.BlockSpec(memory_space=pl.ANY),
        out_shape=out,
        scratch_shapes=[
            pltpu.VMEM(prior.shape, jnp.float32),
            pltpu.VMEM(prior.shape, jnp.float32),
            pltpu.VMEM((chans * rest, strips, SUB, LANES), jnp.float32),
            pltpu.SemaphoreType.DMA((subs,)),
            pltpu.SemaphoreType.DMA((subs,)),
        ],
        compiler_params=pltpu.CompilerParams(vmem_limit_bytes=50 << 20),
        name="reconstruct",
        cost_estimate=pl.CostEstimate(
            flops=8 * math.prod(out.shape) * chans * rest,
            bytes_accessed=8 * math.prod(out.shape),
            transcendentals=0,
        ),
    )(early, mats, prior)


def with_halo(shard, sides, width):
    for axis, dim in sides:
        size, length = (lax.axis_size(axis), shard.shape[dim])
        up = [(i, (i + 1) % size) for i in range(size - 1)]
        down = [(j, i) for i, j in up]
        last = lax.slice_in_dim(shard, length - width, length, axis=dim)
        leading = lax.slice_in_dim(shard, 0, width, axis=dim)
        before = lax.ppermute(last, axis, up)
        after = lax.ppermute(leading, axis, down)
        shard = jnp.concatenate([before, shard, after], axis=dim)
    return shard


def phases(first, second, length):
    left = jnp.arange(first, dtype=jnp.int32)
    right = jnp.arange(second, dtype=jnp.int32)
    product = left[:, None] * right[None, :] % length
    angle = product.astype(jnp.float32) * (2.0 * math.pi / length)
    return (jnp.cos(angle), jnp.sin(angle))


def azimuth_fft(block):
    count = block.shape[-1]
    rows = math.isqrt(count)
    while count % rows:
        rows = rows - 1
    cols = count // rows
    lead = block.shape[1:-1]
    high = lax.Precision.HIGHEST
    real_in = block[0].reshape(lead + (rows, cols))
    imag_in = block[1].reshape(lead + (rows, cols))
    cosine_first, sine_first = phases(rows, rows, rows)
    first_real = jnp.einsum("...ab,af->...bf", real_in, cosine_first, precision=high) + jnp.einsum(
        "...ab,af->...bf", imag_in, sine_first, precision=high
    )
    first_imag = jnp.einsum("...ab,af->...bf", imag_in, cosine_first, precision=high) - jnp.einsum(
        "...ab,af->...bf", real_in, sine_first, precision=high
    )
    twist_cos, twist_sin = phases(cols, rows, count)
    turned_real = first_real * twist_cos + first_imag * twist_sin
    turned_imag = first_imag * twist_cos - first_real * twist_sin
    cosine_second, sine_second = phases(cols, cols, cols)
    out_real = jnp.einsum(
        "...bf,bg->...gf", turned_real, cosine_second, precision=high
    ) + jnp.einsum("...bf,bg->...gf", turned_imag, sine_second, precision=high)
    out_imag = jnp.einsum(
        "...bf,bg->...gf", turned_imag, cosine_second, precision=high
    ) - jnp.einsum("...bf,bg->...gf", turned_real, sine_second, precision=high)
    scale = 1.0 / math.sqrt(count)
    return jnp.stack([out_real.reshape(lead + (count,)), out_imag.reshape(lead + (count,))]) * scale


def general_shards(raw, taps, recon, channel_slot):
    width = taps.shape[1]
    half = (width - 1) // 2
    strip_rows = raw.shape[2]
    padded = with_halo(raw, (("rng", 2),), half)
    real_part = jnp.zeros(raw.shape[1:], jnp.float32)
    imag_part = jnp.zeros(raw.shape[1:], jnp.float32)
    for offset in range(width):
        seg_real = padded[0, :, offset : offset + strip_rows, :]
        seg_imag = padded[1, :, offset : offset + strip_rows, :]
        tap_real = taps[0, offset][None, :, None]
        tap_imag = taps[1, offset][None, :, None]
        real_part = real_part + tap_real * seg_real - tap_imag * seg_imag
        imag_part = imag_part + tap_real * seg_imag + tap_imag * seg_real
    filtered = jnp.stack([real_part, imag_part])
    spectrum = azimuth_fft(lax.all_to_all(filtered, "az", split_axis=2, concat_axis=3, tiled=True))
    strips = lax.axis_size("rng")
    groups = lax.axis_size("chan")
    local_channels = spectrum.shape[1]
    local_range = spectrum.shape[2]
    moved = lax.all_to_all(
        spectrum[:, None], ("chan", "rng"), split_axis=4, concat_axis=1, tiled=True
    )
    bins = moved.shape[-1]
    moved = moved.reshape((2, groups, strips, local_channels, local_range, bins))
    doppler = jnp.transpose(moved, (0, 1, 3, 2, 4, 5)).reshape(
        (2, groups * local_channels, strips * local_range, bins)
    )
    channels = doppler.shape[1]
    selector = (channel_slot[:, None] == jnp.arange(channels, dtype=jnp.int32)[None, :]).astype(
        jnp.float32
    )
    piece = lax.all_gather(recon, "az", axis=1, tiled=True)
    arranged = jnp.einsum("pkjf,cj->pkcf", piece, selector, precision=lax.Precision.HIGHEST)
    shape = (piece.shape[1], doppler.shape[2], doppler.shape[3])
    out_real = jnp.zeros(shape, jnp.float32)
    out_imag = jnp.zeros(shape, jnp.float32)
    for channel in range(channels):
        mat_real = arranged[0, :, channel, None, :]
        mat_imag = arranged[1, :, channel, None, :]
        data_real = doppler[0, channel][None]
        data_imag = doppler[1, channel][None]
        out_real = out_real + mat_real * data_real - mat_imag * data_imag
        out_imag = out_imag + mat_real * data_imag + mat_imag * data_real
    result = jnp.stack([out_real, out_imag])
    total_range = result.shape[2]
    return result.reshape((2, result.shape[1], strips, total_range // strips, result.shape[3]))


def shards(raw, taps, recon, channel_slot):
    chans, azs, strips = (lax.axis_size(n) for n in ("chan", "az", "rng"))
    _, local, rows, pulses = raw.shape
    width = taps.shape[1]
    half = (width - 1) // 2
    peers = chans * strips
    fits = local > azs and rows == azs * SUB and pulses * azs == LANES * LANES and half == SUB
    if not (fits and LANES % peers == 0):
        return general_shards(raw, taps, recon, channel_slot)
    me = lax.axis_index("az").astype(jnp.int32)
    index = me[None]
    count = pulses * azs
    slow = count // LANES
    tables = [jnp.asarray(t) for t in fft_tables(slow, count, azs)]
    rest = local - azs

    def give(step, at):
        to = lax.rem(me + step, azs)
        source = raw if at == 0 and step else lax.optimization_barrier(raw)
        block = lax.dynamic_slice(source, (0, to, at, 0), (2, 1, SUB, pulses))
        return lax.ppermute(block, "az", ring(azs, step)) if step else block

    def turn(spectra):
        return lax.all_to_all(spectra, ("chan", "rng"), 0, 0, tiled=True)

    received = [[give(i, n * SUB) for i in range(azs)] for n in range(rows // SUB)]
    near = lax.axis_index("rng").astype(jnp.int32)
    parts = [taps] + [lax.ppermute(taps, "rng", ring(strips, strips - i)) for i in range(1, strips)]
    strip = jnp.arange(strips, dtype=jnp.int32)[:, None, None, None]
    all_taps = sum(
        jnp.where(strip == lax.rem(near + i, strips), part[None], 0.0) for i, part in enumerate(parts)
    )
    all_taps = jnp.transpose(all_taps, (1, 2, 0, 3)).reshape(2, width, strips * rows)
    up = ring(strips, 1)[:-1]
    down = [(b, a) for a, b in up]


    def edge(c, at):
        source = raw if c == 0 else lax.optimization_barrier(raw)
        return source[:, azs + c : azs + c + 1, at : at + half, :]

    before = [lax.ppermute(edge(c, rows - half), "rng", up) for c in range(rest)]
    after = [lax.ppermute(edge(c, 0), "rng", down) for c in range(rest)]

    early_weights = band_matrix(taps, 0, rows + 2 * half, me, azs)
    late_weights = band_matrix(all_taps, half, strips * rows, me, azs)

    spectra = None
    for n in range(rows // SUB):
        spectra = fft_call(index, received[n], tables, peers, rows // SUB, n, 32 << 20, spectra)
    late = turn(spectra)

    swapped = []
    for c in range(rest):
        filtered = early_filter_call(early_weights, before[c], raw, after[c], azs + c, azs)
        swapped.append([filtered[0]] + [lax.ppermute(filtered[i], "az", ring(azs, i)) for i in range(1, azs)])
    mats = [recon] + [lax.ppermute(recon, "az", ring(azs, i)) for i in range(1, azs)]
    swapped[0][0], late_weights = lax.optimization_barrier((swapped[0][0], late_weights))
    spectra = None
    for c in range(rest):
        spectra = fft_call(index, swapped[c], tables, peers, rest, c, WHOLE, spectra)
    early = turn(spectra)

    filtered = late_filter_call(late_weights, late, chans, azs)
    data = [filtered[0]] + [lax.ppermute(filtered[i], "az", ring(azs, i)) for i in range(1, azs)]

    sums, arranged = mix_late_call(index, channel_slot, data, mats, chans, local, rest)
    return mix_early_call(early, arranged, sums, chans, rest)


def solution(mesh):
    return jax.shard_map(
        shards,
        mesh=mesh,
        in_specs=(
            P(None, "chan", "rng", "az"),
            P(None, None, "rng"),
            P(None, "az", None, ("chan", "rng")),
            P(),
        ),
        out_specs=P(None, None, None, "az", ("chan", "rng")),
        check_vma=False,
    )
```

```python
import math

import jax
import jax.numpy as jnp
import ml_dtypes
import numpy as np
from jax import lax
from jax.experimental import pallas as pl
from jax.experimental.pallas import tpu as pltpu
from jax.sharding import PartitionSpec as P


LANES = 128
SUB = 8
RESIDENT = pl.BlockSpec(memory_space=pltpu.VMEM)
SCALARS = pl.BlockSpec(memory_space=pltpu.SMEM)
WHOLE = 67043328


def ring(size, step):
    return [(i, (i + step) % size) for i in range(size)]


def split_three(matrix):
    high = matrix.astype(np.float32).astype(ml_dtypes.bfloat16)
    low = (matrix - high.astype(np.float64)).astype(ml_dtypes.bfloat16)
    return np.concatenate([high, high, low], axis=1)


def two_parts(value):
    high = value.astype(jnp.bfloat16)
    return high, (value - high.astype(jnp.float32)).astype(jnp.bfloat16)


def fft_tables(slow, count, azs, chans, strips):
    own = slow // azs
    h = np.arange(slow)
    place = np.concatenate([(-i * own + np.arange(own)) % slow for i in range(azs)])
    angle = 2 * np.pi * ((h[:, None] * place[None, :]) % slow) / slow
    first = np.block([[np.cos(angle), np.sin(angle)], [-np.sin(angle), np.cos(angle)]])
    b = np.arange(LANES)
    tables = []
    for me in range(azs):
        turn = 2 * np.pi * ((h[:, None] * (b[None, :] + me * own * LANES)) % count) / count
        tables.append(np.stack([np.cos(turn), -np.sin(turn)]))
    m = np.arange(count // slow).reshape(chans, strips, -1).transpose(1, 0, 2).ravel()
    angle = 2 * np.pi * ((m[:, None] * b[None, :]) % LANES) / LANES
    second = np.block([[np.cos(angle), np.sin(angle)], [-np.sin(angle), np.cos(angle)]])
    second = second / math.sqrt(count)
    return split_three(first), np.stack(tables).astype(np.float32), split_three(second)


def fft_kernel(azs, own, peers, index_ref, *refs):
    inputs = refs[:azs]
    first_ref, turn_ref, second_ref = refs[azs : 3 + azs]
    out_ref, scratch = refs[-2:]
    slow = own * azs
    subs = LANES // peers
    me = index_ref[0]
    for part in range(2):
        for i in range(azs):
            for a in range(own):
                at = (part * slow + i * own + a) * SUB
                scratch[at : at + SUB, :] = inputs[i][
                    part, 0, :, a * LANES : (a + 1) * LANES
                ]
    for row in range(0, SUB, 2):
        x = jnp.concatenate(
            [scratch[pl.ds(row + e, 2 * slow, stride=SUB), :] for e in range(2)], axis=1
        )
        high, low = two_parts(x)
        y = jnp.dot(
            first_ref[...],
            jnp.concatenate([high, low, high], axis=0),
            preferred_element_type=jnp.float32,
        )
        turned = []
        for e in range(2):
            real = y[:slow, e * LANES : (e + 1) * LANES]
            imag = y[slow:, e * LANES : (e + 1) * LANES]
            turned.append(
                jnp.concatenate(
                    [
                        real * turn_ref[me, 0] - imag * turn_ref[me, 1],
                        real * turn_ref[me, 1] + imag * turn_ref[me, 0],
                    ],
                    axis=1,
                )
            )
        high, low = two_parts(jnp.concatenate(turned, axis=0))
        z = lax.dot_general(
            second_ref[...],
            jnp.concatenate([high, low, high], axis=1),
            (((1,), (1,)), ((), ())),
            preferred_element_type=jnp.float32,
        )
        for part in range(2):
            for peer in range(peers):
                for e in range(2):
                    at = part * LANES + peer * subs
                    out_ref[peer, part, 0, pl.ds(row + e, subs, stride=SUB), :] = z[
                        at : at + subs, e * slow : (e + 1) * slow
                    ]


def fft_tile_kernel(azs, own, peers, tile, index_ref, *refs):
    out_ref, scratch, block, done = refs[-4:]
    fft_kernel(azs, own, peers, index_ref, *refs[: azs + 3], block, scratch)
    copy = pltpu.make_async_copy(block, out_ref.at[:, :, pl.ds(tile, 1)], done)
    copy.start()
    copy.wait()


def fft_call(index, inputs, tables, peers, tiles, first, limit, prior=None):
    azs = len(inputs)
    steps = inputs[0].shape[1]
    own = inputs[0].shape[3] // LANES
    slow = own * azs
    subs = LANES // peers
    kept = prior is not None
    work = steps * SUB * slow * LANES
    tile = (peers, 2, 1, SUB * subs, LANES)
    scratch = [pltpu.VMEM((SUB * 2 * slow, LANES), jnp.float32)]
    if limit < WHOLE:
        how = dict(
            in_specs=[SCALARS] + [RESIDENT] * (azs + 3) + [pl.BlockSpec(memory_space=pl.ANY)] * kept,
            out_specs=pl.BlockSpec(memory_space=pl.ANY),
            scratch_shapes=scratch + [pltpu.VMEM(tile, jnp.float32), pltpu.SemaphoreType.DMA],
            input_output_aliases={azs + 4: 0} if kept else {},
        )
        kernel = lambda *refs: fft_tile_kernel(azs, own, peers, first, *refs)
    else:
        how = dict(
            grid=(steps,),
            in_specs=[SCALARS]
            + [pl.BlockSpec((2, 1, SUB, own * LANES), lambda g: (0, g, 0, 0))] * azs
            + [pl.BlockSpec(t.shape, lambda g, n=t.ndim: (0,) * n) for t in tables]
            + [pl.BlockSpec(memory_space=pl.ANY)] * kept,
            out_specs=pl.BlockSpec(tile, lambda g: (0, 0, g + first, 0, 0)),
            scratch_shapes=scratch,
            input_output_aliases={azs + 4: 0} if kept else {},
        )
        kernel = lambda *refs: fft_kernel(azs, own, peers, *refs)
    return pl.pallas_call(
        kernel,
        out_shape=jax.ShapeDtypeStruct((peers, 2, tiles, SUB * subs, LANES), jnp.float32),
        compiler_params=pltpu.CompilerParams(vmem_limit_bytes=limit),
        name="azimuth",
        cost_estimate=pl.CostEstimate(
            flops=work * 2 * 8 * LANES * 3, bytes_accessed=work * 16, transcendentals=0
        ),
        **how,
    )(index, *inputs, *tables, *([prior] if kept else []))


def band_matrix(taps, lead, total_in, me, azs):
    width, total = taps.shape[1:]
    tap = jnp.arange(total_in, dtype=jnp.int32)[None, :] - jnp.arange(total, dtype=jnp.int32)[:, None] + lead
    hit = tap[:, :, None] == jnp.arange(width, dtype=jnp.int32)
    table = jnp.transpose(taps, (0, 2, 1))
    band = jnp.sum(jnp.where(hit[None], table[:, :, None, :], 0.0), axis=3)
    real = jnp.concatenate([band[0], -band[1]], axis=1)
    imag = jnp.concatenate([band[1], band[0]], axis=1)
    both = jnp.stack([real, imag]).reshape(2, total // (azs * SUB), azs, SUB, 2 * total_in)
    both = jnp.transpose(both, (2, 0, 1, 3, 4)).reshape(azs, -1, 2 * total_in)
    both = lax.dynamic_slice_in_dim(jnp.concatenate([both, both]), me, azs, 0)
    return jnp.tile(both.reshape(-1, 2 * total_in), (1, 3))


def rounded_weights(w):
    columns = w.shape[1] // 3
    rounded = w.astype(jnp.bfloat16).astype(jnp.float32)
    low_part = lax.broadcasted_iota(jnp.int32, w.shape, 1) >= 2 * columns
    return jnp.where(low_part, w - rounded, rounded).astype(jnp.bfloat16)


def weighted(weights, blocks):
    high, low = two_parts(jnp.concatenate(blocks, axis=0))
    return jnp.dot(
        weights, jnp.concatenate([high, low, high], axis=0), preferred_element_type=jnp.float32
    )


def early_filter_kernel(azs, width, w_ref, before, own, after, *outs):
    weights = rounded_weights(w_ref[...])

    def body(step, _):
        at = pl.ds(pl.multiple_of(step * width, width), width)
        y = weighted(
            weights,
            [
                block
                for part in range(2)
                for block in (before[part, 0, :, at], own[part, 0, :, at], after[part, 0, :, at])
            ],
        )
        for i in range(azs):
            for part in range(2):
                row = (i * 2 + part) * SUB
                outs[i][part, 0, :, at] = y[row : row + SUB]
        return 0

    lax.fori_loop(0, own.shape[3] // width, body, 0, unroll=2)


def early_filter_call(weights, before, raw, after, at, azs):
    _, count, _, pulses = before.shape
    rows = raw.shape[2]
    out = jax.ShapeDtypeStruct((2, count, SUB, pulses), jnp.float32)
    edge = pl.BlockSpec((2, 1, SUB, pulses), lambda g: (0, g, 0, 0))
    return pl.pallas_call(
        lambda *refs: early_filter_kernel(azs, 4 * LANES, *refs),
        grid=(count,),
        in_specs=[
            pl.BlockSpec(weights.shape, lambda g: (0, 0)),
            edge,
            pl.BlockSpec((2, 1, rows, pulses), lambda g: (0, g + at, 0, 0)),
            edge,
        ],
        out_specs=[edge] * azs,
        out_shape=[out] * azs,
        compiler_params=pltpu.CompilerParams(vmem_limit_bytes=WHOLE),
        name="strip_filter",
        cost_estimate=pl.CostEstimate(
            flops=2 * weights.shape[0] * weights.shape[1] * count * pulses,
            bytes_accessed=24 * count * rows * pulses,
            transcendentals=0,
        ),
    )(weights, before, raw, after)


def late_filter_kernel(azs, w_ref, in_ref, *outs):
    weights = rounded_weights(w_ref[...])
    strips, _, _, tiles, depth, _ = in_ref.shape
    subs = depth // SUB
    chan = pl.program_id(0)
    step = 2 if subs % 2 == 0 else 1

    for sub in range(0, subs, step):
        y = weighted(
            weights,
            [
                jnp.concatenate(
                    [
                        in_ref[strip, 0, part, tile, (sub + s) * SUB : (sub + s + 1) * SUB, :]
                        for s in range(step)
                    ],
                    axis=1,
                )
                for part in range(2)
                for strip in range(strips)
                for tile in range(tiles)
            ],
        )
        at = 0
        for i in range(azs):
            for part in range(2):
                for strip in range(strips):
                    for s in range(step):
                        outs[i][part, chan, strip, sub + s, :, :] = y[
                            at : at + SUB, s * LANES : (s + 1) * LANES
                        ]
                    at += SUB


def late_filter_call(weights, moved, chans, azs):
    peers, _, _, depth, _ = moved.shape
    strips, subs = peers // chans, depth // SUB
    out = jax.ShapeDtypeStruct((2, chans, strips, subs, SUB, LANES), jnp.float32)
    return pl.pallas_call(
        lambda *refs: late_filter_kernel(azs, *refs),
        grid=(chans,),
        in_specs=[
            pl.BlockSpec(weights.shape, lambda g: (0, 0)),
            pl.BlockSpec((strips, 1) + moved.shape[1:], lambda g: (0, g, 0, 0, 0, 0)),
        ],
        out_specs=[RESIDENT] * azs,
        out_shape=[out] * azs,
        compiler_params=pltpu.CompilerParams(vmem_limit_bytes=32 << 20),
        name="range_filter",
        cost_estimate=pl.CostEstimate(
            flops=2 * weights.shape[0] * weights.shape[1] * chans * subs * LANES,
            bytes_accessed=8 * math.prod(moved.shape),
            transcendentals=0,
        ),
    )(weights, moved.reshape((strips, chans) + moved.shape[1:]))


def mix_kernel(sources, matrix, total, strips, kept, out_ref, prior):
    def body(row, _):
        totals = None
        for n, value in enumerate(sources):
            ar = jnp.broadcast_to(matrix(0, row, n), (SUB, LANES))
            ai = jnp.broadcast_to(matrix(1, row, n), (SUB, LANES))
            both = ar + ai
            terms = []
            for s in range(strips):
                dr, di = value(s)
                terms += [ar * dr, ai * di, both * (dr + di)]
            totals = terms if totals is None else [t + u for t, u in zip(totals, terms)]
        for s in range(strips):
            first, second, third = totals[3 * s : 3 * s + 3]
            real, imag = first - second, third - first - second
            if kept:
                out_ref[0, row, s] = real + prior[0, 0, row, s]
                out_ref[1, row, s] = imag + prior[0, 1, row, s]
            else:
                out_ref[0, 0, row, s] = real
                out_ref[0, 1, row, s] = imag
        return 0

    lax.fori_loop(0, total, body, 0, unroll=math.gcd(total, 16 if kept else 8))


def mix_late_kernel(azs, chans, local, rest, index_ref, slot_ref, *refs):
    data, mats = refs[:azs], refs[azs : 2 * azs]
    out_ref, next_ref, own = refs[2 * azs :]
    me = index_ref[0]
    strips = data[0].shape[2]
    here = mats[0].shape[1]
    late = [(i, chan) for i in range(azs) for chan in range(chans)]
    late_slots = [slot_ref[chan * local + lax.rem(me - i + azs, azs)] for i, chan in late]
    next_slots = [slot_ref[chan * local + azs + c] for chan in range(chans) for c in range(rest)]
    for j in range(azs):
        base = lax.rem(me - j + azs, azs) * here

        def arrange(row, _, j=j, base=base):
            for part in range(2):
                for n, slot in enumerate(late_slots):
                    own[part, base + row, n : n + 1, :] = mats[j][part, row, pl.ds(slot, 1), :]
                for n, slot in enumerate(next_slots):
                    next_ref[0, part, base + row, n : n + 1, :] = mats[j][part, row, pl.ds(slot, 1), :]
            return 0

        lax.fori_loop(0, here, arrange, 0, unroll=2)
    sources = [
        lambda s, i=i, chan=chan: (data[i][0, chan, s, 0], data[i][1, chan, s, 0]) for i, chan in late
    ]
    mix_kernel(
        sources,
        lambda part, row, n: own[part, row, n : n + 1, :],
        here * azs,
        strips,
        False,
        out_ref,
        None,
    )


def mix_late_call(index, slots, data, mats, chans, local, rest):
    azs = len(mats)
    _, _, strips, subs, _, _ = data[0].shape
    here = mats[0].shape[1]
    total = here * azs
    sums = jax.ShapeDtypeStruct((subs, 2, total, strips, SUB, LANES), jnp.float32)
    arranged = jax.ShapeDtypeStruct((subs, 2, total, chans * rest, LANES), jnp.float32)
    return pl.pallas_call(
        lambda *refs: mix_late_kernel(azs, chans, local, rest, *refs),
        grid=(subs,),
        in_specs=[SCALARS] * 2
        + [pl.BlockSpec((2, chans, strips, 1, SUB, LANES), lambda g: (0, 0, 0, g, 0, 0))] * azs
        + [pl.BlockSpec(mats[0].shape[:3] + (LANES,), lambda g: (0, 0, 0, g))] * azs,
        out_specs=[
            pl.BlockSpec((1,) + sums.shape[1:], lambda g: (g, 0, 0, 0, 0, 0)),
            pl.BlockSpec((1,) + arranged.shape[1:], lambda g: (g, 0, 0, 0, 0)),
        ],
        out_shape=[sums, arranged],
        scratch_shapes=[
            pltpu.VMEM((2, total, chans * azs, LANES), jnp.float32),
        ],
        compiler_params=pltpu.CompilerParams(vmem_limit_bytes=50 << 20),
        name="reconstruct_late",
        cost_estimate=pl.CostEstimate(
            flops=8 * total * strips * SUB * subs * LANES * chans * azs,
            bytes_accessed=4 * math.prod(sums.shape),
            transcendentals=0,
        ),
    )(index, slots, *data, *mats)


def mix_early_kernel(chans, rest, subs, data, mats, prior_ref, out_ref, prior, block, came, went):
    strips = data.shape[0] // chans
    total = prior.shape[2]

    def fetch(g):
        return pltpu.make_async_copy(prior_ref.at[pl.ds(g, 1)], prior.at[pl.ds(g, 1)], came.at[g])

    def leave(g):
        lanes = pl.ds(pl.multiple_of(g * LANES, LANES), LANES)
        return pltpu.make_async_copy(block.at[g], out_ref.at[:, :, :, :, lanes], went.at[g])

    for g in range(subs):
        fetch(g).start()

    def one(g, _):
        at = pl.ds(pl.multiple_of(g * SUB, SUB), SUB)
        sources = [
            lambda s, c=c, chan=chan: tuple(data[s * chans + chan, p, c, at, :] for p in range(2))
            for chan in range(chans)
            for c in range(rest)
        ]
        fetch(g).wait()
        mix_kernel(
            sources,
            lambda part, row, n: mats[g, part, row, n : n + 1, :],
            total,
            strips,
            True,
            block.at[g],
            prior.at[pl.ds(g, 1)],
        )
        leave(g).start()
        return 0

    lax.fori_loop(0, subs, one, 0)
    for g in range(subs):
        leave(g).wait()


def mix_early_call(early, mats, prior, chans, rest):
    subs, _, total, strips, _, _ = prior.shape
    out = jax.ShapeDtypeStruct((2, total, strips, SUB, subs * LANES), jnp.float32)
    return pl.pallas_call(
        lambda *refs: mix_early_kernel(chans, rest, subs, *refs),
        in_specs=[RESIDENT, RESIDENT, pl.BlockSpec(memory_space=pl.ANY)],
        out_specs=pl.BlockSpec(memory_space=pl.ANY),
        out_shape=out,
        scratch_shapes=[
            pltpu.VMEM(prior.shape, jnp.float32),
            pltpu.VMEM(prior.shape, jnp.float32),
            pltpu.SemaphoreType.DMA((subs,)),
            pltpu.SemaphoreType.DMA((subs,)),
        ],
        compiler_params=pltpu.CompilerParams(vmem_limit_bytes=50 << 20),
        name="reconstruct",
        cost_estimate=pl.CostEstimate(
            flops=8 * math.prod(out.shape) * chans * rest,
            bytes_accessed=8 * math.prod(out.shape),
            transcendentals=0,
        ),
    )(early, mats, prior)


def with_halo(shard, sides, width):
    for axis, dim in sides:
        size, length = (lax.axis_size(axis), shard.shape[dim])
        up = [(i, (i + 1) % size) for i in range(size - 1)]
        down = [(j, i) for i, j in up]
        last = lax.slice_in_dim(shard, length - width, length, axis=dim)
        leading = lax.slice_in_dim(shard, 0, width, axis=dim)
        before = lax.ppermute(last, axis, up)
        after = lax.ppermute(leading, axis, down)
        shard = jnp.concatenate([before, shard, after], axis=dim)
    return shard


def phases(first, second, length):
    left = jnp.arange(first, dtype=jnp.int32)
    right = jnp.arange(second, dtype=jnp.int32)
    product = left[:, None] * right[None, :] % length
    angle = product.astype(jnp.float32) * (2.0 * math.pi / length)
    return (jnp.cos(angle), jnp.sin(angle))


def azimuth_fft(block):
    count = block.shape[-1]
    rows = math.isqrt(count)
    while count % rows:
        rows = rows - 1
    cols = count // rows
    lead = block.shape[1:-1]
    high = lax.Precision.HIGHEST
    real_in = block[0].reshape(lead + (rows, cols))
    imag_in = block[1].reshape(lead + (rows, cols))
    cosine_first, sine_first = phases(rows, rows, rows)
    first_real = jnp.einsum("...ab,af->...bf", real_in, cosine_first, precision=high) + jnp.einsum(
        "...ab,af->...bf", imag_in, sine_first, precision=high
    )
    first_imag = jnp.einsum("...ab,af->...bf", imag_in, cosine_first, precision=high) - jnp.einsum(
        "...ab,af->...bf", real_in, sine_first, precision=high
    )
    twist_cos, twist_sin = phases(cols, rows, count)
    turned_real = first_real * twist_cos + first_imag * twist_sin
    turned_imag = first_imag * twist_cos - first_real * twist_sin
    cosine_second, sine_second = phases(cols, cols, cols)
    out_real = jnp.einsum(
        "...bf,bg->...gf", turned_real, cosine_second, precision=high
    ) + jnp.einsum("...bf,bg->...gf", turned_imag, sine_second, precision=high)
    out_imag = jnp.einsum(
        "...bf,bg->...gf", turned_imag, cosine_second, precision=high
    ) - jnp.einsum("...bf,bg->...gf", turned_real, sine_second, precision=high)
    scale = 1.0 / math.sqrt(count)
    return jnp.stack([out_real.reshape(lead + (count,)), out_imag.reshape(lead + (count,))]) * scale


def general_shards(raw, taps, recon, channel_slot):
    width = taps.shape[1]
    half = (width - 1) // 2
    strip_rows = raw.shape[2]
    padded = with_halo(raw, (("rng", 2),), half)
    real_part = jnp.zeros(raw.shape[1:], jnp.float32)
    imag_part = jnp.zeros(raw.shape[1:], jnp.float32)
    for offset in range(width):
        seg_real = padded[0, :, offset : offset + strip_rows, :]
        seg_imag = padded[1, :, offset : offset + strip_rows, :]
        tap_real = taps[0, offset][None, :, None]
        tap_imag = taps[1, offset][None, :, None]
        real_part = real_part + tap_real * seg_real - tap_imag * seg_imag
        imag_part = imag_part + tap_real * seg_imag + tap_imag * seg_real
    filtered = jnp.stack([real_part, imag_part])
    spectrum = azimuth_fft(lax.all_to_all(filtered, "az", split_axis=2, concat_axis=3, tiled=True))
    strips = lax.axis_size("rng")
    groups = lax.axis_size("chan")
    local_channels = spectrum.shape[1]
    local_range = spectrum.shape[2]
    moved = lax.all_to_all(
        spectrum[:, None], ("chan", "rng"), split_axis=4, concat_axis=1, tiled=True
    )
    bins = moved.shape[-1]
    moved = moved.reshape((2, groups, strips, local_channels, local_range, bins))
    doppler = jnp.transpose(moved, (0, 1, 3, 2, 4, 5)).reshape(
        (2, groups * local_channels, strips * local_range, bins)
    )
    channels = doppler.shape[1]
    selector = (channel_slot[:, None] == jnp.arange(channels, dtype=jnp.int32)[None, :]).astype(
        jnp.float32
    )
    piece = lax.all_gather(recon, "az", axis=1, tiled=True)
    arranged = jnp.einsum("pkjf,cj->pkcf", piece, selector, precision=lax.Precision.HIGHEST)
    shape = (piece.shape[1], doppler.shape[2], doppler.shape[3])
    out_real = jnp.zeros(shape, jnp.float32)
    out_imag = jnp.zeros(shape, jnp.float32)
    for channel in range(channels):
        mat_real = arranged[0, :, channel, None, :]
        mat_imag = arranged[1, :, channel, None, :]
        data_real = doppler[0, channel][None]
        data_imag = doppler[1, channel][None]
        out_real = out_real + mat_real * data_real - mat_imag * data_imag
        out_imag = out_imag + mat_real * data_imag + mat_imag * data_real
    result = jnp.stack([out_real, out_imag])
    total_range = result.shape[2]
    return result.reshape((2, result.shape[1], strips, total_range // strips, result.shape[3]))


def shards(raw, taps, recon, channel_slot):
    chans, azs, strips = (lax.axis_size(n) for n in ("chan", "az", "rng"))
    _, local, rows, pulses = raw.shape
    width = taps.shape[1]
    half = (width - 1) // 2
    peers = chans * strips
    fits = local > azs and rows == azs * SUB and pulses * azs == LANES * LANES and half == SUB
    if not (fits and LANES % peers == 0):
        return general_shards(raw, taps, recon, channel_slot)
    me = lax.axis_index("az").astype(jnp.int32)
    index = me[None]
    count = pulses * azs
    slow = count // LANES
    tables = [jnp.asarray(t) for t in fft_tables(slow, count, azs, chans, strips)]
    rest = local - azs

    def give(step, at):
        to = lax.rem(me + step, azs)
        source = raw if at == 0 and step else lax.optimization_barrier(raw)
        block = lax.dynamic_slice(source, (0, to, at, 0), (2, 1, SUB, pulses))
        return lax.ppermute(block, "az", ring(azs, step)) if step else block

    def turn(spectra):
        return lax.all_to_all(spectra, ("rng", "chan"), 0, 0, tiled=True)

    received = [[give(i, n * SUB) for i in range(azs)] for n in range(rows // SUB)]
    near = lax.axis_index("rng").astype(jnp.int32)
    parts = [taps] + [lax.ppermute(taps, "rng", ring(strips, strips - i)) for i in range(1, strips)]
    strip = jnp.arange(strips, dtype=jnp.int32)[:, None, None, None]
    all_taps = sum(
        jnp.where(strip == lax.rem(near + i, strips), part[None], 0.0) for i, part in enumerate(parts)
    )
    all_taps = jnp.transpose(all_taps, (1, 2, 0, 3)).reshape(2, width, strips * rows)
    up = ring(strips, 1)[:-1]
    down = [(b, a) for a, b in up]


    def edge(c, at):
        source = raw if c == 0 else lax.optimization_barrier(raw)
        return source[:, azs + c : azs + c + 1, at : at + half, :]

    before = [lax.ppermute(edge(c, rows - half), "rng", up) for c in range(rest)]
    after = [lax.ppermute(edge(c, 0), "rng", down) for c in range(rest)]

    early_weights = band_matrix(taps, 0, rows + 2 * half, me, azs)
    late_weights = band_matrix(all_taps, half, strips * rows, me, azs)

    spectra = None
    for n in range(rows // SUB):
        spectra = fft_call(index, received[n], tables, peers, rows // SUB, n, 32 << 20, spectra)
    late = turn(spectra)

    swapped = []
    for c in range(rest):
        filtered = early_filter_call(early_weights, before[c], raw, after[c], azs + c, azs)
        swapped.append(
            [filtered[0]]
            + [lax.ppermute(filtered[i], "az", ring(azs, i)) for i in range(1, azs)]
        )
    mats = [recon] + [lax.ppermute(recon, "az", ring(azs, i)) for i in range(1, azs)]
    swapped[0][0], late_weights = lax.optimization_barrier((swapped[0][0], late_weights))
    spectra = None
    for c in range(rest):
        spectra = fft_call(index, swapped[c], tables, peers, rest, c, WHOLE, spectra)
    early = turn(spectra)

    filtered = late_filter_call(late_weights, late, chans, azs)
    data = [filtered[0]] + [lax.ppermute(filtered[i], "az", ring(azs, i)) for i in range(1, azs)]

    sums, arranged = mix_late_call(index, channel_slot, data, mats, chans, local, rest)
    return mix_early_call(early, arranged, sums, chans, rest)


def solution(mesh):
    return jax.shard_map(
        shards,
        mesh=mesh,
        in_specs=(
            P(None, "chan", "rng", "az"),
            P(None, None, "rng"),
            P(None, "az", None, ("chan", "rng")),
            P(),
        ),
        out_specs=P(None, None, None, "az", ("chan", "rng")),
        check_vma=False,
    )
```

```python
import math

import jax
import jax.numpy as jnp
import ml_dtypes
import numpy as np
from jax import lax
from jax.experimental import pallas as pl
from jax.experimental.pallas import tpu as pltpu
from jax.sharding import PartitionSpec as P


LANES = 128
SUB = 8
RESIDENT = pl.BlockSpec(memory_space=pltpu.VMEM)
SCALARS = pl.BlockSpec(memory_space=pltpu.SMEM)
WHOLE = 67043328


def ring(size, step):
    return [(i, (i + step) % size) for i in range(size)]


def split_three(matrix):
    high = matrix.astype(np.float32).astype(ml_dtypes.bfloat16)
    low = (matrix - high.astype(np.float64)).astype(ml_dtypes.bfloat16)
    return np.concatenate([high, high, low], axis=1)


def two_parts(value):
    high = value.astype(jnp.bfloat16)
    return high, (value - high.astype(jnp.float32)).astype(jnp.bfloat16)


def fft_tables(slow, count, azs, chans, strips):
    own = slow // azs
    h = np.arange(slow)
    place = np.concatenate([(-i * own + np.arange(own)) % slow for i in range(azs)])
    angle = 2 * np.pi * ((h[:, None] * place[None, :]) % slow) / slow
    first = np.block([[np.cos(angle), np.sin(angle)], [-np.sin(angle), np.cos(angle)]])
    b = np.arange(LANES)
    tables = []
    for me in range(azs):
        turn = 2 * np.pi * ((h[:, None] * (b[None, :] + me * own * LANES)) % count) / count
        tables.append(np.stack([np.cos(turn), -np.sin(turn)]))
    m = np.arange(count // slow).reshape(chans, strips, -1).transpose(1, 0, 2).ravel()
    angle = 2 * np.pi * ((m[:, None] * b[None, :]) % LANES) / LANES
    second = np.block([[np.cos(angle), np.sin(angle)], [-np.sin(angle), np.cos(angle)]])
    second = second / math.sqrt(count)
    return split_three(first), np.stack(tables).astype(np.float32), split_three(second)


def fft_kernel(azs, own, peers, index_ref, *refs):
    inputs = refs[:azs]
    first_ref, turn_ref, second_ref = refs[azs : 3 + azs]
    out_ref, scratch = refs[-2:]
    slow = own * azs
    subs = LANES // peers
    me = index_ref[0]
    for part in range(2):
        for i in range(azs):
            for a in range(own):
                at = (part * slow + i * own + a) * SUB
                scratch[at : at + SUB, :] = inputs[i][
                    part, 0, :, a * LANES : (a + 1) * LANES
                ]
    for row in range(0, SUB, 2):
        x = jnp.concatenate(
            [scratch[pl.ds(row + e, 2 * slow, stride=SUB), :] for e in range(2)], axis=1
        )
        high, low = two_parts(x)
        y = jnp.dot(
            first_ref[...],
            jnp.concatenate([high, low, high], axis=0),
            preferred_element_type=jnp.float32,
        )
        turned = []
        for e in range(2):
            real = y[:slow, e * LANES : (e + 1) * LANES]
            imag = y[slow:, e * LANES : (e + 1) * LANES]
            turned.append(
                jnp.concatenate(
                    [
                        real * turn_ref[me, 0] - imag * turn_ref[me, 1],
                        real * turn_ref[me, 1] + imag * turn_ref[me, 0],
                    ],
                    axis=1,
                )
            )
        high, low = two_parts(jnp.concatenate(turned, axis=0))
        z = lax.dot_general(
            second_ref[...],
            jnp.concatenate([high, low, high], axis=1),
            (((1,), (1,)), ((), ())),
            preferred_element_type=jnp.float32,
        )
        for part in range(2):
            for peer in range(peers):
                for e in range(2):
                    at = part * LANES + peer * subs
                    out_ref[peer, part, 0, pl.ds(row + e, subs, stride=SUB), :] = z[
                        at : at + subs, e * slow : (e + 1) * slow
                    ]


def fft_tile_kernel(azs, own, peers, tile, index_ref, *refs):
    out_ref, scratch, block, done = refs[-4:]
    fft_kernel(azs, own, peers, index_ref, *refs[: azs + 3], block, scratch)
    copy = pltpu.make_async_copy(block, out_ref.at[:, :, pl.ds(tile, 1)], done)
    copy.start()
    copy.wait()


def fft_call(index, inputs, tables, peers, tiles, first, limit, prior=None):
    azs = len(inputs)
    steps = inputs[0].shape[1]
    own = inputs[0].shape[3] // LANES
    slow = own * azs
    subs = LANES // peers
    kept = prior is not None
    work = steps * SUB * slow * LANES
    tile = (peers, 2, 1, SUB * subs, LANES)
    scratch = [pltpu.VMEM((SUB * 2 * slow, LANES), jnp.float32)]
    if limit < WHOLE:
        how = dict(
            in_specs=[SCALARS] + [RESIDENT] * (azs + 3) + [pl.BlockSpec(memory_space=pl.ANY)] * kept,
            out_specs=pl.BlockSpec(memory_space=pl.ANY),
            scratch_shapes=scratch + [pltpu.VMEM(tile, jnp.float32), pltpu.SemaphoreType.DMA],
            input_output_aliases={azs + 4: 0} if kept else {},
        )
        kernel = lambda *refs: fft_tile_kernel(azs, own, peers, first, *refs)
    else:
        how = dict(
            grid=(steps,),
            in_specs=[SCALARS]
            + [pl.BlockSpec((2, 1, SUB, own * LANES), lambda g: (0, g, 0, 0))] * azs
            + [pl.BlockSpec(t.shape, lambda g, n=t.ndim: (0,) * n) for t in tables]
            + [pl.BlockSpec(memory_space=pl.ANY)] * kept,
            out_specs=pl.BlockSpec(tile, lambda g: (0, 0, g + first, 0, 0)),
            scratch_shapes=scratch,
            input_output_aliases={azs + 4: 0} if kept else {},
        )
        kernel = lambda *refs: fft_kernel(azs, own, peers, *refs)
    return pl.pallas_call(
        kernel,
        out_shape=jax.ShapeDtypeStruct((peers, 2, tiles, SUB * subs, LANES), jnp.float32),
        compiler_params=pltpu.CompilerParams(vmem_limit_bytes=limit),
        name="azimuth",
        cost_estimate=pl.CostEstimate(
            flops=work * 2 * 8 * LANES * 3, bytes_accessed=work * 16, transcendentals=0
        ),
        **how,
    )(index, *inputs, *tables, *([prior] if kept else []))


def band_matrix(taps, lead, total_in, me, azs):
    width, total = taps.shape[1:]
    tap = jnp.arange(total_in, dtype=jnp.int32)[None, :] - jnp.arange(total, dtype=jnp.int32)[:, None] + lead
    hit = tap[:, :, None] == jnp.arange(width, dtype=jnp.int32)
    table = jnp.transpose(taps, (0, 2, 1))
    band = jnp.sum(jnp.where(hit[None], table[:, :, None, :], 0.0), axis=3)
    real = jnp.concatenate([band[0], -band[1]], axis=1)
    imag = jnp.concatenate([band[1], band[0]], axis=1)
    both = jnp.stack([real, imag]).reshape(2, total // (azs * SUB), azs, SUB, 2 * total_in)
    both = jnp.transpose(both, (2, 0, 1, 3, 4)).reshape(azs, -1, 2 * total_in)
    both = lax.dynamic_slice_in_dim(jnp.concatenate([both, both]), me, azs, 0)
    return jnp.tile(both.reshape(-1, 2 * total_in), (1, 3))


def rounded_weights(w):
    columns = w.shape[1] // 3
    rounded = w.astype(jnp.bfloat16).astype(jnp.float32)
    low_part = lax.broadcasted_iota(jnp.int32, w.shape, 1) >= 2 * columns
    return jnp.where(low_part, w - rounded, rounded).astype(jnp.bfloat16)


def weighted(weights, blocks):
    high, low = two_parts(jnp.concatenate(blocks, axis=0))
    return jnp.dot(
        weights, jnp.concatenate([high, low, high], axis=0), preferred_element_type=jnp.float32
    )


def early_filter_kernel(azs, width, w_ref, before, own, after, *outs):
    weights = rounded_weights(w_ref[...])

    def body(step, _):
        at = pl.ds(pl.multiple_of(step * width, width), width)
        y = weighted(
            weights,
            [
                block
                for part in range(2)
                for block in (before[part, 0, :, at], own[part, 0, :, at], after[part, 0, :, at])
            ],
        )
        for i in range(azs):
            for part in range(2):
                row = (i * 2 + part) * SUB
                outs[i][part, 0, :, at] = y[row : row + SUB]
        return 0

    lax.fori_loop(0, own.shape[3] // width, body, 0, unroll=2)


def early_filter_call(weights, before, raw, after, c, azs):
    count, pulses = 1, raw.shape[3]
    at = raw.shape[1] - before.shape[1] + c
    rows = raw.shape[2]
    out = jax.ShapeDtypeStruct((2, count, SUB, pulses), jnp.float32)
    edge = pl.BlockSpec((2, 1, SUB, pulses), lambda g: (0, c, 0, 0))
    whole = pl.BlockSpec((2, 1, SUB, pulses), lambda g: (0, 0, 0, 0))
    return pl.pallas_call(
        lambda *refs: early_filter_kernel(azs, 8 * LANES, *refs),
        grid=(count,),
        in_specs=[
            pl.BlockSpec(weights.shape, lambda g: (0, 0)),
            edge,
            pl.BlockSpec((2, 1, rows, pulses), lambda g: (0, g + at, 0, 0)),
            edge,
        ],
        out_specs=[whole] * azs,
        out_shape=[out] * azs,
        compiler_params=pltpu.CompilerParams(vmem_limit_bytes=WHOLE),
        name="strip_filter",
        cost_estimate=pl.CostEstimate(
            flops=2 * weights.shape[0] * weights.shape[1] * count * pulses,
            bytes_accessed=24 * count * rows * pulses,
            transcendentals=0,
        ),
    )(weights, before, raw, after)


def late_filter_kernel(azs, w_ref, in_ref, *outs):
    weights = rounded_weights(w_ref[...])
    strips, _, _, tiles, depth, _ = in_ref.shape
    subs = depth // SUB
    chan = pl.program_id(0)
    step = 2 if subs % 2 == 0 else 1

    for sub in range(0, subs, step):
        y = weighted(
            weights,
            [
                jnp.concatenate(
                    [
                        in_ref[strip, 0, part, tile, (sub + s) * SUB : (sub + s + 1) * SUB, :]
                        for s in range(step)
                    ],
                    axis=1,
                )
                for part in range(2)
                for strip in range(strips)
                for tile in range(tiles)
            ],
        )
        at = 0
        for i in range(azs):
            for part in range(2):
                for strip in range(strips):
                    for s in range(step):
                        outs[i][part, chan, strip, sub + s, :, :] = y[
                            at : at + SUB, s * LANES : (s + 1) * LANES
                        ]
                    at += SUB


def late_filter_call(weights, moved, chans, azs):
    peers, _, _, depth, _ = moved.shape
    strips, subs = peers // chans, depth // SUB
    out = jax.ShapeDtypeStruct((2, chans, strips, subs, SUB, LANES), jnp.float32)
    return pl.pallas_call(
        lambda *refs: late_filter_kernel(azs, *refs),
        grid=(chans,),
        in_specs=[
            pl.BlockSpec(weights.shape, lambda g: (0, 0)),
            pl.BlockSpec((strips, 1) + moved.shape[1:], lambda g: (0, g, 0, 0, 0, 0)),
        ],
        out_specs=[RESIDENT] * azs,
        out_shape=[out] * azs,
        compiler_params=pltpu.CompilerParams(vmem_limit_bytes=32 << 20),
        name="range_filter",
        cost_estimate=pl.CostEstimate(
            flops=2 * weights.shape[0] * weights.shape[1] * chans * subs * LANES,
            bytes_accessed=8 * math.prod(moved.shape),
            transcendentals=0,
        ),
    )(weights, moved.reshape((strips, chans) + moved.shape[1:]))


def mix_kernel(sources, matrix, total, strips, kept, out_ref, prior):
    def body(row, _):
        totals = None
        for n, value in enumerate(sources):
            ar = jnp.broadcast_to(matrix(0, row, n), (SUB, LANES))
            ai = jnp.broadcast_to(matrix(1, row, n), (SUB, LANES))
            both = ar + ai
            terms = []
            for s in range(strips):
                dr, di = value(s)
                terms += [ar * dr, ai * di, both * (dr + di)]
            totals = terms if totals is None else [t + u for t, u in zip(totals, terms)]
        for s in range(strips):
            first, second, third = totals[3 * s : 3 * s + 3]
            real, imag = first - second, third - first - second
            if kept:
                out_ref[0, row, s] = real + prior[0, 0, row, s]
                out_ref[1, row, s] = imag + prior[0, 1, row, s]
            else:
                out_ref[0, 0, row, s] = real
                out_ref[0, 1, row, s] = imag
        return 0

    lax.fori_loop(0, total, body, 0, unroll=math.gcd(total, 16))


def mix_late_kernel(azs, chans, local, rest, index_ref, slot_ref, *refs):
    data, mats = refs[:azs], refs[azs : 2 * azs]
    out_ref, next_ref, own = refs[2 * azs :]
    me = index_ref[0]
    strips = data[0].shape[2]
    here = mats[0].shape[1]
    late = [(i, chan) for i in range(azs) for chan in range(chans)]
    late_slots = [slot_ref[chan * local + lax.rem(me - i + azs, azs)] for i, chan in late]
    next_slots = [slot_ref[chan * local + azs + c] for chan in range(chans) for c in range(rest)]
    for j in range(azs):
        base = lax.rem(me - j + azs, azs) * here

        def arrange(row, _, j=j, base=base):
            for part in range(2):
                for n, slot in enumerate(late_slots):
                    own[part, base + row, n : n + 1, :] = mats[j][part, row, pl.ds(slot, 1), :]
                for n, slot in enumerate(next_slots):
                    next_ref[0, part, base + row, n : n + 1, :] = mats[j][part, row, pl.ds(slot, 1), :]
            return 0

        lax.fori_loop(0, here, arrange, 0, unroll=2)
    sources = [
        lambda s, i=i, chan=chan: (data[i][0, chan, s, 0], data[i][1, chan, s, 0]) for i, chan in late
    ]
    mix_kernel(
        sources,
        lambda part, row, n: own[part, row, n : n + 1, :],
        here * azs,
        strips,
        False,
        out_ref,
        None,
    )


def mix_late_call(index, slots, data, mats, chans, local, rest):
    azs = len(mats)
    _, _, strips, subs, _, _ = data[0].shape
    here = mats[0].shape[1]
    total = here * azs
    sums = jax.ShapeDtypeStruct((subs, 2, total, strips, SUB, LANES), jnp.float32)
    arranged = jax.ShapeDtypeStruct((subs, 2, total, chans * rest, LANES), jnp.float32)
    return pl.pallas_call(
        lambda *refs: mix_late_kernel(azs, chans, local, rest, *refs),
        grid=(subs,),
        in_specs=[SCALARS] * 2
        + [pl.BlockSpec((2, chans, strips, 1, SUB, LANES), lambda g: (0, 0, 0, g, 0, 0))] * azs
        + [pl.BlockSpec(mats[0].shape[:3] + (LANES,), lambda g: (0, 0, 0, g))] * azs,
        out_specs=[
            pl.BlockSpec((1,) + sums.shape[1:], lambda g: (g, 0, 0, 0, 0, 0)),
            pl.BlockSpec((1,) + arranged.shape[1:], lambda g: (g, 0, 0, 0, 0)),
        ],
        out_shape=[sums, arranged],
        scratch_shapes=[
            pltpu.VMEM((2, total, chans * azs, LANES), jnp.float32),
        ],
        compiler_params=pltpu.CompilerParams(vmem_limit_bytes=50 << 20),
        name="reconstruct_late",
        cost_estimate=pl.CostEstimate(
            flops=8 * total * strips * SUB * subs * LANES * chans * azs,
            bytes_accessed=4 * math.prod(sums.shape),
            transcendentals=0,
        ),
    )(index, slots, *data, *mats)


def mix_early_kernel(chans, rest, subs, data, mats, prior_ref, out_ref, prior, block, came, went):
    strips = data.shape[0] // chans
    total = prior.shape[2]

    def fetch(g):
        return pltpu.make_async_copy(prior_ref.at[pl.ds(g, 1)], prior.at[pl.ds(g, 1)], came.at[g])

    def leave(g):
        lanes = pl.ds(pl.multiple_of(g * LANES, LANES), LANES)
        return pltpu.make_async_copy(block.at[g], out_ref.at[:, :, :, :, lanes], went.at[g])

    for g in range(subs):
        fetch(g).start()

    def one(g, _):
        at = pl.ds(pl.multiple_of(g * SUB, SUB), SUB)
        sources = [
            lambda s, c=c, chan=chan: tuple(data[s * chans + chan, p, c, at, :] for p in range(2))
            for chan in range(chans)
            for c in range(rest)
        ]
        fetch(g).wait()
        mix_kernel(
            sources,
            lambda part, row, n: mats[g, part, row, n : n + 1, :],
            total,
            strips,
            True,
            block.at[g],
            prior.at[pl.ds(g, 1)],
        )
        leave(g).start()
        return 0

    lax.fori_loop(0, subs, one, 0)
    for g in range(subs):
        leave(g).wait()


def mix_early_call(early, mats, prior, chans, rest):
    subs, _, total, strips, _, _ = prior.shape
    out = jax.ShapeDtypeStruct((2, total, strips, SUB, subs * LANES), jnp.float32)
    return pl.pallas_call(
        lambda *refs: mix_early_kernel(chans, rest, subs, *refs),
        in_specs=[RESIDENT, RESIDENT, pl.BlockSpec(memory_space=pl.ANY)],
        out_specs=pl.BlockSpec(memory_space=pl.ANY),
        out_shape=out,
        scratch_shapes=[
            pltpu.VMEM(prior.shape, jnp.float32),
            pltpu.VMEM(prior.shape, jnp.float32),
            pltpu.SemaphoreType.DMA((subs,)),
            pltpu.SemaphoreType.DMA((subs,)),
        ],
        compiler_params=pltpu.CompilerParams(vmem_limit_bytes=50 << 20),
        name="reconstruct",
        cost_estimate=pl.CostEstimate(
            flops=8 * math.prod(out.shape) * chans * rest,
            bytes_accessed=8 * math.prod(out.shape),
            transcendentals=0,
        ),
    )(early, mats, prior)


def with_halo(shard, sides, width):
    for axis, dim in sides:
        size, length = (lax.axis_size(axis), shard.shape[dim])
        up = [(i, (i + 1) % size) for i in range(size - 1)]
        down = [(j, i) for i, j in up]
        last = lax.slice_in_dim(shard, length - width, length, axis=dim)
        leading = lax.slice_in_dim(shard, 0, width, axis=dim)
        before = lax.ppermute(last, axis, up)
        after = lax.ppermute(leading, axis, down)
        shard = jnp.concatenate([before, shard, after], axis=dim)
    return shard


def phases(first, second, length):
    left = jnp.arange(first, dtype=jnp.int32)
    right = jnp.arange(second, dtype=jnp.int32)
    product = left[:, None] * right[None, :] % length
    angle = product.astype(jnp.float32) * (2.0 * math.pi / length)
    return (jnp.cos(angle), jnp.sin(angle))


def azimuth_fft(block):
    count = block.shape[-1]
    rows = math.isqrt(count)
    while count % rows:
        rows = rows - 1
    cols = count // rows
    lead = block.shape[1:-1]
    high = lax.Precision.HIGHEST
    real_in = block[0].reshape(lead + (rows, cols))
    imag_in = block[1].reshape(lead + (rows, cols))
    cosine_first, sine_first = phases(rows, rows, rows)
    first_real = jnp.einsum("...ab,af->...bf", real_in, cosine_first, precision=high) + jnp.einsum(
        "...ab,af->...bf", imag_in, sine_first, precision=high
    )
    first_imag = jnp.einsum("...ab,af->...bf", imag_in, cosine_first, precision=high) - jnp.einsum(
        "...ab,af->...bf", real_in, sine_first, precision=high
    )
    twist_cos, twist_sin = phases(cols, rows, count)
    turned_real = first_real * twist_cos + first_imag * twist_sin
    turned_imag = first_imag * twist_cos - first_real * twist_sin
    cosine_second, sine_second = phases(cols, cols, cols)
    out_real = jnp.einsum(
        "...bf,bg->...gf", turned_real, cosine_second, precision=high
    ) + jnp.einsum("...bf,bg->...gf", turned_imag, sine_second, precision=high)
    out_imag = jnp.einsum(
        "...bf,bg->...gf", turned_imag, cosine_second, precision=high
    ) - jnp.einsum("...bf,bg->...gf", turned_real, sine_second, precision=high)
    scale = 1.0 / math.sqrt(count)
    return jnp.stack([out_real.reshape(lead + (count,)), out_imag.reshape(lead + (count,))]) * scale


def general_shards(raw, taps, recon, channel_slot):
    width = taps.shape[1]
    half = (width - 1) // 2
    strip_rows = raw.shape[2]
    padded = with_halo(raw, (("rng", 2),), half)
    real_part = jnp.zeros(raw.shape[1:], jnp.float32)
    imag_part = jnp.zeros(raw.shape[1:], jnp.float32)
    for offset in range(width):
        seg_real = padded[0, :, offset : offset + strip_rows, :]
        seg_imag = padded[1, :, offset : offset + strip_rows, :]
        tap_real = taps[0, offset][None, :, None]
        tap_imag = taps[1, offset][None, :, None]
        real_part = real_part + tap_real * seg_real - tap_imag * seg_imag
        imag_part = imag_part + tap_real * seg_imag + tap_imag * seg_real
    filtered = jnp.stack([real_part, imag_part])
    spectrum = azimuth_fft(lax.all_to_all(filtered, "az", split_axis=2, concat_axis=3, tiled=True))
    strips = lax.axis_size("rng")
    groups = lax.axis_size("chan")
    local_channels = spectrum.shape[1]
    local_range = spectrum.shape[2]
    moved = lax.all_to_all(
        spectrum[:, None], ("chan", "rng"), split_axis=4, concat_axis=1, tiled=True
    )
    bins = moved.shape[-1]
    moved = moved.reshape((2, groups, strips, local_channels, local_range, bins))
    doppler = jnp.transpose(moved, (0, 1, 3, 2, 4, 5)).reshape(
        (2, groups * local_channels, strips * local_range, bins)
    )
    channels = doppler.shape[1]
    selector = (channel_slot[:, None] == jnp.arange(channels, dtype=jnp.int32)[None, :]).astype(
        jnp.float32
    )
    piece = lax.all_gather(recon, "az", axis=1, tiled=True)
    arranged = jnp.einsum("pkjf,cj->pkcf", piece, selector, precision=lax.Precision.HIGHEST)
    shape = (piece.shape[1], doppler.shape[2], doppler.shape[3])
    out_real = jnp.zeros(shape, jnp.float32)
    out_imag = jnp.zeros(shape, jnp.float32)
    for channel in range(channels):
        mat_real = arranged[0, :, channel, None, :]
        mat_imag = arranged[1, :, channel, None, :]
        data_real = doppler[0, channel][None]
        data_imag = doppler[1, channel][None]
        out_real = out_real + mat_real * data_real - mat_imag * data_imag
        out_imag = out_imag + mat_real * data_imag + mat_imag * data_real
    result = jnp.stack([out_real, out_imag])
    total_range = result.shape[2]
    return result.reshape((2, result.shape[1], strips, total_range // strips, result.shape[3]))


def shards(raw, taps, recon, channel_slot):
    chans, azs, strips = (lax.axis_size(n) for n in ("chan", "az", "rng"))
    _, local, rows, pulses = raw.shape
    width = taps.shape[1]
    half = (width - 1) // 2
    peers = chans * strips
    fits = local > azs and rows == azs * SUB and pulses * azs == LANES * LANES and half == SUB
    if not (fits and LANES % peers == 0):
        return general_shards(raw, taps, recon, channel_slot)
    me = lax.axis_index("az").astype(jnp.int32)
    index = me[None]
    count = pulses * azs
    slow = count // LANES
    tables = [jnp.asarray(t) for t in fft_tables(slow, count, azs, chans, strips)]
    rest = local - azs

    def give(step, at):
        to = lax.rem(me + step, azs)
        source = raw if at == 0 and step else lax.optimization_barrier(raw)
        block = lax.dynamic_slice(source, (0, to, at, 0), (2, 1, SUB, pulses))
        return lax.ppermute(block, "az", ring(azs, step)) if step else block

    def turn(spectra):
        return lax.all_to_all(spectra, ("rng", "chan"), 0, 0, tiled=True)

    received = [[give(i, n * SUB) for i in range(azs)] for n in range(rows // SUB)]
    near = lax.axis_index("rng").astype(jnp.int32)
    parts = [taps] + [lax.ppermute(taps, "rng", ring(strips, strips - i)) for i in range(1, strips)]
    strip = jnp.arange(strips, dtype=jnp.int32)[:, None, None, None]
    all_taps = sum(
        jnp.where(strip == lax.rem(near + i, strips), part[None], 0.0) for i, part in enumerate(parts)
    )
    all_taps = jnp.transpose(all_taps, (1, 2, 0, 3)).reshape(2, width, strips * rows)
    up = ring(strips, 1)[:-1]
    down = [(b, a) for a, b in up]


    before = lax.ppermute(raw[:, azs:, rows - half :, :], "rng", up)
    after = lax.ppermute(raw[:, azs:, :half, :], "rng", down)

    early_weights = band_matrix(taps, 0, rows + 2 * half, me, azs)
    late_weights = band_matrix(all_taps, half, strips * rows, me, azs)

    spectra = None
    for n in range(rows // SUB):
        spectra = fft_call(index, received[n], tables, peers, rows // SUB, n, 32 << 20, spectra)
    late = turn(spectra)

    swapped = []
    for c in range(rest):
        filtered = early_filter_call(early_weights, before, raw, after, c, azs)
        swapped.append([filtered[0]] + [lax.ppermute(filtered[i], "az", ring(azs, i)) for i in range(1, azs)])
    mats = [recon] + [lax.ppermute(recon, "az", ring(azs, i)) for i in range(1, azs)]
    swapped[0][0], late_weights = lax.optimization_barrier((swapped[0][0], late_weights))
    spectra = None
    for c in range(rest):
        spectra = fft_call(index, swapped[c], tables, peers, rest, c, WHOLE, spectra)
    early = turn(spectra)

    filtered = late_filter_call(late_weights, late, chans, azs)
    data = [filtered[0]] + [lax.ppermute(filtered[i], "az", ring(azs, i)) for i in range(1, azs)]

    sums, arranged = mix_late_call(index, channel_slot, data, mats, chans, local, rest)
    return mix_early_call(early, arranged, sums, chans, rest)


def solution(mesh):
    return jax.shard_map(
        shards,
        mesh=mesh,
        in_specs=(
            P(None, "chan", "rng", "az"),
            P(None, None, "rng"),
            P(None, "az", None, ("chan", "rng")),
            P(),
        ),
        out_specs=P(None, None, None, "az", ("chan", "rng")),
        check_vma=False,
    )
```
